32 devices in a mesh: seg: 4 (over z), sec: 8 (over y, x, core).
Axes of the slice: x: 2, y: 2, z: 4, core: 2. Of those that a mesh axis runs over, the one named last changes fastest.
Arguments:
- env_left: bfloat16 [4, 56, 34, 128, 128], P('seg', 'sec'), may hold values from -6 to 6
- isometry: bfloat16 [1, 4, 56, 4, 128, 128], P(None, 'seg', 'sec'), may hold values from -0.25 to 0.25
- sing_vals: float32 [4, 56, 128], P('seg', 'sec'), may hold values from 0.5 to 2
- kept: int32 [1, 4, 56], P(None, 'seg', 'sec'), may hold values from 32 to 128
- twosite_sector: int32 [1, 4, 56], P(None, 'seg'), may hold values from 0 to 55, as said below
- mpo_row: int32 [34, 3], replicated, may hold values from 0 to 33
- mpo_op: int32 [34, 3], replicated, may hold values from 0 to 5
- op_table: float32 [6, 4, 4], replicated, may hold values from -6 to 6
Outputs:
- env_right: bfloat16 [4, 56, 34, 128, 128], P('seg', 'sec')
- handoff: bfloat16 [4, 56, 34, 128, 128], P('seg', 'sec')
The draws below stay inside these ranges and needn't reach their ends.
Inputs may be any that keep to these rules, and one draw needn't show every extreme that they name: `twosite_sector`: each row along the last dimension is a permutation of the 56 sectors. The 7 positions n with the same n // 7 hold sectors q with 7 different values of q // 7.
All inputs are finite; a program needn't handle non-finite values.
Results may differ from the reference program's by a relative error of at most 0.0081.
Values may be sent and summed in bfloat16 or wider, within the bound.
A program may use at most 128 MiB of HBM per device.

```python
import math
import jax
import jax.numpy as jnp
from jax import lax

SEC_DEV = 7
BLK = 128
DW = 34
PHYS = 4
NOPS = 6
TERMS = 3
SITES = 1
SEGS = 4
NSEC = 56
N_SEC = 8


def one_layout(sub_key):
    key_outer, key_inner, key_offset, key_slots = jax.random.split(sub_key, 4)
    outer = jax.random.permutation(key_outer, N_SEC).astype(jnp.int32)
    inner = jax.random.permutation(key_inner, N_SEC).astype(jnp.int32)
    offsets = jax.random.permutation(key_offset, N_SEC).astype(jnp.int32)[:SEC_DEV]
    slot_keys = jax.random.split(key_slots, N_SEC)
    slots = jax.vmap(lambda each_key: jax.random.permutation(each_key, SEC_DEV).astype(jnp.int32))(slot_keys)
    position = (inner[:, None] + offsets[None, :]) % N_SEC
    owner = outer[position]
    column = jnp.arange(SEC_DEV, dtype=jnp.int32)[None, :]
    slot_taken = slots[owner, column]
    sector = owner * SEC_DEV + slot_taken
    return sector.reshape(N_SEC * SEC_DEV).astype(jnp.int32)


def draw_twosite_sector(key, part):
    keys = jax.random.split(jax.random.fold_in(key, 17), SITES * SEGS)
    table = jax.vmap(one_layout)(keys)
    return table.reshape(SITES, SEGS, NSEC).astype(jnp.int32)


def place_ends(entries, key, smallest, largest):
    spot = [jax.random.randint(jax.random.fold_in(key, axis), (), 0, length) for axis, length in enumerate(entries.shape)]
    main_axis = entries.shape.index(max(entries.shape))
    next_to = spot[:main_axis] + [(spot[main_axis] + 1) % entries.shape[main_axis]] + spot[main_axis + 1:]
    return entries.at[tuple(spot)].set(smallest).at[tuple(next_to)].set(largest)


def shard_levels(rng, dims, shards, smallest, top_value):
    level = 1.0
    for dim, blocks in shards:
        draws = jax.random.uniform(jax.random.fold_in(jax.random.fold_in(rng, 6), dim), (blocks,), jnp.float32, smallest / len(shards), top_value / len(shards))
        level = level * jnp.repeat(jnp.exp(draws), dims[dim] // blocks).reshape((-1,) + (1,) * (len(dims) - 1 - dim))
    return level


def scatter_about(own_key, shape, deviation, reach, pieces=(), kind=jnp.bfloat16):
    result = deviation * jax.random.normal(own_key, shape, jnp.float32)
    if pieces:
        result = result * shard_levels(own_key, shape, pieces, -0.22, 0.18)
    return jnp.clip(result, -reach, reach).astype(kind)


def setup_inputs(seed: int = 0) -> dict:
    streams_of = jax.random.split(jax.random.key(seed), 9)
    return {
        "env_left": scatter_about(streams_of[0], (SEGS, NSEC, DW, BLK, BLK), 1.0, 6.0, ((0, 4), (1, 8))),
        "isometry": scatter_about(streams_of[1], (SITES, SEGS, NSEC, PHYS, BLK, BLK), (PHYS * BLK) ** -0.5, 0.25, ((1, 4), (2, 8))),
        "sing_vals": jnp.clip(jnp.exp(math.log(2.0) - 1.3862944 * jax.random.uniform(streams_of[2], (SEGS, NSEC, BLK), jnp.float32) ** shard_levels(streams_of[2], (SEGS, NSEC, BLK), ((0, 4), (1, 8)), -0.2, 0.2)), 0.5, 2.0),
        "kept": place_ends(jax.random.randint(streams_of[3], (SITES, SEGS, NSEC), BLK // 4, BLK + 1), jax.random.fold_in(streams_of[3], 1), BLK // 4, BLK).astype(jnp.int32),
        "twosite_sector": draw_twosite_sector(jax.random.fold_in(streams_of[8], 71), 0),
        "mpo_row": place_ends(jax.random.randint(streams_of[5], (DW, TERMS), 0, DW), jax.random.fold_in(streams_of[5], 1), 0, DW - 1).astype(jnp.int32),
        "mpo_op": place_ends(jax.random.randint(streams_of[6], (DW, TERMS), 0, NOPS), jax.random.fold_in(streams_of[6], 1), 0, NOPS - 1).astype(jnp.int32),
        "op_table": scatter_about(streams_of[7], (NOPS, PHYS, PHYS), 1.0, 6.0, (), jnp.float32),
    }


CHARGES = (0, 1, 1, 2)


def mpo_matrix(mpo_row, mpo_op, op_table):
    width = mpo_row.shape[0]
    row_hot = (mpo_row[:, :, None] == jnp.arange(width, dtype=jnp.int32)[None, None, :]).astype(jnp.float32)
    op_hot = (mpo_op[:, :, None] == jnp.arange(op_table.shape[0], dtype=jnp.int32)[None, None, :]).astype(jnp.float32)
    charge = jnp.array(CHARGES, dtype=jnp.int32)
    same = (charge[:, None] == charge[None, :]).astype(jnp.float32)
    full = jnp.einsum('vtw,vtx,xpq->vpwq', row_hot, op_hot, op_table.astype(jnp.float32))
    full = full * same[None, :, None, :]
    return full.reshape(width * 4, width * 4).astype(jnp.bfloat16)


def sector_update(lower, isom, w_matrix):
    lower_f = lower.astype(jnp.float32)
    isom_f = isom.astype(jnp.float32)
    first = jnp.einsum('wbc,ca->wba', lower_f[2], isom_f[0])[:, None]
    middle = jnp.einsum('wbc,sca->wsba', lower_f[1], isom_f[1:3])
    last = jnp.einsum('wbc,ca->wba', lower_f[0], isom_f[3])[:, None]
    partial_value = jnp.concatenate([first, middle, last], axis=1).astype(jnp.bfloat16)
    width = partial_value.shape[0]
    blk = partial_value.shape[2]
    mixed = jnp.dot(w_matrix, partial_value.reshape(width * 4, blk * blk), preferred_element_type=jnp.float32)
    mixed = mixed.astype(jnp.bfloat16).reshape(width, 4, blk, blk)
    return jnp.einsum('sba,vsbc->vac', isom_f, mixed.astype(jnp.float32)).astype(jnp.bfloat16)


def reference(env_left, isometry, sing_vals, kept, twosite_sector, mpo_row, mpo_op, op_table):
    w_matrix = mpo_matrix(mpo_row, mpo_op, op_table)
    blk = env_left.shape[-1]
    columns = jnp.arange(blk, dtype=jnp.int32)
    finals = []
    inverses = []
    for segment in range(SEGS):
        env = env_left[segment]
        for site_index in range(SITES):
            order = twosite_sector[site_index, segment].astype(jnp.int32)
            blocks = isometry[site_index, segment]
            placed = jnp.zeros_like(blocks).at[order].set(blocks)
            keep = columns[None, :] < kept[site_index, segment][:, None]
            placed = jnp.where(keep[:, None, None, :], placed, jnp.zeros_like(placed))
            padded = jnp.concatenate([jnp.zeros((2,) + env.shape[1:], env.dtype), env], axis=0)

            def one_sector(index, padded=padded, placed=placed):
                lower = lax.dynamic_slice_in_dim(padded, index, 3, 0)
                isom = lax.dynamic_index_in_dim(placed, index, 0, keepdims=False)
                return sector_update(lower, isom, w_matrix)

            env = lax.map(one_sector, jnp.arange(env.shape[0], dtype=jnp.int32))
        keep_last = columns[None, :] < kept[SITES - 1, segment][:, None]
        inverse = jnp.where(keep_last, 1.0 / sing_vals[segment], jnp.zeros_like(sing_vals[segment]))
        finals.append(env)
        inverses.append(inverse.astype(jnp.bfloat16))
    env_right = jnp.stack(finals)
    outputs = [jnp.zeros_like(finals[0])]
    for segment in range(1, SEGS):
        scale = inverses[segment - 1].astype(jnp.float32)
        value = scale[:, None, :, None] * finals[segment - 1].astype(jnp.float32) * scale[:, None, None, :]
        outputs.append(value.astype(jnp.bfloat16))
    return env_right, jnp.stack(outputs)
```

```python
import functools

import jax
import jax.numpy as jnp
from jax import lax
from jax.experimental import pallas as pl
from jax.experimental.pallas import tpu as pltpu
from jax.sharding import PartitionSpec as P

SITES = 1
CHARGES = (0, 1, 1, 2)
VMEM_LIMIT = 56 * 1024 * 1024
SHARES = (0.575, 0.625, 0.665, 0.705, 0.745, 0.80, 1.0)
EARLY = 3


def passed_along(block, axis, distance):
    devices = range(lax.axis_size(axis))
    route = [(i - distance, i) for i in devices if i - distance in devices]
    return lax.ppermute(block, axis, route)


def packed_shape(keep, width, blk):
    blocks = (width * keep + blk - 1) // blk
    rows = (keep + 7) // 8 * 8
    return blocks, rows, (blocks * rows + 15) // 16 * 16


def start_of(plan, unit, width, blk, chunk):
    count = 0
    end = 0
    start = 0
    for u in range(unit + 1):
        start = jnp.maximum(end, u * chunk)
        count = packed_shape(plan[units_of(plan) + u], width, blk)[2]
        end = start + count
    return start, count


def units_of(plan):
    return plan.shape[0] // 4


def plan_kernel(width, me_ref, sector_ref, kept_ref, src_ref, dst_ref, plan_ref):
    per_dev = src_ref.shape[0]
    blk = src_ref.shape[-1]
    room = units_of(plan_ref)
    first = me_ref[0] * per_dev
    for i in range(per_dev):
        owner = sector_ref[first + i] // per_dev
        dst_ref[owner] = src_ref[i]
    kept = [kept_ref[i] for i in range(per_dev)]

    def before(i, j):
        return kept[i] > kept[j] if i > j else kept[i] >= kept[j]

    def rank(j, members):
        total = jnp.int32(0)
        for i, inside in members:
            if i != j:
                total = total + (before(i, j) & inside).astype(jnp.int32)
        return total

    top = [(i, True) for i in range(2, per_dev)]
    high = {j: rank(j, top) for j in range(2, per_dev)}
    rest = [(0, True), (1, True)] + [(i, high[i] >= EARLY) for i in range(2, per_dev)]
    place = []
    for j in range(per_dev):
        late = EARLY + rank(j, rest)
        place.append(late if j < 2 else jnp.where(high[j] < EARLY, high[j], late))
    for i in range(4 * room):
        plan_ref[i] = 0
    for j in range(per_dev):
        plan_ref[place[j]] = j + 1
        plan_ref[room + place[j]] = kept[j]

    def find(n, carry):
        slot = sector_ref[n] - first
        inside = (slot >= 0) & (slot < per_dev)

        @pl.when(inside)
        def _():
            plan_ref[3 * room + slot] = n // per_dev

        return carry

    lax.fori_loop(0, sector_ref.shape[0], find, 0)
    tail = jnp.int32(0)
    need = jnp.int32(0)
    for u in reversed(range(per_dev)):
        tail = tail + packed_shape(plan_ref[room + u], width, blk)[2]
        left = per_dev - u
        need = jnp.maximum(need, (tail + left - 1) // left)
    plan_ref[2 * room] = need


def make_plan(blocks, sector_row, kept, me, devices, width):
    scalar_spec = pl.BlockSpec(memory_space=pltpu.SMEM)
    vector_spec = pl.BlockSpec(memory_space=pltpu.VMEM)
    return pl.pallas_call(
        functools.partial(plan_kernel, width),
        in_specs=[scalar_spec, scalar_spec, scalar_spec, vector_spec],
        out_specs=[vector_spec, scalar_spec],
        out_shape=[
            jax.ShapeDtypeStruct((devices,) + blocks.shape[1:], blocks.dtype),
            jax.ShapeDtypeStruct((32,), jnp.int32),
        ],
        name="make_plan",
    )(me.reshape(1), sector_row, kept, blocks)


def sector_kernel(unit, chunk, late, plan, row, op, table, *refs):
    if late:
        lower, refs = refs[0], refs[1:]
    env, iso_all, sing = refs[:3]
    (
        env_right,
        stream,
        piece,
        e,
        iso,
        placed_t,
        mixer,
        left,
        prod,
        out,
        stage,
        packed,
        in_sems,
        out_sems,
    ) = refs[-14:]
    room = units_of(plan)
    width, blk = e.shape[1], e.shape[-1]
    nops = table.shape[0] // 16
    slot = plan[unit] - 1
    keep = plan[room + unit]
    start, _ = start_of(plan, unit, width, blk, chunk)
    half = width // 2

    iso_copy = pltpu.make_async_copy(iso_all.at[plan[3 * room + slot]], iso, in_sems.at[0])
    iso_copy.start()
    env_copies = []
    for part in range(2):
        for c in range(3):
            rows = pl.ds(part * half, half)
            sem = in_sems.at[1 + 3 * part + c]
            target = e.at[c, rows]
            usual = pltpu.make_async_copy(env.at[0, jnp.maximum(slot - c, 0), rows], target, sem)
            if late and c:
                passed = pltpu.make_async_copy(
                    lower.at[jnp.clip(slot - c + 2, 0, 1), rows], target, sem
                )

                @pl.when(slot >= c)
                def _(usual=usual):
                    usual.start()

                @pl.when(slot < c)
                def _(passed=passed):
                    passed.start()

            else:
                usual.start()
            env_copies.append(usual)

    lane = lax.broadcasted_iota(jnp.int32, (blk, blk), 1)
    high = lax.broadcasted_iota(jnp.int32, (blk, blk), 0)
    inside = lane < keep
    scale = jnp.where(inside[:1], 1.0 / sing[pl.ds(slot, 1), :], 0.0)
    scale = scale.astype(jnp.bfloat16).astype(jnp.float32)
    scale = jnp.broadcast_to(scale, (blk, blk))
    outer = scale * scale.T

    iso_copy.wait()
    placed = []
    for s in range(4):
        value = jnp.where(inside, iso[s].astype(jnp.float32), 0.0)
        placed.append(value)
        placed_t[s * blk : (s + 1) * blk, :] = value.T.astype(jnp.bfloat16)
    for x in range(nops):
        for p in range(4):
            total = None
            for s in range(4):
                if CHARGES[p] == CHARGES[s]:
                    term = table[x * 16 + p * 4 + s] * placed[s]
                    total = term if total is None else total + term
            mixer[p * blk : (p + 1) * blk, x * blk : (x + 1) * blk] = total.astype(jnp.bfloat16)

    tall = (keep + 15) // 16 * 16

    def bra_step(w, carry):
        rows = pl.ds(pl.multiple_of(w * tall, 16), blk)
        first = jnp.dot(placed_t[0:blk], e[0, w], preferred_element_type=jnp.float32)
        middle = jnp.dot(placed_t[blk : 3 * blk], e[1, w], preferred_element_type=jnp.float32)
        last = jnp.dot(placed_t[3 * blk :], e[2, w], preferred_element_type=jnp.float32)
        left[rows, 0:blk] = first.astype(jnp.bfloat16)
        left[rows, blk : 2 * blk] = middle[:blk].astype(jnp.bfloat16)
        left[rows, 2 * blk : 3 * blk] = middle[blk:].astype(jnp.bfloat16)
        left[rows, 3 * blk :] = last.astype(jnp.bfloat16)
        return carry

    for part in range(2):
        for c in range(3):
            env_copies[3 * part + c].wait()
        lax.fori_loop(part * half, (part + 1) * half, bra_step, 0, unroll=half)

    def ket_step(i, carry):
        rows = pl.ds(pl.multiple_of(i * (16 * width), 16), 16 * width)
        for x in range(0, nops, 2):
            pair = jnp.dot(
                left[rows, :],
                mixer[:, x * blk : (x + 2) * blk],
                preferred_element_type=jnp.float32,
            )
            prod[x, rows, :] = pair[:, :blk]
            prod[x + 1, rows, :] = pair[:, blk:]
        return carry

    lax.fori_loop(0, tall // 16, ket_step, 0)

    _, rows8, count = packed_shape(keep, width, blk)
    live = high < keep

    def column_step(v, current):
        total = None
        for t in range(3):
            begin = pl.multiple_of(row[v * 3 + t] * tall, 16)
            term = prod[op[v * 3 + t], pl.ds(begin, blk), :]
            total = term if total is None else total + term
        value = jnp.where(live, total, 0.0).astype(jnp.bfloat16)
        out[v] = value
        shift = (v * keep) % blk
        turned = pltpu.roll(value.astype(jnp.float32) * outer, shift, 1)
        current = jnp.where(lane < shift, current, turned)
        stage[pl.ds(pl.multiple_of((v * keep) // blk * rows8, 8), blk), :] = current
        return jnp.where(shift + keep >= blk, turned, current)

    current = jnp.zeros((blk, blk), jnp.float32)
    out_copies = []
    for part in range(2):
        current = lax.fori_loop(part * half, (part + 1) * half, column_step, current)
        rows = pl.ds(part * half, half)
        copy = pltpu.make_async_copy(out.at[rows], env_right.at[0, slot, rows], out_sems.at[part])
        copy.start()
        out_copies.append(copy)
    stage[pl.ds(pl.multiple_of((width * keep) // blk * rows8, 8), blk), :] = current

    def cast_step(i, carry):
        rows = pl.ds(pl.multiple_of(i * blk, blk), blk)
        packed[rows, :] = stage[rows, :].astype(jnp.bfloat16)
        return carry

    lax.fori_loop(0, (count + blk - 1) // blk, cast_step, 0)
    write = pltpu.make_async_copy(
        packed,
        stream.at[pl.ds(pl.multiple_of(start, 16), packed.shape[0]), :],
        out_sems.at[2],
    )
    write.start()
    write.wait()
    cut = pltpu.make_async_copy(
        stream.at[pl.ds(unit * chunk, chunk), :], piece, out_sems.at[3]
    )
    cut.start()
    cut.wait()
    for copy in out_copies:
        copy.wait()


def sector_call(unit, chunk, scalars, env, lower, isom, sing, env_right, stream):
    width, blk = env.shape[2], env.shape[3]
    units = env.shape[1]
    nops = scalars[3].shape[0] // 16
    any_spec = pl.BlockSpec(memory_space=pl.ANY)
    operands = [env, isom, sing]
    in_specs = [any_spec, any_spec, pl.BlockSpec(memory_space=pltpu.VMEM)]
    if lower is not None:
        operands.insert(0, lower)
        in_specs.insert(0, any_spec)
    aliases = {}
    for index, array in ((0, env_right), (1, stream)):
        if array is not None:
            aliases[len(scalars) + len(operands)] = index
            operands.append(array)
            in_specs.append(any_spec)
    rows = width * blk
    stream_shape = (units * chunk + rows, blk)
    bf16, f32 = jnp.bfloat16, jnp.float32
    return pl.pallas_call(
        functools.partial(sector_kernel, unit, chunk, lower is not None),
        in_specs=[pl.BlockSpec(memory_space=pltpu.SMEM)] * len(scalars) + in_specs,
        out_specs=[any_spec] * 3,
        out_shape=[
            jax.ShapeDtypeStruct(env.shape, bf16),
            jax.ShapeDtypeStruct(stream_shape, bf16),
            jax.ShapeDtypeStruct((chunk, blk), bf16),
        ],
        scratch_shapes=[
            pltpu.VMEM((3, width, blk, blk), bf16),
            pltpu.VMEM((4, blk, blk), bf16),
            pltpu.VMEM((4 * blk, blk), bf16),
            pltpu.VMEM((4 * blk, nops * blk), bf16),
            pltpu.VMEM((rows, 4 * blk), bf16),
            pltpu.VMEM((nops, rows, blk), f32),
            pltpu.VMEM((width, blk, blk), bf16),
            pltpu.VMEM((rows + blk, blk), f32),
            pltpu.VMEM((rows, blk), bf16),
            pltpu.SemaphoreType.DMA((7,)),
            pltpu.SemaphoreType.DMA((4,)),
        ],
        input_output_aliases=aliases,
        compiler_params=pltpu.CompilerParams(vmem_limit_bytes=VMEM_LIMIT),
        cost_estimate=pl.CostEstimate(
            flops=2 * rows * blk * blk, bytes_accessed=rows * blk, transcendentals=0
        ),
        name=f"sector_{unit}",
    )(*scalars, *operands)


def unpack_kernel(chunk, before, after, begin, plan, *refs):
    count = after - begin
    pieces = refs[:count]
    handoff, held, stage, out, in_sems, out_sems = refs[-6:]
    room = units_of(plan)
    width, blk = out.shape[1], out.shape[-1]
    units = handoff.shape[1]
    copies = []
    for i in range(count):
        copy = pltpu.make_async_copy(
            pieces[i], held.at[pl.ds(i * chunk, chunk), :], in_sems.at[i]
        )
        copy.start()
        copies.append(copy)
    for copy in copies:
        copy.wait()
    lane = lax.broadcasted_iota(jnp.int32, (blk, blk), 1)
    high = lax.broadcasted_iota(jnp.int32, (blk, blk), 0)

    def store(turn, slot):
        return pltpu.make_async_copy(out.at[turn], handoff.at[0, slot], out_sems.at[turn])

    def unit_step(u, carry):
        end, done = carry
        code = plan[u]
        keep = plan[room + u]
        slot = jnp.where(code > 0, code - 1, u)
        _, rows8, rows = packed_shape(keep, width, blk)
        start = jnp.maximum(end, u * chunk)
        end = start + rows
        active = (end > before * chunk) & (end <= after * chunk)
        if before == 0:
            active = end <= after * chunk
        turn = done % 2

        @pl.when(active)
        def _():
            @pl.when(done >= 2)
            def _():
                store(turn, slot).wait()

            shift_rows = start - begin * chunk

            def cast_step(i, carry):
                source = pl.ds(pl.multiple_of(shift_rows + i * blk, 16), blk)
                target = pl.ds(pl.multiple_of(i * blk, blk), blk)
                stage[target, :] = held[source, :].astype(jnp.float32)
                return carry

            lax.fori_loop(0, (rows + blk - 1) // blk, cast_step, 0)
            live = (high < keep) & (lane < keep)

            def column_step(v, carry):
                shift = (v * keep) % blk
                base = pl.multiple_of((v * keep) // blk * rows8, 8)
                this = stage[pl.ds(base, blk), :]
                following = stage[pl.ds(pl.multiple_of(base + rows8, 8), blk), :]
                value = jnp.where(lane >= shift, this, following)
                value = pltpu.roll(value, (blk - shift) % blk, 1)
                out[turn, v] = jnp.where(live, value, 0.0).astype(jnp.bfloat16)
                return carry

            lax.fori_loop(0, width, column_step, 0, unroll=2)
            store(turn, slot).start()

        return end, done + active.astype(jnp.int32)

    _, done = lax.fori_loop(0, units, unit_step, (jnp.int32(0), jnp.int32(0)))

    for back in (1, 2):

        @pl.when(done >= back)
        def _(back=back):
            store((done - back) % 2, 0).wait()


def unpack_call(chunk, before, after, plan, pieces, handoff, shape):
    width, blk = shape[2], shape[3]
    rows = width * blk
    begin = max(0, before - -(-rows // chunk)) if before else 0
    any_spec = pl.BlockSpec(memory_space=pl.ANY)
    operands = list(pieces[begin:after])
    aliases = {}
    if handoff is not None:
        aliases[1 + len(operands)] = 0
        operands.append(handoff)
    return pl.pallas_call(
        functools.partial(unpack_kernel, chunk, before, after, begin),
        in_specs=[pl.BlockSpec(memory_space=pltpu.SMEM)] + [any_spec] * len(operands),
        out_specs=any_spec,
        out_shape=jax.ShapeDtypeStruct(shape, jnp.bfloat16),
        scratch_shapes=[
            pltpu.VMEM(((after - begin) * chunk + blk, blk), jnp.bfloat16),
            pltpu.VMEM((rows + 2 * blk, blk), jnp.float32),
            pltpu.VMEM((2, width, blk, blk), jnp.bfloat16),
            pltpu.SemaphoreType.DMA((after - begin,)),
            pltpu.SemaphoreType.DMA((2,)),
        ],
        input_output_aliases=aliases,
        compiler_params=pltpu.CompilerParams(vmem_limit_bytes=VMEM_LIMIT),
        name=f"unpack_{after}",
    )(plan, *operands)


def sweep(chunk, scalars, plan_before, env_left, isom, sing):
    units = env_left.shape[1]
    env_right = stream = lower = handoff = None
    pieces = []
    for unit in range(units):
        env_right, stream, piece = sector_call(
            unit,
            chunk,
            scalars,
            env_left,
            lower if unit >= EARLY else None,
            isom,
            sing,
            env_right,
            stream,
        )
        if unit == 0:
            late_env, _ = lax.optimization_barrier((env_left[0, units - 2 :], piece))
            lower = passed_along(late_env, "sec", 1)
        pieces.append(passed_along(piece, "seg", 1))
    before = 0
    for after in (units - 2, units - 1, units):
        handoff = unpack_call(
            chunk, before, after, plan_before, pieces, handoff, env_left.shape
        )
        before = after
    return env_right, handoff


def body(env_left, isometry, sing_vals, kept, twosite_sector, mpo_row, mpo_op, op_table):
    my_index = lax.axis_index("sec")
    devices = lax.axis_size("sec")
    width, blk = env_left.shape[2], env_left.shape[3]
    routed, plan = make_plan(
        isometry[0, 0], twosite_sector[0, 0], kept[SITES - 1, 0], my_index, devices, width
    )
    isom = lax.all_to_all(routed, "sec", 0, 0, tiled=True)
    room = plan.shape[0] // 4
    need = lax.pmax(plan[2 * room], ("seg", "sec"))
    plan_before = passed_along(plan, "seg", 1)
    chunks = [int(round(share * width * blk / 16)) * 16 for share in SHARES]
    level = sum((need > chunk).astype(jnp.int32) for chunk in chunks[:-1])
    scalars = (plan, mpo_row.reshape(-1), mpo_op.reshape(-1), op_table.reshape(-1))
    branches = [functools.partial(sweep, chunk) for chunk in chunks]
    return lax.switch(
        level, branches, scalars, plan_before, env_left, isom, sing_vals[0]
    )


def solution(mesh):
    in_specs = (
        P("seg", "sec", None, None, None),
        P(None, "seg", "sec", None, None, None),
        P("seg", "sec", None),
        P(None, "seg", "sec"),
        P(None, "seg", None),
        P(),
        P(),
        P(),
    )
    out_specs = (P("seg", "sec", None, None, None), P("seg", "sec", None, None, None))
    return jax.shard_map(body, mesh=mesh, in_specs=in_specs, out_specs=out_specs, check_vma=False)
```

```python
import functools

import jax
import jax.numpy as jnp
from jax import lax
from jax.experimental import pallas as pl
from jax.experimental.pallas import tpu as pltpu
from jax.sharding import PartitionSpec as P

SITES = 1
CHARGES = (0, 1, 1, 2)
VMEM_LIMIT = 56 * 1024 * 1024
BASE = 0.6
TAILS = (0.63, 0.66, 0.69, 0.72, 0.75, 0.79, 0.85, 1.0)
MESH = pl.DeviceIdType.MESH
EARLY = 3


def passed_along(block, axis, distance):
    devices = range(lax.axis_size(axis))
    route = [(i - distance, i) for i in devices if i - distance in devices]
    return lax.ppermute(block, axis, route)


def packed_shape(keep, width, blk):
    blocks = (width * keep + blk - 1) // blk
    rows = (keep + 7) // 8 * 8
    return blocks, rows, (blocks * rows + 15) // 16 * 16


def begin_of(plan, unit, width, blk, chunk):
    end = jnp.int32(0)
    begin = jnp.int32(0)
    for u in range(unit + 1):
        begin = jnp.maximum(end, u * chunk)
        end = begin + packed_shape(plan[units_of(plan) + u], width, blk)[2]
    return begin, end


def units_of(plan):
    return plan.shape[0] // 4


def plan_kernel(width, chunk, me_ref, sector_ref, kept_ref, src_ref, dst_ref, plan_ref, tile_ref):
    per_dev = src_ref.shape[0]
    blk = src_ref.shape[-1]
    room = units_of(plan_ref)
    first = me_ref[0] * per_dev
    for i in range(per_dev):
        owner = sector_ref[first + i] // per_dev
        dst_ref[owner] = src_ref[i]
    kept = [kept_ref[i] for i in range(per_dev)]

    def before(i, j):
        return kept[i] > kept[j] if i > j else kept[i] >= kept[j]

    def rank(j, members):
        total = jnp.int32(0)
        for i, inside in members:
            if i != j:
                total = total + (before(i, j) & inside).astype(jnp.int32)
        return total

    top = [(i, True) for i in range(2, per_dev)]
    high = {j: rank(j, top) for j in range(2, per_dev)}
    rest = [(0, True), (1, True)] + [(i, high[i] >= EARLY) for i in range(2, per_dev)]
    place = []
    for j in range(per_dev):
        late = EARLY + rank(j, rest)
        place.append(late if j < 2 else jnp.where(high[j] < EARLY, high[j], late))
    for i in range(4 * room):
        plan_ref[i] = 0
    for j in range(per_dev):
        plan_ref[place[j]] = j + 1
        plan_ref[room + place[j]] = kept[j]

    def find(n, carry):
        slot = sector_ref[n] - first
        inside = (slot >= 0) & (slot < per_dev)

        @pl.when(inside)
        def _():
            plan_ref[3 * room + slot] = n // per_dev

        return carry

    lax.fori_loop(0, sector_ref.shape[0], find, 0)
    _, end = begin_of(plan_ref, per_dev - 1, width, blk, chunk)
    plan_ref[2 * room] = jnp.maximum(end - per_dev * chunk, 0)
    lane = lax.broadcasted_iota(jnp.int32, tile_ref.shape, 1)
    tile = jnp.zeros(tile_ref.shape, jnp.int32)
    for i in list(range(per_dev)) + list(range(room, room + per_dev)) + [2 * room]:
        tile = jnp.where(lane == i, plan_ref[i], tile)
    tile_ref[...] = tile


def make_plan(blocks, sector_row, kept, me, devices, width, chunk):
    scalar_spec = pl.BlockSpec(memory_space=pltpu.SMEM)
    vector_spec = pl.BlockSpec(memory_space=pltpu.VMEM)
    return pl.pallas_call(
        functools.partial(plan_kernel, width, chunk),
        in_specs=[scalar_spec, scalar_spec, scalar_spec, vector_spec],
        out_specs=[vector_spec, scalar_spec, vector_spec],
        out_shape=[
            jax.ShapeDtypeStruct((devices,) + blocks.shape[1:], blocks.dtype),
            jax.ShapeDtypeStruct((32,), jnp.int32),
            jax.ShapeDtypeStruct((8, 128), jnp.int32),
        ],
        name="make_plan",
    )(me.reshape(1), sector_row, kept, blocks)


def exchange_kernel(
    devices,
    segments,
    routed,
    tile,
    isom,
    before,
    most,
    tiles,
    mine,
    ends,
    block_sems,
    tile_sems,
    end_sems,
    own_sem,
):
    me = lax.axis_index("sec")
    seg = lax.axis_index("seg")
    peers = [lax.rem(me + k, devices) for k in range(1, devices)]
    others = [lax.rem(seg + k, segments) for k in range(1, segments)]
    barrier = pltpu.get_barrier_semaphore()
    for peer in peers:
        pl.semaphore_signal(barrier, inc=1, device_id={"sec": peer}, device_id_type=MESH)
    for other in others:
        pl.semaphore_signal(barrier, inc=1, device_id={"seg": other}, device_id_type=MESH)
    pl.semaphore_wait(barrier, len(peers) + len(others))

    own = pltpu.make_async_copy(routed.at[me], isom.at[me], own_sem)
    own.start()

    def along(source, target, sems, axis, index, here, there):
        return pltpu.make_async_remote_copy(
            src_ref=source,
            dst_ref=target.at[here],
            send_sem=sems.at[0, index],
            recv_sem=sems.at[1, index],
            device_id={axis: there},
            device_id_type=MESH,
        )

    tile_copies = [
        along(tile, tiles, tile_sems, "sec", i, me, peer) for i, peer in enumerate(peers)
    ]
    block_copies = [
        along(routed.at[peer], isom, block_sems, "sec", i, me, peer)
        for i, peer in enumerate(peers)
    ]
    for copy in tile_copies + block_copies:
        copy.start()
    tiles[me] = tile[...]
    for copy in tile_copies:
        copy.wait()
    total = tiles[0]
    for i in range(1, devices):
        total = jnp.maximum(total, tiles[i])
    mine[0] = tile[...]
    mine[1] = total
    end_copies = [
        along(mine, ends, end_sems, "seg", i, seg, other) for i, other in enumerate(others)
    ]
    for copy in end_copies:
        copy.start()
    ends[seg] = mine[...]
    for copy in end_copies:
        copy.wait()
    total = ends[0, 1]
    for i in range(1, segments):
        total = jnp.maximum(total, ends[i, 1])
    most[...] = total
    before[...] = jnp.where(seg > 0, ends[jnp.maximum(seg - 1, 0), 0], 0)
    for copy in block_copies:
        copy.wait()
    own.wait()


def exchange(routed, tile, devices, segments):
    any_spec = pl.BlockSpec(memory_space=pltpu.HBM)
    vector_spec = pl.BlockSpec(memory_space=pltpu.VMEM)
    small = jax.ShapeDtypeStruct(tile.shape, tile.dtype)
    return pl.pallas_call(
        functools.partial(exchange_kernel, devices, segments),
        in_specs=[any_spec, vector_spec],
        out_specs=[any_spec, vector_spec, vector_spec],
        out_shape=[jax.ShapeDtypeStruct(routed.shape, routed.dtype), small, small],
        scratch_shapes=[
            pltpu.VMEM((devices,) + tile.shape, tile.dtype),
            pltpu.VMEM((2,) + tile.shape, tile.dtype),
            pltpu.VMEM((segments, 2) + tile.shape, tile.dtype),
            pltpu.SemaphoreType.DMA((2, devices - 1)),
            pltpu.SemaphoreType.DMA((2, devices - 1)),
            pltpu.SemaphoreType.DMA((2, segments - 1)),
            pltpu.SemaphoreType.DMA,
        ],
        compiler_params=pltpu.CompilerParams(collective_id=0, has_side_effects=True),
        name="exchange",
    )(routed, tile)


def sector_kernel(unit, chunk, late, spill, plan, row, op, table, *refs):
    if late:
        lower, refs = refs[0], refs[1:]
    env, iso_all, sing = refs[:3]
    (
        env_right,
        piece,
        excess,
        e,
        iso,
        placed_t,
        mixer,
        left,
        prod,
        out,
        stage,
        packed,
        in_sems,
        out_sems,
    ) = refs[-14:]
    room = units_of(plan)
    width, blk = e.shape[1], e.shape[-1]
    nops = table.shape[-1]
    slot = plan[unit] - 1
    keep = plan[room + unit]
    begin, _ = begin_of(plan, unit, width, blk, chunk)
    half = width // 2

    iso_copy = pltpu.make_async_copy(iso_all.at[plan[3 * room + slot]], iso, in_sems.at[0])
    iso_copy.start()
    spill_copy = None
    if unit:
        spill_copy = pltpu.make_async_copy(
            refs[3 + (unit > 0)], packed.at[pl.ds(0, unit * spill), :], in_sems.at[7]
        )
        spill_copy.start()
    env_copies = []
    for part in range(2):
        for c in range(3):
            rows = pl.ds(part * half, half)
            sem = in_sems.at[1 + 3 * part + c]
            target = e.at[c, rows]
            usual = pltpu.make_async_copy(env.at[0, jnp.maximum(slot - c, 0), rows], target, sem)
            if late and c:
                passed = pltpu.make_async_copy(
                    lower.at[jnp.clip(slot - c + 2, 0, 1), rows], target, sem
                )

                @pl.when(slot >= c)
                def _(usual=usual):
                    usual.start()

                @pl.when(slot < c)
                def _(passed=passed):
                    passed.start()

            else:
                usual.start()
            env_copies.append(usual)

    lane = lax.broadcasted_iota(jnp.int32, (blk, blk), 1)
    high = lax.broadcasted_iota(jnp.int32, (blk, blk), 0)
    inside = lane < keep
    scale = jnp.where(inside[:1], 1.0 / sing[slot], 0.0)
    scale = scale.astype(jnp.bfloat16).astype(jnp.float32)
    scale = jnp.broadcast_to(scale, (blk, blk))
    outer = scale * scale.T

    iso_copy.wait()
    placed = []
    for s in range(4):
        value = jnp.where(inside, iso[s].astype(jnp.float32), 0.0)
        placed.append(value)
        placed_t[s * blk : (s + 1) * blk, :] = value.T.astype(jnp.bfloat16)
    for x in range(nops):
        for p in range(4):
            total = None
            for s in range(4):
                if CHARGES[p] == CHARGES[s]:
                    term = table[p, s, x] * placed[s]
                    total = term if total is None else total + term
            mixer[p * blk : (p + 1) * blk, x * blk : (x + 1) * blk] = total.astype(jnp.bfloat16)

    tall = (keep + 15) // 16 * 16

    def bra_step(w, carry):
        rows = pl.ds(pl.multiple_of(w * tall, 16), blk)
        first = jnp.dot(placed_t[0:blk], e[0, w], preferred_element_type=jnp.float32)
        middle = jnp.dot(placed_t[blk : 3 * blk], e[1, w], preferred_element_type=jnp.float32)
        last = jnp.dot(placed_t[3 * blk :], e[2, w], preferred_element_type=jnp.float32)
        left[rows, 0:blk] = first.astype(jnp.bfloat16)
        left[rows, blk : 2 * blk] = middle[:blk].astype(jnp.bfloat16)
        left[rows, 2 * blk : 3 * blk] = middle[blk:].astype(jnp.bfloat16)
        left[rows, 3 * blk :] = last.astype(jnp.bfloat16)
        return carry

    for part in range(2):
        for c in range(3):
            env_copies[3 * part + c].wait()
        lax.fori_loop(part * half, (part + 1) * half, bra_step, 0, unroll=half)

    def ket_step(i, carry):
        rows = pl.ds(pl.multiple_of(i * (16 * width), 16), 16 * width)
        for x in range(0, nops, 2):
            pair = jnp.dot(
                left[rows, :],
                mixer[:, x * blk : (x + 2) * blk],
                preferred_element_type=jnp.float32,
            )
            prod[x, rows, :] = pair[:, :blk]
            prod[x + 1, rows, :] = pair[:, blk:]
        return carry

    lax.fori_loop(0, tall // 16, ket_step, 0)

    _, rows8, count = packed_shape(keep, width, blk)
    live = high < keep

    def column_step(v, current):
        total = None
        for t in range(3):
            begin = pl.multiple_of(row[t, v] * tall, 16)
            term = prod[op[t, v], pl.ds(begin, blk), :]
            total = term if total is None else total + term
        value = jnp.where(live, total, 0.0).astype(jnp.bfloat16)
        out[v] = value
        shift = (v * keep) % blk
        turned = pltpu.roll(value.astype(jnp.float32) * outer, shift, 1)
        current = jnp.where(lane < shift, current, turned)
        stage[pl.ds(pl.multiple_of((v * keep) // blk * rows8, 8), blk), :] = current
        return jnp.where(shift + keep >= blk, turned, current)

    current = jnp.zeros((blk, blk), jnp.float32)
    out_copies = []
    for part in range(2):
        current = lax.fori_loop(part * half, (part + 1) * half, column_step, current)
        rows = pl.ds(part * half, half)
        copy = pltpu.make_async_copy(out.at[rows], env_right.at[0, slot, rows], out_sems.at[part])
        copy.start()
        out_copies.append(copy)
    stage[pl.ds(pl.multiple_of((width * keep) // blk * rows8, 8), blk), :] = current

    if spill_copy is not None:
        spill_copy.wait()

    def cast_step(i, carry):
        source = pl.ds(pl.multiple_of(i * blk, blk), blk)
        target = pl.ds(pl.multiple_of(begin - unit * chunk + i * blk, 16), blk)
        packed[target, :] = stage[source, :].astype(jnp.bfloat16)
        return carry

    lax.fori_loop(0, (count + blk - 1) // blk, cast_step, 0)
    out_copies.append(
        pltpu.make_async_copy(packed.at[pl.ds(0, chunk), :], piece, out_sems.at[2])
    )
    out_copies[-1].start()
    out_copies.append(
        pltpu.make_async_copy(
            packed.at[pl.ds(chunk, (unit + 1) * spill), :], excess, out_sems.at[3]
        )
    )
    out_copies[-1].start()
    for copy in out_copies:
        copy.wait()


def sector_call(unit, chunk, scalars, env, lower, isom, sing, env_right, excess, arrived):
    width, blk = env.shape[2], env.shape[3]
    nops = scalars[3].shape[-1]
    hbm_spec = pl.BlockSpec(memory_space=pltpu.HBM)
    operands = [env, isom, sing]
    in_specs = [hbm_spec, hbm_spec, pl.BlockSpec(memory_space=pltpu.VMEM)]
    if lower is not None:
        operands.insert(0, lower)
        in_specs.insert(0, hbm_spec)
    aliases = {}
    if unit:
        aliases[len(scalars) + len(operands)] = 0
    extra = [array for array in (env_right, excess, arrived) if array is not None]
    operands += extra
    in_specs += [hbm_spec] * len(extra)
    rows = width * blk
    spill = rows - chunk
    bf16, f32 = jnp.bfloat16, jnp.float32
    return pl.pallas_call(
        functools.partial(sector_kernel, unit, chunk, lower is not None, spill),
        in_specs=[pl.BlockSpec(memory_space=pltpu.SMEM)] * len(scalars) + in_specs,
        out_specs=[hbm_spec] * 3,
        out_shape=[
            jax.ShapeDtypeStruct(env.shape, bf16),
            jax.ShapeDtypeStruct((chunk, blk), bf16),
            jax.ShapeDtypeStruct(((unit + 1) * spill, blk), bf16),
        ],
        scratch_shapes=[
            pltpu.VMEM((3, width, blk, blk), bf16),
            pltpu.VMEM((4, blk, blk), bf16),
            pltpu.VMEM((4 * blk, blk), bf16),
            pltpu.VMEM((4 * blk, nops * blk), bf16),
            pltpu.VMEM((rows, 4 * blk), bf16),
            pltpu.VMEM((nops, rows, blk), f32),
            pltpu.VMEM((width, blk, blk), bf16),
            pltpu.VMEM((rows + blk, blk), f32),
            pltpu.VMEM((unit * spill + rows + blk, blk), bf16),
            pltpu.SemaphoreType.DMA((8,)),
            pltpu.SemaphoreType.DMA((4,)),
        ],
        input_output_aliases=aliases,
        compiler_params=pltpu.CompilerParams(vmem_limit_bytes=VMEM_LIMIT),
        cost_estimate=pl.CostEstimate(
            flops=2 * rows * blk * blk, bytes_accessed=rows * blk, transcendentals=0
        ),
        name=f"sector_{unit}",
    )(*scalars, *operands)


def unpack_kernel(chunk, before, after, begin, last, plan, *refs):
    pieces = refs[: after - begin + last]
    handoff, held, stage, out, in_sems, out_sems = refs[-6:]
    room = 8
    width, blk = out.shape[1], out.shape[-1]
    units = handoff.shape[1]
    copies = []
    at = 0
    for i, piece in enumerate(pieces):
        copy = pltpu.make_async_copy(
            piece, held.at[pl.ds(at, piece.shape[0]), :], in_sems.at[i]
        )
        copy.start()
        copies.append(copy)
        at += piece.shape[0]
    for copy in copies:
        copy.wait()
    lane = lax.broadcasted_iota(jnp.int32, (blk, blk), 1)
    high = lax.broadcasted_iota(jnp.int32, (blk, blk), 0)

    def store(turn, slot):
        return pltpu.make_async_copy(out.at[turn], handoff.at[0, slot], out_sems.at[turn])

    def unit_step(u, carry):
        end, done = carry
        code = plan[0, u]
        keep = plan[0, room + u]
        slot = jnp.where(code > 0, code - 1, u)
        _, rows8, rows = packed_shape(keep, width, blk)
        start = jnp.maximum(end, u * chunk)
        end = start + rows
        active = jnp.bool_(True)
        if before:
            active = active & (end > before * chunk)
        if not last:
            active = active & (end <= after * chunk)
        turn = done % 2

        @pl.when(active)
        def _():
            @pl.when(done >= 2)
            def _():
                store(turn, slot).wait()

            shift_rows = start - begin * chunk

            def cast_step(i, carry):
                source = pl.ds(pl.multiple_of(shift_rows + i * blk, 16), blk)
                target = pl.ds(pl.multiple_of(i * blk, blk), blk)
                stage[target, :] = held[source, :].astype(jnp.float32)
                return carry

            lax.fori_loop(0, (rows + blk - 1) // blk, cast_step, 0)
            live = (high < keep) & (lane < keep)

            def column_step(v, carry):
                shift = (v * keep) % blk
                base = pl.multiple_of((v * keep) // blk * rows8, 8)
                this = stage[pl.ds(base, blk), :]
                following = stage[pl.ds(pl.multiple_of(base + rows8, 8), blk), :]
                value = jnp.where(lane >= shift, this, following)
                value = pltpu.roll(value, (blk - shift) % blk, 1)
                out[turn, v] = jnp.where(live, value, 0.0).astype(jnp.bfloat16)
                return carry

            lax.fori_loop(0, width, column_step, 0, unroll=2)
            store(turn, slot).start()

        return end, done + active.astype(jnp.int32)

    _, done = lax.fori_loop(0, units, unit_step, (jnp.int32(0), jnp.int32(0)))

    for back in (1, 2):

        @pl.when(done >= back)
        def _(back=back):
            store((done - back) % 2, 0).wait()


def unpack_call(chunk, before, after, plan, pieces, tail, handoff, shape):
    width, blk = shape[2], shape[3]
    rows = width * blk
    begin = max(0, before - -(-rows // chunk)) if before else 0
    hbm_spec = pl.BlockSpec(memory_space=pltpu.HBM)
    operands = list(pieces[begin:after]) + ([] if tail is None else [tail])
    count = len(operands)
    held = sum(piece.shape[0] for piece in operands)
    aliases = {}
    if handoff is not None:
        aliases[1 + count] = 0
        operands.append(handoff)
    return pl.pallas_call(
        functools.partial(unpack_kernel, chunk, before, after, begin, tail is not None),
        in_specs=[pl.BlockSpec(memory_space=pltpu.SMEM)] + [hbm_spec] * len(operands),
        out_specs=hbm_spec,
        out_shape=jax.ShapeDtypeStruct(shape, jnp.bfloat16),
        scratch_shapes=[
            pltpu.VMEM((held + blk, blk), jnp.bfloat16),
            pltpu.VMEM((rows + 2 * blk, blk), jnp.float32),
            pltpu.VMEM((2, width, blk, blk), jnp.bfloat16),
            pltpu.SemaphoreType.DMA((count,)),
            pltpu.SemaphoreType.DMA((2,)),
        ],
        input_output_aliases=aliases,
        compiler_params=pltpu.CompilerParams(vmem_limit_bytes=VMEM_LIMIT),
        name=f"unpack_{after}",
    )(plan, *operands)


def send_tail(rows, excess):
    if not rows:
        return excess
    got = passed_along(excess[:rows], "seg", 1)
    return lax.dynamic_update_slice(excess, got, (0, 0))


def body(env_left, isometry, sing_vals, kept, twosite_sector, mpo_row, mpo_op, op_table):
    my_index = lax.axis_index("sec")
    devices, segments = lax.axis_size("sec"), lax.axis_size("seg")
    units, width, blk = env_left.shape[1:4]
    rows = width * blk
    chunk = int(rows * BASE) // 16 * 16
    routed, plan, tile = make_plan(
        isometry[0, 0], twosite_sector[0, 0], kept[SITES - 1, 0], my_index, devices, width, chunk
    )
    isom, plan_before, most = exchange(routed, tile, devices, segments)
    scalars = (plan, mpo_row.T, mpo_op.T, jnp.transpose(op_table, (1, 2, 0)))
    sing = jnp.transpose(sing_vals, (1, 0, 2))
    env_right = excess = lower = handoff = None
    pieces = []
    for unit in range(units):
        env_right, piece, excess = sector_call(
            unit,
            chunk,
            scalars,
            env_left,
            lower if unit >= EARLY else None,
            isom,
            sing,
            env_right,
            excess,
            pieces[unit - 2] if unit > 1 else None,
        )
        if unit == 0:
            late_env, _ = lax.optimization_barrier((env_left[0, units - 2 :], piece))
            lower = passed_along(late_env, "sec", 1)
        pieces.append(passed_along(piece, "seg", 1))
    handoff = unpack_call(chunk, 0, units - 2, plan_before, pieces, None, None, env_left.shape)
    limits = [0]
    for share in TAILS:
        limit = int(units * (share * rows - chunk)) // 16 * 16
        limits.append(min(limit + 16, units * (rows - chunk)))
    room = plan.shape[0] // 4
    need = most[0, 2 * room]
    level = sum((need > limit).astype(jnp.int32) for limit in limits[:-1])
    branches = [functools.partial(send_tail, limit) for limit in limits]
    tail = lax.switch(level, branches, excess)
    handoff = unpack_call(
        chunk, units - 2, units, plan_before, pieces, tail, handoff, env_left.shape
    )
    return env_right, handoff


def solution(mesh):
    in_specs = (
        P("seg", "sec", None, None, None),
        P(None, "seg", "sec", None, None, None),
        P("seg", "sec", None),
        P(None, "seg", "sec"),
        P(None, "seg", None),
        P(),
        P(),
        P(),
    )
    out_specs = (P("seg", "sec", None, None, None), P("seg", "sec", None, None, None))
    return jax.shard_map(body, mesh=mesh, in_specs=in_specs, out_specs=out_specs, check_vma=False)
```

```python
import functools

import jax
import jax.numpy as jnp
from jax import lax
from jax.experimental import pallas as pl
from jax.experimental.pallas import tpu as pltpu
from jax.sharding import PartitionSpec as P

SITES = 1
CHARGES = (0, 1, 1, 2)
VMEM_LIMIT = 56 * 1024 * 1024
BASE = 0.6
TOTALS = (0.57, 0.60, 0.63, 0.66, 0.69, 0.72, 0.75, 0.79, 0.85, 1.0)
COST = 142606336
MESH = pl.DeviceIdType.MESH
EARLY = 4


def passed_along(block, axis, distance):
    devices = range(lax.axis_size(axis))
    route = [(i - distance, i) for i in devices if i - distance in devices]
    return lax.ppermute(block, axis, route)


def packed_shape(keep, width, blk):
    blocks = (width * keep + blk - 1) // blk
    rows = (keep + 7) // 8 * 8
    return blocks, rows, (blocks * rows + 15) // 16 * 16


def begin_of(plan, unit, width, blk, chunk):
    end = jnp.int32(0)
    begin = jnp.int32(0)
    for u in range(unit + 1):
        begin = jnp.maximum(end, u * chunk)
        end = begin + packed_shape(plan[units_of(plan) + u], width, blk)[2]
    return begin, end


def units_of(plan):
    return plan.shape[0] // 4


def plan_kernel(width, chunk, me_ref, sector_ref, kept_ref, src_ref, dst_ref, plan_ref, tile_ref):
    per_dev = src_ref.shape[0]
    blk = src_ref.shape[-1]
    room = units_of(plan_ref)
    first = me_ref[0] * per_dev
    for i in range(per_dev):
        owner = sector_ref[first + i] // per_dev
        dst_ref[owner] = src_ref[i]
    kept = [kept_ref[i] for i in range(per_dev)]

    def before(i, j):
        return kept[i] > kept[j] if i > j else kept[i] >= kept[j]

    def rank(j, members):
        total = jnp.int32(0)
        for i, inside in members:
            if i != j:
                total = total + (before(i, j) & inside).astype(jnp.int32)
        return total

    top = [(i, True) for i in range(2, per_dev)]
    high = {j: rank(j, top) for j in range(2, per_dev)}
    rest = [(0, True), (1, True)] + [(i, high[i] >= EARLY) for i in range(2, per_dev)]
    place = []
    for j in range(per_dev):
        late = EARLY + rank(j, rest)
        place.append(late if j < 2 else jnp.where(high[j] < EARLY, high[j], late))
    for i in range(4 * room):
        plan_ref[i] = 0
    for j in range(per_dev):
        plan_ref[place[j]] = j + 1
        plan_ref[room + place[j]] = kept[j]

    def find(n, carry):
        slot = sector_ref[n] - first
        inside = (slot >= 0) & (slot < per_dev)

        @pl.when(inside)
        def _():
            plan_ref[3 * room + slot] = n // per_dev

        return carry

    lax.fori_loop(0, sector_ref.shape[0], find, 0)
    _, end = begin_of(plan_ref, per_dev - 1, width, blk, chunk)
    plan_ref[2 * room] = end - (per_dev - 1) * chunk
    lane = lax.broadcasted_iota(jnp.int32, tile_ref.shape, 1)
    tile = jnp.zeros(tile_ref.shape, jnp.int32)
    for i in list(range(per_dev)) + list(range(room, room + per_dev)) + [2 * room]:
        tile = jnp.where(lane == i, plan_ref[i], tile)
    tile_ref[...] = tile


def make_plan(blocks, sector_row, kept, me, devices, width, chunk):
    scalar_spec = pl.BlockSpec(memory_space=pltpu.SMEM)
    vector_spec = pl.BlockSpec(memory_space=pltpu.VMEM)
    return pl.pallas_call(
        functools.partial(plan_kernel, width, chunk),
        in_specs=[scalar_spec, scalar_spec, scalar_spec, vector_spec],
        out_specs=[vector_spec, scalar_spec, vector_spec],
        out_shape=[
            jax.ShapeDtypeStruct((devices,) + blocks.shape[1:], blocks.dtype),
            jax.ShapeDtypeStruct((32,), jnp.int32),
            jax.ShapeDtypeStruct((8, 128), jnp.int32),
        ],
        name="make_plan",
    )(me.reshape(1), sector_row, kept, blocks)


def exchange_kernel(
    devices,
    segments,
    routed,
    tile,
    isom,
    before,
    most,
    tiles,
    mine,
    ends,
    block_sems,
    tile_sems,
    end_sems,
    own_sem,
):
    me = lax.axis_index("sec")
    seg = lax.axis_index("seg")
    peers = [lax.rem(me + k, devices) for k in range(1, devices)]
    others = [lax.rem(seg + k, segments) for k in range(1, segments)]
    barrier = pltpu.get_barrier_semaphore()
    for peer in peers:
        pl.semaphore_signal(barrier, inc=1, device_id={"sec": peer}, device_id_type=MESH)
    for other in others:
        pl.semaphore_signal(barrier, inc=1, device_id={"seg": other}, device_id_type=MESH)
    pl.semaphore_wait(barrier, len(peers) + len(others))

    own = pltpu.make_async_copy(routed.at[me], isom.at[me], own_sem)
    own.start()

    def along(source, target, sems, axis, index, here, there):
        return pltpu.make_async_remote_copy(
            src_ref=source,
            dst_ref=target.at[here],
            send_sem=sems.at[0, index],
            recv_sem=sems.at[1, index],
            device_id={axis: there},
            device_id_type=MESH,
        )

    tile_copies = [
        along(tile, tiles, tile_sems, "sec", i, me, peer) for i, peer in enumerate(peers)
    ]
    block_copies = [
        along(routed.at[peer], isom, block_sems, "sec", i, me, peer)
        for i, peer in enumerate(peers)
    ]
    for copy in tile_copies + block_copies:
        copy.start()
    tiles[me] = tile[...]
    for copy in tile_copies:
        copy.wait()
    total = tiles[0]
    for i in range(1, devices):
        total = jnp.maximum(total, tiles[i])
    mine[0] = tile[...]
    mine[1] = total
    end_copies = [
        along(mine, ends, end_sems, "seg", i, seg, other) for i, other in enumerate(others)
    ]
    for copy in end_copies:
        copy.start()
    ends[seg] = mine[...]
    for copy in end_copies:
        copy.wait()
    total = ends[0, 1]
    for i in range(1, segments):
        total = jnp.maximum(total, ends[i, 1])
    most[...] = total
    before[...] = jnp.where(seg > 0, ends[jnp.maximum(seg - 1, 0), 0], 0)
    for copy in block_copies:
        copy.wait()
    own.wait()


def exchange(routed, tile, devices, segments):
    vector_spec = pl.BlockSpec(memory_space=pltpu.VMEM)
    small = jax.ShapeDtypeStruct(tile.shape, tile.dtype)
    return pl.pallas_call(
        functools.partial(exchange_kernel, devices, segments),
        in_specs=[vector_spec, vector_spec],
        out_specs=[vector_spec, vector_spec, vector_spec],
        out_shape=[jax.ShapeDtypeStruct(routed.shape, routed.dtype), small, small],
        scratch_shapes=[
            pltpu.VMEM((devices,) + tile.shape, tile.dtype),
            pltpu.VMEM((2,) + tile.shape, tile.dtype),
            pltpu.VMEM((segments, 2) + tile.shape, tile.dtype),
            pltpu.SemaphoreType.DMA((2, devices - 1)),
            pltpu.SemaphoreType.DMA((2, devices - 1)),
            pltpu.SemaphoreType.DMA((2, segments - 1)),
            pltpu.SemaphoreType.DMA,
        ],
        compiler_params=pltpu.CompilerParams(collective_id=0, has_side_effects=True),
        name="exchange",
    )(routed, tile)


def sector_kernel(unit, chunk, late, last, spill, plan, row, op, table, *refs):
    if late:
        lower, refs = refs[0], refs[1:]
    env, iso_all, sing = refs[:3]
    env_right, excess = refs[-14 + last], refs[-12]
    piece = None if last else refs[-13]
    e, iso, placed_t, mixer, left, prod, out, stage, packed, in_sems, out_sems = refs[-11:]
    room = units_of(plan)
    width, blk = e.shape[1], e.shape[-1]
    nops = table.shape[-1]
    slot = plan[unit] - 1
    keep = plan[room + unit]
    begin, _ = begin_of(plan, unit, width, blk, chunk)
    half = width // 2

    iso_copy = pltpu.make_async_copy(iso_all.at[plan[3 * room + slot]], iso, in_sems.at[0])
    iso_copy.start()
    spilled = begin - unit * chunk

    def spill_blocks(source, source_row, target, target_row, first, rows, held, sem, act):
        for i in range(rows // spill):

            @pl.when(i * spill < held)
            def _(i=i):
                act(
                    pltpu.make_async_copy(
                        source.at[pl.ds(source_row + i * spill, spill), :],
                        target.at[pl.ds(target_row + i * spill, spill), :],
                        sem.at[first + i],
                    )
                )

    start_copy = lambda copy: copy.start()
    wait_copy = lambda copy: copy.wait()
    if unit:
        spill_in = (refs[4], 0, packed, 0, 7, unit * spill, spilled, in_sems)
        spill_blocks(*spill_in, start_copy)
    env_copies = []
    for part in range(2):
        for c in range(3):
            rows = pl.ds(part * half, half)
            sem = in_sems.at[1 + 3 * part + c]
            target = e.at[c, rows]
            usual = pltpu.make_async_copy(env.at[0, jnp.maximum(slot - c, 0), rows], target, sem)
            if late and c:
                passed = pltpu.make_async_copy(
                    lower.at[jnp.clip(slot - c + 2, 0, 1), rows], target, sem
                )

                @pl.when(slot >= c)
                def _(usual=usual):
                    usual.start()

                @pl.when(slot < c)
                def _(passed=passed):
                    passed.start()

            else:
                usual.start()
            env_copies.append(usual)

    lane = lax.broadcasted_iota(jnp.int32, (blk, blk), 1)
    high = lax.broadcasted_iota(jnp.int32, (blk, blk), 0)
    inside = lane < keep
    scale = jnp.where(inside[:1], 1.0 / sing[slot], 0.0)
    scale = scale.astype(jnp.bfloat16).astype(jnp.float32)
    scale = jnp.broadcast_to(scale, (blk, blk))
    outer = scale * scale.T

    iso_copy.wait()
    placed = []
    for s in range(4):
        value = jnp.where(inside, iso[s].astype(jnp.float32), 0.0)
        placed.append(value)
        placed_t[s * blk : (s + 1) * blk, :] = value.T.astype(jnp.bfloat16)
    for x in range(nops):
        for p in range(4):
            total = None
            for s in range(4):
                if CHARGES[p] == CHARGES[s]:
                    term = table[p, s, x] * placed[s]
                    total = term if total is None else total + term
            mixer[p * blk : (p + 1) * blk, x * blk : (x + 1) * blk] = total.astype(jnp.bfloat16)

    tall = (keep + 15) // 16 * 16

    def bra_step(w, carry):
        rows = pl.ds(pl.multiple_of(w * tall, 16), blk)
        first = jnp.dot(placed_t[0:blk], e[0, w], preferred_element_type=jnp.float32)
        middle = jnp.dot(placed_t[blk : 3 * blk], e[1, w], preferred_element_type=jnp.float32)
        last = jnp.dot(placed_t[3 * blk :], e[2, w], preferred_element_type=jnp.float32)
        left[rows, 0:blk] = first.astype(jnp.bfloat16)
        left[rows, blk : 2 * blk] = middle[:blk].astype(jnp.bfloat16)
        left[rows, 2 * blk : 3 * blk] = middle[blk:].astype(jnp.bfloat16)
        left[rows, 3 * blk :] = last.astype(jnp.bfloat16)
        return carry

    def ket_step(begin, i, carry):
        rows = pl.ds(pl.multiple_of(begin + i * (32 * half), 16), 32 * half)
        for x in range(0, nops, 2):
            pair = jnp.dot(
                left[rows, :],
                mixer[:, x * blk : (x + 2) * blk],
                preferred_element_type=jnp.float32,
            )
            prod[x, rows, :] = pair[:, :blk]
            prod[x + 1, rows, :] = pair[:, blk:]
        return carry

    for part in range(2):
        for c in range(3):
            env_copies[3 * part + c].wait()
        lax.fori_loop(part * half, (part + 1) * half, bra_step, 0, unroll=half)
        lax.fori_loop(
            0, (tall + 31) // 32, functools.partial(ket_step, part * half * tall), 0
        )

    _, rows8, count = packed_shape(keep, width, blk)
    live = high < keep

    def column_step(v, current):
        total = None
        for t in range(3):
            begin = pl.multiple_of(row[t, v] * tall, 16)
            term = prod[op[t, v], pl.ds(begin, blk), :]
            total = term if total is None else total + term
        value = jnp.where(live, total, 0.0).astype(jnp.bfloat16)
        out[v] = value
        shift = (v * keep) % blk
        turned = pltpu.roll(value.astype(jnp.float32) * outer, shift, 1)
        current = jnp.where(lane < shift, current, turned)
        stage[pl.ds(pl.multiple_of((v * keep) // blk * rows8, 8), blk), :] = current
        return jnp.where(shift + keep >= blk, turned, current)

    current = jnp.zeros((blk, blk), jnp.float32)
    out_copies = []
    for part in range(2):
        current = lax.fori_loop(part * half, (part + 1) * half, column_step, current, unroll=half)
        rows = pl.ds(part * half, half)
        copy = pltpu.make_async_copy(out.at[rows], env_right.at[0, slot, rows], out_sems.at[part])
        copy.start()
        out_copies.append(copy)
    stage[pl.ds(pl.multiple_of((width * keep) // blk * rows8, 8), blk), :] = current

    if unit:
        spill_blocks(*spill_in, wait_copy)

    def cast_step(i, carry):
        source = pl.ds(pl.multiple_of(i * blk, blk), blk)
        target = pl.ds(pl.multiple_of(begin - unit * chunk + i * blk, 16), blk)
        packed[target, :] = stage[source, :].astype(jnp.bfloat16)
        return carry

    lax.fori_loop(0, (count + blk - 1) // blk, cast_step, 0)
    target = excess.at[pl.ds(0, chunk), :] if last else piece
    out_copies.append(
        pltpu.make_async_copy(packed.at[pl.ds(0, chunk), :], target, out_sems.at[2])
    )
    out_copies[-1].start()
    spill_out = (packed, chunk, excess, chunk * last, 3, (unit + 1) * spill, spilled + count - chunk)
    spill_blocks(*spill_out, out_sems, start_copy)
    spill_blocks(*spill_out, out_sems, wait_copy)
    for copy in out_copies:
        copy.wait()


def sector_call(unit, chunk, scalars, env, lower, isom, sing, env_right, excess, arrived):
    width, blk = env.shape[2], env.shape[3]
    nops = scalars[3].shape[-1]
    hbm_spec = pl.BlockSpec(memory_space=pltpu.HBM)
    operands = [env, isom, sing]
    in_specs = [hbm_spec, hbm_spec, pl.BlockSpec(memory_space=pltpu.VMEM)]
    if lower is not None:
        operands.insert(0, lower)
        in_specs.insert(0, pl.BlockSpec(memory_space=pl.ANY))
    aliases = {}
    if unit:
        aliases[len(scalars) + len(operands)] = 0
    extra = [array for array in (env_right, excess, arrived) if array is not None]
    operands += extra
    in_specs += [hbm_spec] * len(extra)
    if arrived is not None:
        in_specs[-1] = pl.BlockSpec(memory_space=pl.ANY)
    rows = width * blk
    spill = rows - chunk
    last = unit == env.shape[1] - 1
    bf16, f32 = jnp.bfloat16, jnp.float32
    return pl.pallas_call(
        functools.partial(sector_kernel, unit, chunk, lower is not None, last, spill),
        in_specs=[pl.BlockSpec(memory_space=pltpu.SMEM)] * len(scalars) + in_specs,
        out_specs=[hbm_spec] * (3 - last),
        out_shape=[jax.ShapeDtypeStruct(env.shape, bf16)]
        + [jax.ShapeDtypeStruct((chunk, blk), bf16)] * (not last)
        + [jax.ShapeDtypeStruct(((unit + 1) * spill + chunk * last, blk), bf16)],
        scratch_shapes=[
            pltpu.VMEM((3, width, blk, blk), bf16),
            pltpu.VMEM((4, blk, blk), bf16),
            pltpu.VMEM((4 * blk, blk), bf16),
            pltpu.VMEM((4 * blk, nops * blk), bf16),
            pltpu.VMEM((rows, 4 * blk), bf16),
            pltpu.VMEM((nops, rows, blk), f32),
            pltpu.VMEM((width, blk, blk), bf16),
            pltpu.VMEM((rows + blk, blk), f32),
            pltpu.VMEM((unit * spill + rows + blk, blk), bf16),
            pltpu.SemaphoreType.DMA((7 + unit,)),
            pltpu.SemaphoreType.DMA((4 + unit,)),
        ],
        input_output_aliases=aliases,
        compiler_params=pltpu.CompilerParams(vmem_limit_bytes=VMEM_LIMIT),
        cost_estimate=pl.CostEstimate(
            flops=COST, bytes_accessed=rows * blk, transcendentals=0
        ),
        name=f"sector_{unit}",
    )(*scalars, *operands)


def unpack_kernel(chunk, before, after, begin, last, plan, *refs):
    pieces = refs[: after - begin + last]
    handoff, held, stage, out, in_sems, out_sems = refs[-6:]
    room = 8
    width, blk = out.shape[1], out.shape[-1]
    units = handoff.shape[1]
    copies = []
    at = 0
    for i, piece in enumerate(pieces):
        copy = pltpu.make_async_copy(
            piece, held.at[pl.ds(at, piece.shape[0]), :], in_sems.at[i]
        )
        copy.start()
        copies.append(copy)
        at += piece.shape[0]
    for copy in copies:
        copy.wait()
    lane = lax.broadcasted_iota(jnp.int32, (blk, blk), 1)
    high = lax.broadcasted_iota(jnp.int32, (blk, blk), 0)

    def store(turn, slot):
        return pltpu.make_async_copy(out.at[turn], handoff.at[0, slot], out_sems.at[turn])

    def unit_step(u, carry):
        end, done = carry
        code = plan[0, u]
        keep = plan[0, room + u]
        slot = jnp.where(code > 0, code - 1, u)
        _, rows8, rows = packed_shape(keep, width, blk)
        start = jnp.maximum(end, u * chunk)
        end = start + rows
        active = jnp.bool_(True)
        if before:
            active = active & (end > before * chunk)
        if not last:
            active = active & (end <= after * chunk)
        turn = done % 2

        @pl.when(active)
        def _():
            @pl.when(done >= 2)
            def _():
                store(turn, slot).wait()

            shift_rows = start - begin * chunk

            def cast_step(i, carry):
                source = pl.ds(pl.multiple_of(shift_rows + i * blk, 16), blk)
                target = pl.ds(pl.multiple_of(i * blk, blk), blk)
                stage[target, :] = held[source, :].astype(jnp.float32)
                return carry

            lax.fori_loop(0, (rows + blk - 1) // blk, cast_step, 0)
            live = (high < keep) & (lane < keep)

            def column_step(v, carry):
                shift = (v * keep) % blk
                base = pl.multiple_of((v * keep) // blk * rows8, 8)
                this = stage[pl.ds(base, blk), :]
                following = stage[pl.ds(pl.multiple_of(base + rows8, 8), blk), :]
                value = jnp.where(lane >= shift, this, following)
                value = pltpu.roll(value, (blk - shift) % blk, 1)
                out[turn, v] = jnp.where(live, value, 0.0).astype(jnp.bfloat16)
                return carry

            lax.fori_loop(0, width, column_step, 0, unroll=2)
            store(turn, slot).start()

        return end, done + active.astype(jnp.int32)

    _, done = lax.fori_loop(0, units, unit_step, (jnp.int32(0), jnp.int32(0)))

    for back in (1, 2):

        @pl.when(done >= back)
        def _(back=back):
            store((done - back) % 2, 0).wait()


def unpack_call(chunk, before, after, plan, pieces, tail, handoff, shape):
    width, blk = shape[2], shape[3]
    rows = width * blk
    begin = max(0, before - -(-rows // chunk)) if before else 0
    hbm_spec = pl.BlockSpec(memory_space=pltpu.HBM)
    any_spec = pl.BlockSpec(memory_space=pl.ANY)
    operands = list(pieces[begin:after]) + ([] if tail is None else [tail])
    count = len(operands)
    held = sum(piece.shape[0] for piece in operands)
    aliases = {}
    if handoff is not None:
        aliases[1 + count] = 0
        operands.append(handoff)
    return pl.pallas_call(
        functools.partial(unpack_kernel, chunk, before, after, begin, tail is not None),
        in_specs=[pl.BlockSpec(memory_space=pltpu.SMEM)]
        + [any_spec] * count
        + [hbm_spec] * (len(operands) - count),
        out_specs=hbm_spec,
        out_shape=jax.ShapeDtypeStruct(shape, jnp.bfloat16),
        scratch_shapes=[
            pltpu.VMEM((held + blk, blk), jnp.bfloat16),
            pltpu.VMEM((rows + 2 * blk, blk), jnp.float32),
            pltpu.VMEM((2, width, blk, blk), jnp.bfloat16),
            pltpu.SemaphoreType.DMA((count,)),
            pltpu.SemaphoreType.DMA((2,)),
        ],
        input_output_aliases=aliases,
        compiler_params=pltpu.CompilerParams(vmem_limit_bytes=VMEM_LIMIT),
        name=f"unpack_{after}",
    )(plan, *operands)


def send_tail(rows, chunk, shape, plan, excess, *pieces):
    got = passed_along(excess[:rows], "seg", 1)
    handoff = unpack_call(chunk, 0, len(pieces), plan, pieces, None, None, shape)
    return lax.dynamic_update_slice(excess, got, (0, 0)), handoff


def body(env_left, isometry, sing_vals, kept, twosite_sector, mpo_row, mpo_op, op_table):
    my_index = lax.axis_index("sec")
    devices, segments = lax.axis_size("sec"), lax.axis_size("seg")
    units, width, blk = env_left.shape[1:4]
    rows = width * blk
    chunk = int(rows * BASE) // 16 * 16
    routed, plan, tile = make_plan(
        isometry[0, 0], twosite_sector[0, 0], kept[SITES - 1, 0], my_index, devices, width, chunk
    )
    isom, plan_before, most = exchange(routed, tile, devices, segments)
    scalars = (plan, mpo_row.T, mpo_op.T, jnp.transpose(op_table, (1, 2, 0)))
    sing = jnp.transpose(sing_vals, (1, 0, 2))
    env_right = excess = lower = None
    pieces = []
    for unit in range(units):
        env_right, *sent, excess = sector_call(
            unit,
            chunk,
            scalars,
            env_left,
            lower if unit >= EARLY else None,
            isom,
            sing,
            env_right,
            excess,
            pieces[unit - 2] if unit > 1 else None,
        )
        if unit == 1:
            late_env, _ = lax.optimization_barrier((env_left, sent))
            lower = passed_along(late_env[0, units - 2 :], "sec", 1)
        pieces += [passed_along(piece, "seg", 1) for piece in sent]
    limits = []
    for share in TOTALS:
        limit = (int(units * share * rows) // 16 + 1) * 16 - (units - 1) * chunk
        limits.append(min(limit, excess.shape[0]))
    room = plan.shape[0] // 4
    need = most[0, 2 * room]
    level = sum((need > limit).astype(jnp.int32) for limit in limits[:-1])
    branches = [
        functools.partial(send_tail, limit, chunk, env_left.shape) for limit in limits
    ]
    early = units - 2
    tail, handoff = lax.switch(level, branches, plan_before, excess, *pieces[:early])
    handoff = unpack_call(
        chunk, early, units - 1, plan_before, pieces, tail, handoff, env_left.shape
    )
    return env_right, handoff


def solution(mesh):
    in_specs = (
        P("seg", "sec", None, None, None),
        P(None, "seg", "sec", None, None, None),
        P("seg", "sec", None),
        P(None, "seg", "sec"),
        P(None, "seg", None),
        P(),
        P(),
        P(),
    )
    out_specs = (P("seg", "sec", None, None, None), P("seg", "sec", None, None, None))
    return jax.shard_map(body, mesh=mesh, in_specs=in_specs, out_specs=out_specs, check_vma=False)
```

```python
import functools

import jax
import jax.numpy as jnp
from jax import lax
from jax.experimental import pallas as pl
from jax.experimental.pallas import tpu as pltpu
from jax.sharding import PartitionSpec as P

SITES = 1
CHARGES = (0, 1, 1, 2)
VMEM_LIMIT = 56 * 1024 * 1024
BASE = 0.6
TOTALS = tuple(x / 1000 for x in (575, 600, 615, 630, 645, 660, 675, 690, 705, 720, 740, 760, 785, 815, 855, 910, 1000))
COST = 142606336
MESH = pl.DeviceIdType.MESH
EARLY = 4


def passed_along(block, axis, distance):
    devices = range(lax.axis_size(axis))
    route = [(i - distance, i) for i in devices if i - distance in devices]
    return lax.ppermute(block, axis, route)


def packed_shape(keep, width, blk):
    blocks = (width * keep + blk - 1) // blk
    rows = (keep + 7) // 8 * 8
    return blocks, rows, (blocks * rows + 15) // 16 * 16


def begin_of(plan, unit, width, blk, chunk):
    end = jnp.int32(0)
    begin = jnp.int32(0)
    for u in range(unit + 1):
        begin = jnp.maximum(end, u * chunk)
        end = begin + packed_shape(plan[units_of(plan) + u], width, blk)[2]
    return begin, end


def units_of(plan):
    return plan.shape[0] // 4


def plan_kernel(width, chunk, me_ref, sector_ref, kept_ref, src_ref, dst_ref, plan_ref, tile_ref):
    per_dev = src_ref.shape[0]
    blk = src_ref.shape[-1]
    room = units_of(plan_ref)
    first = me_ref[0] * per_dev
    for i in range(per_dev):
        owner = sector_ref[first + i] // per_dev
        dst_ref[owner] = src_ref[i]
    kept = [kept_ref[i] for i in range(per_dev)]

    def before(i, j):
        return kept[i] > kept[j] if i > j else kept[i] >= kept[j]

    def rank(j, members):
        total = jnp.int32(0)
        for i, inside in members:
            if i != j:
                total = total + (before(i, j) & inside).astype(jnp.int32)
        return total

    top = [(i, True) for i in range(2, per_dev)]
    high = {j: rank(j, top) for j in range(2, per_dev)}
    rest = [(0, True), (1, True)] + [(i, high[i] >= EARLY) for i in range(2, per_dev)]
    place = []
    for j in range(per_dev):
        late = EARLY + rank(j, rest)
        place.append(late if j < 2 else jnp.where(high[j] < EARLY, high[j], late))
    for i in range(4 * room):
        plan_ref[i] = 0
    for j in range(per_dev):
        plan_ref[place[j]] = j + 1
        plan_ref[room + place[j]] = kept[j]

    def find(n, carry):
        slot = sector_ref[n] - first
        inside = (slot >= 0) & (slot < per_dev)

        @pl.when(inside)
        def _():
            plan_ref[3 * room + slot] = n // per_dev

        return carry

    lax.fori_loop(0, sector_ref.shape[0], find, 0)
    _, end = begin_of(plan_ref, per_dev - 1, width, blk, chunk)
    plan_ref[2 * room] = end - (per_dev - 1) * chunk
    lane = lax.broadcasted_iota(jnp.int32, tile_ref.shape, 1)
    tile = jnp.zeros(tile_ref.shape, jnp.int32)
    for i in list(range(per_dev)) + list(range(room, room + per_dev)) + [2 * room]:
        tile = jnp.where(lane == i, plan_ref[i], tile)
    tile_ref[...] = tile


def make_plan(blocks, sector_row, kept, me, devices, width, chunk):
    scalar_spec = pl.BlockSpec(memory_space=pltpu.SMEM)
    vector_spec = pl.BlockSpec(memory_space=pltpu.VMEM)
    return pl.pallas_call(
        functools.partial(plan_kernel, width, chunk),
        in_specs=[scalar_spec, scalar_spec, scalar_spec, vector_spec],
        out_specs=[vector_spec, scalar_spec, vector_spec],
        out_shape=[
            jax.ShapeDtypeStruct((devices,) + blocks.shape[1:], blocks.dtype),
            jax.ShapeDtypeStruct((32,), jnp.int32),
            jax.ShapeDtypeStruct((8, 128), jnp.int32),
        ],
        name="make_plan",
    )(me.reshape(1), sector_row, kept, blocks)


def exchange_kernel(
    devices,
    segments,
    routed,
    tile,
    env,
    isom,
    before,
    most,
    late,
    tiles,
    mine,
    ends,
    block_sems,
    tile_sems,
    end_sems,
    own_sem,
    late_sem,
):
    me = lax.axis_index("sec")
    seg = lax.axis_index("seg")
    peers = [lax.rem(me + k, devices) for k in range(1, devices)]
    others = [lax.rem(seg + k, segments) for k in range(1, segments)]
    barrier = pltpu.get_barrier_semaphore()
    for peer in peers:
        pl.semaphore_signal(barrier, inc=1, device_id={"sec": peer}, device_id_type=MESH)
    for other in others:
        pl.semaphore_signal(barrier, inc=1, device_id={"seg": other}, device_id_type=MESH)
    pl.semaphore_wait(barrier, len(peers) + len(others))

    own = pltpu.make_async_copy(routed.at[me], isom.at[me], own_sem)
    own.start()
    count = late.shape[0]
    aside = pltpu.make_async_copy(
        env.at[0, pl.ds(env.shape[1] - count, count)], late, late_sem
    )
    aside.start()

    def along(source, target, sems, axis, index, here, there):
        return pltpu.make_async_remote_copy(
            src_ref=source,
            dst_ref=target.at[here],
            send_sem=sems.at[0, index],
            recv_sem=sems.at[1, index],
            device_id={axis: there},
            device_id_type=MESH,
        )

    tile_copies = [
        along(tile, tiles, tile_sems, "sec", i, me, peer) for i, peer in enumerate(peers)
    ]
    block_copies = [
        along(routed.at[peer], isom, block_sems, "sec", i, me, peer)
        for i, peer in enumerate(peers)
    ]
    for copy in tile_copies + block_copies:
        copy.start()
    tiles[me] = tile[...]
    for copy in tile_copies:
        copy.wait()
    total = tiles[0]
    for i in range(1, devices):
        total = jnp.maximum(total, tiles[i])
    mine[0] = tile[...]
    mine[1] = total
    end_copies = [
        along(mine, ends, end_sems, "seg", i, seg, other) for i, other in enumerate(others)
    ]
    for copy in end_copies:
        copy.start()
    ends[seg] = mine[...]
    for copy in end_copies:
        copy.wait()
    total = ends[0, 1]
    for i in range(1, segments):
        total = jnp.maximum(total, ends[i, 1])
    most[...] = total
    before[...] = jnp.where(seg > 0, ends[jnp.maximum(seg - 1, 0), 0], 0)
    for copy in block_copies:
        copy.wait()
    own.wait()
    aside.wait()


def exchange(routed, tile, env, devices, segments):
    vector_spec = pl.BlockSpec(memory_space=pltpu.VMEM)
    small = jax.ShapeDtypeStruct(tile.shape, tile.dtype)
    return pl.pallas_call(
        functools.partial(exchange_kernel, devices, segments),
        in_specs=[vector_spec, vector_spec, pl.BlockSpec(memory_space=pltpu.HBM)],
        out_specs=[vector_spec] * 4,
        out_shape=[
            jax.ShapeDtypeStruct(routed.shape, routed.dtype),
            small,
            small,
            jax.ShapeDtypeStruct((CHARGES[-1],) + env.shape[2:], env.dtype),
        ],
        scratch_shapes=[
            pltpu.VMEM((devices,) + tile.shape, tile.dtype),
            pltpu.VMEM((2,) + tile.shape, tile.dtype),
            pltpu.VMEM((segments, 2) + tile.shape, tile.dtype),
            pltpu.SemaphoreType.DMA((2, devices - 1)),
            pltpu.SemaphoreType.DMA((2, devices - 1)),
            pltpu.SemaphoreType.DMA((2, segments - 1)),
            pltpu.SemaphoreType.DMA,
            pltpu.SemaphoreType.DMA,
        ],
        compiler_params=pltpu.CompilerParams(
            collective_id=0, has_side_effects=True, vmem_limit_bytes=VMEM_LIMIT
        ),
        name="exchange",
    )(routed, tile, env)


def sector_kernel(unit, chunk, late, last, spill, plan, row, op, table, *refs):
    if late:
        lower, refs = refs[0], refs[1:]
    env, iso_all, sing = refs[:3]
    env_right, excess = refs[-14 + last], refs[-12]
    piece = None if last else refs[-13]
    e, iso, placed_t, mixer, left, prod, out, stage, packed, in_sems, out_sems = refs[-11:]
    room = units_of(plan)
    width, blk = e.shape[1], e.shape[-1]
    nops = table.shape[-1]
    slot = plan[unit] - 1
    keep = plan[room + unit]
    begin, _ = begin_of(plan, unit, width, blk, chunk)
    half = width // 2

    iso_copy = pltpu.make_async_copy(iso_all.at[plan[3 * room + slot]], iso, in_sems.at[0])
    iso_copy.start()
    spilled = begin - unit * chunk

    def spill_blocks(source, source_row, target, target_row, first, rows, held, sem, act):
        for i in range(rows // spill):

            @pl.when(i * spill < held)
            def _(i=i):
                act(
                    pltpu.make_async_copy(
                        source.at[pl.ds(source_row + i * spill, spill), :],
                        target.at[pl.ds(target_row + i * spill, spill), :],
                        sem.at[first + i],
                    )
                )

    start_copy = lambda copy: copy.start()
    wait_copy = lambda copy: copy.wait()
    if unit:
        spill_in = (refs[4], 0, packed, 0, 7, unit * spill, spilled, in_sems)
        spill_blocks(*spill_in, start_copy)
    env_copies = []
    for part in range(2):
        for c in range(3):
            rows = pl.ds(part * half, half)
            sem = in_sems.at[1 + 3 * part + c]
            target = e.at[c, rows]
            usual = pltpu.make_async_copy(env.at[0, jnp.maximum(slot - c, 0), rows], target, sem)
            if late and c:
                passed = pltpu.make_async_copy(
                    lower.at[jnp.clip(slot - c + 2, 0, 1), rows], target, sem
                )

                @pl.when(slot >= c)
                def _(usual=usual):
                    usual.start()

                @pl.when(slot < c)
                def _(passed=passed):
                    passed.start()

            else:
                usual.start()
            env_copies.append(usual)

    lane = lax.broadcasted_iota(jnp.int32, (blk, blk), 1)
    high = lax.broadcasted_iota(jnp.int32, (blk, blk), 0)
    inside = lane < keep
    scale = jnp.where(inside[:1], 1.0 / sing[slot], 0.0)
    scale = scale.astype(jnp.bfloat16).astype(jnp.float32)
    scale = jnp.broadcast_to(scale, (blk, blk))
    outer = scale * scale.T

    iso_copy.wait()
    placed = []
    for s in range(4):
        value = jnp.where(inside, iso[s].astype(jnp.float32), 0.0)
        placed.append(value)
        placed_t[s * blk : (s + 1) * blk, :] = value.T.astype(jnp.bfloat16)
    for x in range(nops):
        for p in range(4):
            total = None
            for s in range(4):
                if CHARGES[p] == CHARGES[s]:
                    term = table[p, s, x] * placed[s]
                    total = term if total is None else total + term
            mixer[p * blk : (p + 1) * blk, x * blk : (x + 1) * blk] = total.astype(jnp.bfloat16)

    tall = (keep + 15) // 16 * 16

    def bra_step(w, carry):
        rows = pl.ds(pl.multiple_of(w * tall, 16), blk)
        first = jnp.dot(placed_t[0:blk], e[0, w], preferred_element_type=jnp.float32)
        middle = jnp.dot(placed_t[blk : 3 * blk], e[1, w], preferred_element_type=jnp.float32)
        last = jnp.dot(placed_t[3 * blk :], e[2, w], preferred_element_type=jnp.float32)
        left[rows, 0:blk] = first.astype(jnp.bfloat16)
        left[rows, blk : 2 * blk] = middle[:blk].astype(jnp.bfloat16)
        left[rows, 2 * blk : 3 * blk] = middle[blk:].astype(jnp.bfloat16)
        left[rows, 3 * blk :] = last.astype(jnp.bfloat16)
        return carry

    def ket_step(begin, i, carry):
        rows = pl.ds(pl.multiple_of(begin + i * (32 * half), 16), 32 * half)
        for x in range(0, nops, 2):
            pair = jnp.dot(
                left[rows, :],
                mixer[:, x * blk : (x + 2) * blk],
                preferred_element_type=jnp.float32,
            )
            prod[x, rows, :] = pair[:, :blk]
            prod[x + 1, rows, :] = pair[:, blk:]
        return carry

    for part in range(2):
        for c in range(3):
            env_copies[3 * part + c].wait()
        lax.fori_loop(part * half, (part + 1) * half, bra_step, 0, unroll=half)
        lax.fori_loop(
            0, (tall + 31) // 32, functools.partial(ket_step, part * half * tall), 0
        )

    _, rows8, count = packed_shape(keep, width, blk)
    live = high < keep

    def column_step(v, current):
        total = None
        for t in range(3):
            begin = pl.multiple_of(row[t, v] * tall, 16)
            term = prod[op[t, v], pl.ds(begin, blk), :]
            total = term if total is None else total + term
        value = jnp.where(live, total, 0.0).astype(jnp.bfloat16)
        out[v] = value
        shift = (v * keep) % blk
        turned = pltpu.roll(value.astype(jnp.float32) * outer, shift, 1)
        current = jnp.where(lane < shift, current, turned)
        stage[pl.ds(pl.multiple_of((v * keep) // blk * rows8, 8), blk), :] = current
        return jnp.where(shift + keep >= blk, turned, current)

    current = jnp.zeros((blk, blk), jnp.float32)
    out_copies = []
    for part in range(2):
        current = lax.fori_loop(part * half, (part + 1) * half, column_step, current, unroll=half)
        rows = pl.ds(part * half, half)
        copy = pltpu.make_async_copy(out.at[rows], env_right.at[0, slot, rows], out_sems.at[part])
        copy.start()
        out_copies.append(copy)
    stage[pl.ds(pl.multiple_of((width * keep) // blk * rows8, 8), blk), :] = current

    if unit:
        spill_blocks(*spill_in, wait_copy)

    def cast_step(i, carry):
        source = pl.ds(pl.multiple_of(i * blk, blk), blk)
        target = pl.ds(pl.multiple_of(begin - unit * chunk + i * blk, 16), blk)
        packed[target, :] = stage[source, :].astype(jnp.bfloat16)
        return carry

    lax.fori_loop(0, (count + blk - 1) // blk, cast_step, 0)
    target = excess.at[pl.ds(0, chunk), :] if last else piece
    out_copies.append(
        pltpu.make_async_copy(packed.at[pl.ds(0, chunk), :], target, out_sems.at[2])
    )
    out_copies[-1].start()
    spill_out = (packed, chunk, excess, chunk * last, 3, (unit + 1) * spill, spilled + count - chunk)
    spill_blocks(*spill_out, out_sems, start_copy)
    spill_blocks(*spill_out, out_sems, wait_copy)
    for copy in out_copies:
        copy.wait()


def sector_call(unit, chunk, scalars, env, lower, isom, sing, env_right, excess, arrived):
    width, blk = env.shape[2], env.shape[3]
    nops = scalars[3].shape[-1]
    hbm_spec = pl.BlockSpec(memory_space=pltpu.HBM)
    operands = [env, isom, sing]
    in_specs = [hbm_spec, hbm_spec, pl.BlockSpec(memory_space=pltpu.VMEM)]
    if lower is not None:
        operands.insert(0, lower)
        in_specs.insert(0, pl.BlockSpec(memory_space=pl.ANY))
    aliases = {}
    if unit:
        aliases[len(scalars) + len(operands)] = 0
    extra = [array for array in (env_right, excess, arrived) if array is not None]
    operands += extra
    in_specs += [hbm_spec] * len(extra)
    if arrived is not None:
        in_specs[-1] = pl.BlockSpec(memory_space=pl.ANY)
    rows = width * blk
    spill = rows - chunk
    last = unit == env.shape[1] - 1
    bf16, f32 = jnp.bfloat16, jnp.float32
    return pl.pallas_call(
        functools.partial(sector_kernel, unit, chunk, lower is not None, last, spill),
        in_specs=[pl.BlockSpec(memory_space=pltpu.SMEM)] * len(scalars) + in_specs,
        out_specs=[hbm_spec] * (3 - last),
        out_shape=[jax.ShapeDtypeStruct(env.shape, bf16)]
        + [jax.ShapeDtypeStruct((chunk, blk), bf16)] * (not last)
        + [jax.ShapeDtypeStruct(((unit + 1) * spill + chunk * last, blk), bf16)],
        scratch_shapes=[
            pltpu.VMEM((3, width, blk, blk), bf16),
            pltpu.VMEM((4, blk, blk), bf16),
            pltpu.VMEM((4 * blk, blk), bf16),
            pltpu.VMEM((4 * blk, nops * blk), bf16),
            pltpu.VMEM((rows, 4 * blk), bf16),
            pltpu.VMEM((nops, rows, blk), f32),
            pltpu.VMEM((width, blk, blk), bf16),
            pltpu.VMEM((rows + blk, blk), f32),
            pltpu.VMEM((unit * spill + rows + blk, blk), bf16),
            pltpu.SemaphoreType.DMA((7 + unit,)),
            pltpu.SemaphoreType.DMA((4 + unit,)),
        ],
        input_output_aliases=aliases,
        compiler_params=pltpu.CompilerParams(vmem_limit_bytes=VMEM_LIMIT),
        cost_estimate=pl.CostEstimate(
            flops=COST, bytes_accessed=rows * blk, transcendentals=0
        ),
        name=f"sector_{unit}",
    )(*scalars, *operands)


def unpack_kernel(chunk, before, after, begin, last, plan, *refs):
    pieces = refs[: after - begin + last]
    handoff, held, stage, out, in_sems, out_sems = refs[-6:]
    room = 8
    width, blk = out.shape[1], out.shape[-1]
    units = handoff.shape[1]
    copies = []
    at = 0
    for i, piece in enumerate(pieces):
        copy = pltpu.make_async_copy(
            piece, held.at[pl.ds(at, piece.shape[0]), :], in_sems.at[i]
        )
        copy.start()
        copies.append(copy)
        at += piece.shape[0]
    for copy in copies:
        copy.wait()
    lane = lax.broadcasted_iota(jnp.int32, (blk, blk), 1)
    high = lax.broadcasted_iota(jnp.int32, (blk, blk), 0)

    def store(turn, slot):
        return pltpu.make_async_copy(out.at[turn], handoff.at[0, slot], out_sems.at[turn])

    def unit_step(u, carry):
        end, done = carry
        code = plan[0, u]
        keep = plan[0, room + u]
        slot = jnp.where(code > 0, code - 1, u)
        _, rows8, rows = packed_shape(keep, width, blk)
        start = jnp.maximum(end, u * chunk)
        end = start + rows
        active = jnp.bool_(True)
        if before:
            active = active & (end > before * chunk)
        if not last:
            active = active & (end <= after * chunk)
        turn = done % 2

        @pl.when(active)
        def _():
            @pl.when(done >= 2)
            def _():
                store(turn, slot).wait()

            shift_rows = start - begin * chunk

            def cast_step(i, carry):
                source = pl.ds(pl.multiple_of(shift_rows + i * blk, 16), blk)
                target = pl.ds(pl.multiple_of(i * blk, blk), blk)
                stage[target, :] = held[source, :].astype(jnp.float32)
                return carry

            lax.fori_loop(0, (rows + blk - 1) // blk, cast_step, 0)
            live = (high < keep) & (lane < keep)

            def column_step(v, carry):
                shift = (v * keep) % blk
                base = pl.multiple_of((v * keep) // blk * rows8, 8)
                this = stage[pl.ds(base, blk), :]
                following = stage[pl.ds(pl.multiple_of(base + rows8, 8), blk), :]
                value = jnp.where(lane >= shift, this, following)
                value = pltpu.roll(value, (blk - shift) % blk, 1)
                out[turn, v] = jnp.where(live, value, 0.0).astype(jnp.bfloat16)
                return carry

            lax.fori_loop(0, width, column_step, 0, unroll=width // 2)
            store(turn, slot).start()

        return end, done + active.astype(jnp.int32)

    _, done = lax.fori_loop(0, units, unit_step, (jnp.int32(0), jnp.int32(0)))

    for back in (1, 2):

        @pl.when(done >= back)
        def _(back=back):
            store((done - back) % 2, 0).wait()


def unpack_call(chunk, before, after, plan, pieces, tail, handoff, shape):
    width, blk = shape[2], shape[3]
    rows = width * blk
    begin = max(0, before - -(-rows // chunk)) if before else 0
    hbm_spec = pl.BlockSpec(memory_space=pltpu.HBM)
    any_spec = pl.BlockSpec(memory_space=pl.ANY)
    operands = list(pieces[begin:after]) + ([] if tail is None else [tail])
    count = len(operands)
    held = sum(piece.shape[0] for piece in operands)
    aliases = {}
    if handoff is not None:
        aliases[1 + count] = 0
        operands.append(handoff)
    return pl.pallas_call(
        functools.partial(unpack_kernel, chunk, before, after, begin, tail is not None),
        in_specs=[pl.BlockSpec(memory_space=pltpu.SMEM)]
        + [any_spec] * count
        + [hbm_spec] * (len(operands) - count),
        out_specs=hbm_spec,
        out_shape=jax.ShapeDtypeStruct(shape, jnp.bfloat16),
        scratch_shapes=[
            pltpu.VMEM((held + blk, blk), jnp.bfloat16),
            pltpu.VMEM((rows + 2 * blk, blk), jnp.float32),
            pltpu.VMEM((2, width, blk, blk), jnp.bfloat16),
            pltpu.SemaphoreType.DMA((count,)),
            pltpu.SemaphoreType.DMA((2,)),
        ],
        input_output_aliases=aliases,
        compiler_params=pltpu.CompilerParams(vmem_limit_bytes=VMEM_LIMIT),
        name=f"unpack_{after}",
    )(plan, *operands)


def send_tail(rows, chunk, shape, plan, excess, *pieces):
    got = passed_along(excess[:rows], "seg", 1)
    handoff = unpack_call(chunk, 0, len(pieces), plan, pieces, None, None, shape)
    return lax.dynamic_update_slice(excess, got, (0, 0)), handoff


def body(env_left, isometry, sing_vals, kept, twosite_sector, mpo_row, mpo_op, op_table):
    my_index = lax.axis_index("sec")
    devices, segments = lax.axis_size("sec"), lax.axis_size("seg")
    units, width, blk = env_left.shape[1:4]
    rows = width * blk
    chunk = int(rows * BASE) // 16 * 16
    routed, plan, tile = make_plan(
        isometry[0, 0], twosite_sector[0, 0], kept[SITES - 1, 0], my_index, devices, width, chunk
    )
    isom, plan_before, most, late_env = exchange(routed, tile, env_left, devices, segments)
    scalars = (plan, mpo_row.T, mpo_op.T, jnp.transpose(op_table, (1, 2, 0)))
    sing = jnp.transpose(sing_vals, (1, 0, 2))
    lower = passed_along(late_env, "sec", 1)
    env_right = excess = None
    pieces = []
    for unit in range(units):
        env_right, *sent, excess = sector_call(
            unit,
            chunk,
            scalars,
            env_left,
            lower if unit >= EARLY else None,
            isom,
            sing,
            env_right,
            excess,
            pieces[unit - 2] if unit > 1 else None,
        )
        pieces += [passed_along(piece, "seg", 1) for piece in sent]
    limits = []
    for share in TOTALS:
        limit = (int(units * share * rows) // 16 + 1) * 16 - (units - 1) * chunk
        limits.append(min(limit, excess.shape[0]))
    room = plan.shape[0] // 4
    need = most[0, 2 * room]
    level = sum((need > limit).astype(jnp.int32) for limit in limits[:-1])
    branches = [
        functools.partial(send_tail, limit, chunk, env_left.shape) for limit in limits
    ]
    early = units - 2
    tail, handoff = lax.switch(level, branches, plan_before, excess, *pieces[:early])
    handoff = unpack_call(
        chunk, early, units - 1, plan_before, pieces, tail, handoff, env_left.shape
    )
    return env_right, handoff


def solution(mesh):
    in_specs = (
        P("seg", "sec", None, None, None),
        P(None, "seg", "sec", None, None, None),
        P("seg", "sec", None),
        P(None, "seg", "sec"),
        P(None, "seg", None),
        P(),
        P(),
        P(),
    )
    out_specs = (P("seg", "sec", None, None, None), P("seg", "sec", None, None, None))
    return jax.shard_map(body, mesh=mesh, in_specs=in_specs, out_specs=out_specs, check_vma=False)
```

```python
import functools

import jax
import jax.numpy as jnp
from jax import lax
from jax.experimental import pallas as pl
from jax.experimental.pallas import tpu as pltpu
from jax.sharding import PartitionSpec as P

SITES = 1
CHARGES = (0, 1, 1, 2)
VMEM_LIMIT = 56 * 1024 * 1024
BASE = 0.6
TOTALS = tuple(x / 1000 for x in (575, 600, 615, 630, 645, 660, 675, 690, 705, 720, 740, 760, 785, 815, 855, 910, 1000))
COST = 142606336
MESH = pl.DeviceIdType.MESH
EARLY = 4


def passed_along(block, axis, distance):
    devices = range(lax.axis_size(axis))
    route = [(i - distance, i) for i in devices if i - distance in devices]
    return lax.ppermute(block, axis, route)


def packed_shape(keep, width, blk):
    blocks = (width * keep + blk - 1) // blk
    rows = (keep + 7) // 8 * 8
    return blocks, rows, (blocks * rows + 15) // 16 * 16


def begin_of(plan, unit, width, blk, chunk):
    end = jnp.int32(0)
    begin = jnp.int32(0)
    for u in range(unit + 1):
        begin = jnp.maximum(end, u * chunk)
        end = begin + packed_shape(plan[units_of(plan) + u], width, blk)[2]
    return begin, end


def units_of(plan):
    return plan.shape[0] // 4


def plan_kernel(width, chunk, me_ref, sector_ref, kept_ref, src_ref, dst_ref, plan_ref, tile_ref):
    per_dev = src_ref.shape[0]
    blk = src_ref.shape[-1]
    room = units_of(plan_ref)
    first = me_ref[0] * per_dev
    for i in range(per_dev):
        owner = sector_ref[first + i] // per_dev
        dst_ref[owner] = src_ref[i]
    kept = [kept_ref[i] for i in range(per_dev)]

    def before(i, j):
        return kept[i] > kept[j] if i > j else kept[i] >= kept[j]

    def rank(j, members):
        total = jnp.int32(0)
        for i, inside in members:
            if i != j:
                total = total + (before(i, j) & inside).astype(jnp.int32)
        return total

    top = [(i, True) for i in range(2, per_dev)]
    high = {j: rank(j, top) for j in range(2, per_dev)}
    rest = [(0, True), (1, True)] + [(i, high[i] >= EARLY) for i in range(2, per_dev)]
    place = []
    for j in range(per_dev):
        late = EARLY + rank(j, rest)
        place.append(late if j < 2 else jnp.where(high[j] < EARLY, high[j], late))
    for i in range(4 * room):
        plan_ref[i] = 0
    for j in range(per_dev):
        plan_ref[place[j]] = j + 1
        plan_ref[room + place[j]] = kept[j]

    def find(n, carry):
        slot = sector_ref[n] - first
        inside = (slot >= 0) & (slot < per_dev)

        @pl.when(inside)
        def _():
            plan_ref[3 * room + slot] = n // per_dev

        return carry

    lax.fori_loop(0, sector_ref.shape[0], find, 0)
    _, end = begin_of(plan_ref, per_dev - 1, width, blk, chunk)
    plan_ref[2 * room] = end - (per_dev - 1) * chunk
    lane = lax.broadcasted_iota(jnp.int32, tile_ref.shape, 1)
    tile = jnp.zeros(tile_ref.shape, jnp.int32)
    for i in list(range(per_dev)) + list(range(room, room + per_dev)) + [2 * room]:
        tile = jnp.where(lane == i, plan_ref[i], tile)
    tile_ref[...] = tile


def make_plan(blocks, sector_row, kept, me, devices, width, chunk):
    scalar_spec = pl.BlockSpec(memory_space=pltpu.SMEM)
    vector_spec = pl.BlockSpec(memory_space=pltpu.VMEM)
    return pl.pallas_call(
        functools.partial(plan_kernel, width, chunk),
        in_specs=[scalar_spec, scalar_spec, scalar_spec, vector_spec],
        out_specs=[vector_spec, scalar_spec, vector_spec],
        out_shape=[
            jax.ShapeDtypeStruct((devices,) + blocks.shape[1:], blocks.dtype),
            jax.ShapeDtypeStruct((32,), jnp.int32),
            jax.ShapeDtypeStruct((8, 128), jnp.int32),
        ],
        name="make_plan",
    )(me.reshape(1), sector_row, kept, blocks)


def exchange_kernel(
    devices,
    segments,
    routed,
    tile,
    env,
    isom,
    before,
    most,
    late,
    tiles,
    mine,
    ends,
    block_sems,
    tile_sems,
    end_sems,
    own_sem,
    late_sem,
):
    me = lax.axis_index("sec")
    seg = lax.axis_index("seg")
    peers = [lax.rem(me + k, devices) for k in range(1, devices)]
    others = [lax.rem(seg + k, segments) for k in range(1, segments)]
    barrier = pltpu.get_barrier_semaphore()
    for peer in peers:
        pl.semaphore_signal(barrier, inc=1, device_id={"sec": peer}, device_id_type=MESH)
    for other in others:
        pl.semaphore_signal(barrier, inc=1, device_id={"seg": other}, device_id_type=MESH)
    pl.semaphore_wait(barrier, len(peers) + len(others))

    own = pltpu.make_async_copy(routed.at[me], isom.at[me], own_sem)
    own.start()
    count = late.shape[0]
    aside = pltpu.make_async_copy(
        env.at[0, pl.ds(env.shape[1] - count, count)], late, late_sem
    )
    aside.start()

    def along(source, target, sems, axis, index, here, there):
        return pltpu.make_async_remote_copy(
            src_ref=source,
            dst_ref=target.at[here],
            send_sem=sems.at[0, index],
            recv_sem=sems.at[1, index],
            device_id={axis: there},
            device_id_type=MESH,
        )

    tile_copies = [
        along(tile, tiles, tile_sems, "sec", i, me, peer) for i, peer in enumerate(peers)
    ]
    block_copies = [
        along(routed.at[peer], isom, block_sems, "sec", i, me, peer)
        for i, peer in enumerate(peers)
    ]
    for copy in tile_copies + block_copies:
        copy.start()
    tiles[me] = tile[...]
    for copy in tile_copies:
        copy.wait()
    total = tiles[0]
    for i in range(1, devices):
        total = jnp.maximum(total, tiles[i])
    mine[0] = tile[...]
    mine[1] = total
    end_copies = [
        along(mine, ends, end_sems, "seg", i, seg, other) for i, other in enumerate(others)
    ]
    for copy in end_copies:
        copy.start()
    ends[seg] = mine[...]
    for copy in end_copies:
        copy.wait()
    total = ends[0, 1]
    for i in range(1, segments):
        total = jnp.maximum(total, ends[i, 1])
    most[...] = total
    before[...] = jnp.where(seg > 0, ends[jnp.maximum(seg - 1, 0), 0], 0)
    for copy in block_copies:
        copy.wait()
    own.wait()
    aside.wait()


def exchange(routed, tile, env, devices, segments):
    vector_spec = pl.BlockSpec(memory_space=pltpu.VMEM)
    small = jax.ShapeDtypeStruct(tile.shape, tile.dtype)
    return pl.pallas_call(
        functools.partial(exchange_kernel, devices, segments),
        in_specs=[vector_spec, vector_spec, pl.BlockSpec(memory_space=pltpu.HBM)],
        out_specs=[vector_spec] * 4,
        out_shape=[
            jax.ShapeDtypeStruct(routed.shape, routed.dtype),
            small,
            small,
            jax.ShapeDtypeStruct((CHARGES[-1],) + env.shape[2:], env.dtype),
        ],
        scratch_shapes=[
            pltpu.VMEM((devices,) + tile.shape, tile.dtype),
            pltpu.VMEM((2,) + tile.shape, tile.dtype),
            pltpu.VMEM((segments, 2) + tile.shape, tile.dtype),
            pltpu.SemaphoreType.DMA((2, devices - 1)),
            pltpu.SemaphoreType.DMA((2, devices - 1)),
            pltpu.SemaphoreType.DMA((2, segments - 1)),
            pltpu.SemaphoreType.DMA,
            pltpu.SemaphoreType.DMA,
        ],
        compiler_params=pltpu.CompilerParams(
            collective_id=0, has_side_effects=True, vmem_limit_bytes=VMEM_LIMIT
        ),
        name="exchange",
    )(routed, tile, env)


def sector_kernel(unit, chunk, late, last, spill, plan, row, op, table, *refs):
    if late:
        lower, refs = refs[0], refs[1:]
    env, iso_all, sing = refs[:3]
    env_right, excess = refs[-14 + last], refs[-12]
    piece = None if last else refs[-13]
    e, iso, placed_t, mixer, left, prod, out, stage, packed, in_sems, out_sems = refs[-11:]
    room = units_of(plan)
    width, blk = e.shape[1], e.shape[-1]
    nops = table.shape[-1]
    slot = plan[unit] - 1
    keep = plan[room + unit]
    begin, _ = begin_of(plan, unit, width, blk, chunk)
    half = width // 2

    iso_copy = pltpu.make_async_copy(iso_all.at[plan[3 * room + slot]], iso, in_sems.at[0])
    iso_copy.start()
    spilled = begin - unit * chunk

    def spill_blocks(source, source_row, target, target_row, first, rows, held, sem, act):
        for i in range(rows // spill):

            @pl.when(i * spill < held)
            def _(i=i):
                act(
                    pltpu.make_async_copy(
                        source.at[pl.ds(source_row + i * spill, spill), :],
                        target.at[pl.ds(target_row + i * spill, spill), :],
                        sem.at[first + i],
                    )
                )

    start_copy = lambda copy: copy.start()
    wait_copy = lambda copy: copy.wait()
    if unit:
        spill_in = (refs[4], 0, packed, 0, 7, unit * spill, spilled, in_sems)
        spill_blocks(*spill_in, start_copy)
    env_copies = []
    for part in range(2):
        for c in range(3):
            rows = pl.ds(part * half, half)
            sem = in_sems.at[1 + 3 * part + c]
            target = e.at[c, rows]
            usual = pltpu.make_async_copy(env.at[0, jnp.maximum(slot - c, 0), rows], target, sem)
            if late and c:
                passed = pltpu.make_async_copy(
                    lower.at[jnp.clip(slot - c + 2, 0, 1), rows], target, sem
                )

                @pl.when(slot >= c)
                def _(usual=usual):
                    usual.start()

                @pl.when(slot < c)
                def _(passed=passed):
                    passed.start()

            else:
                usual.start()
            env_copies.append(usual)

    lane = lax.broadcasted_iota(jnp.int32, (blk, blk), 1)
    high = lax.broadcasted_iota(jnp.int32, (blk, blk), 0)
    inside = lane < keep
    scale = jnp.where(inside[:1], 1.0 / sing[slot], 0.0)
    scale = scale.astype(jnp.bfloat16).astype(jnp.float32)
    scale = jnp.broadcast_to(scale, (blk, blk))
    outer = scale * scale.T

    iso_copy.wait()
    placed = []
    for s in range(4):
        value = jnp.where(inside, iso[s].astype(jnp.float32), 0.0)
        placed.append(value)
        placed_t[s * blk : (s + 1) * blk, :] = value.T.astype(jnp.bfloat16)
    for x in range(nops):
        for p in range(4):
            total = None
            for s in range(4):
                if CHARGES[p] == CHARGES[s]:
                    term = table[p, s, x] * placed[s]
                    total = term if total is None else total + term
            mixer[p * blk : (p + 1) * blk, x * blk : (x + 1) * blk] = total.astype(jnp.bfloat16)

    tall = (keep + 15) // 16 * 16

    def bra_step(w, carry):
        rows = pl.ds(pl.multiple_of(w * tall, 16), blk)
        first = jnp.dot(placed_t[0:blk], e[0, w], preferred_element_type=jnp.float32)
        middle = jnp.dot(placed_t[blk : 3 * blk], e[1, w], preferred_element_type=jnp.float32)
        last = jnp.dot(placed_t[3 * blk :], e[2, w], preferred_element_type=jnp.float32)
        left[rows, 0:blk] = first.astype(jnp.bfloat16)
        left[rows, blk : 2 * blk] = middle[:blk].astype(jnp.bfloat16)
        left[rows, 2 * blk : 3 * blk] = middle[blk:].astype(jnp.bfloat16)
        left[rows, 3 * blk :] = last.astype(jnp.bfloat16)
        return carry

    def ket_step(begin, i, carry):
        rows = pl.ds(pl.multiple_of(begin + i * (32 * half), 16), 32 * half)
        for x in range(0, nops, 2):
            pair = jnp.dot(
                left[rows, :],
                mixer[:, x * blk : (x + 2) * blk],
                preferred_element_type=jnp.float32,
            )
            prod[x, rows, :] = pair[:, :blk]
            prod[x + 1, rows, :] = pair[:, blk:]
        return carry

    for part in range(2):
        for c in range(3):
            env_copies[3 * part + c].wait()
        lax.fori_loop(part * half, (part + 1) * half, bra_step, 0, unroll=half)
        lax.fori_loop(
            0, (tall + 31) // 32, functools.partial(ket_step, part * half * tall), 0
        )

    _, rows8, count = packed_shape(keep, width, blk)
    live = high < keep

    def column_step(v, current):
        total = None
        for t in range(3):
            begin = pl.multiple_of(row[t, v] * tall, 16)
            term = prod[op[t, v], pl.ds(begin, blk), :]
            total = term if total is None else total + term
        value = jnp.where(live, total, 0.0).astype(jnp.bfloat16)
        out[v] = value
        shift = (v * keep) % blk
        turned = pltpu.roll(value.astype(jnp.float32) * outer, shift, 1)
        current = jnp.where(lane < shift, current, turned)
        stage[pl.ds(pl.multiple_of((v * keep) // blk * rows8, 8), blk), :] = current
        return jnp.where(shift + keep >= blk, turned, current)

    current = jnp.zeros((blk, blk), jnp.float32)
    out_copies = []
    for part in range(2):
        current = lax.fori_loop(part * half, (part + 1) * half, column_step, current, unroll=half)
        rows = pl.ds(part * half, half)
        copy = pltpu.make_async_copy(out.at[rows], env_right.at[0, slot, rows], out_sems.at[part])
        copy.start()
        out_copies.append(copy)
    stage[pl.ds(pl.multiple_of((width * keep) // blk * rows8, 8), blk), :] = current

    if unit:
        spill_blocks(*spill_in, wait_copy)

    def cast_step(i, carry):
        source = pl.ds(pl.multiple_of(i * blk, blk), blk)
        target = pl.ds(pl.multiple_of(begin - unit * chunk + i * blk, 16), blk)
        packed[target, :] = stage[source, :].astype(jnp.bfloat16)
        return carry

    lax.fori_loop(0, (count + blk - 1) // blk, cast_step, 0)
    target = excess.at[pl.ds(0, chunk), :] if last else piece
    out_copies.append(
        pltpu.make_async_copy(packed.at[pl.ds(0, chunk), :], target, out_sems.at[2])
    )
    out_copies[-1].start()
    spill_out = (packed, chunk, excess, chunk * last, 3, (unit + 1) * spill, spilled + count - chunk)
    spill_blocks(*spill_out, out_sems, start_copy)
    spill_blocks(*spill_out, out_sems, wait_copy)
    for copy in out_copies:
        copy.wait()


def sector_call(unit, chunk, scalars, env, lower, isom, sing, env_right, excess, arrived):
    width, blk = env.shape[2], env.shape[3]
    nops = scalars[3].shape[-1]
    hbm_spec = pl.BlockSpec(memory_space=pltpu.HBM)
    operands = [env, isom, sing]
    in_specs = [hbm_spec, hbm_spec, pl.BlockSpec(memory_space=pltpu.VMEM)]
    if lower is not None:
        operands.insert(0, lower)
        in_specs.insert(0, pl.BlockSpec(memory_space=pl.ANY))
    aliases = {}
    if unit:
        aliases[len(scalars) + len(operands)] = 0
    extra = [array for array in (env_right, excess, arrived) if array is not None]
    operands += extra
    in_specs += [hbm_spec] * len(extra)
    if arrived is not None:
        in_specs[-1] = pl.BlockSpec(memory_space=pl.ANY)
    rows = width * blk
    spill = rows - chunk
    last = unit == env.shape[1] - 1
    bf16, f32 = jnp.bfloat16, jnp.float32
    return pl.pallas_call(
        functools.partial(sector_kernel, unit, chunk, lower is not None, last, spill),
        in_specs=[pl.BlockSpec(memory_space=pltpu.SMEM)] * len(scalars) + in_specs,
        out_specs=[hbm_spec] * (3 - last),
        out_shape=[jax.ShapeDtypeStruct(env.shape, bf16)]
        + [jax.ShapeDtypeStruct((chunk, blk), bf16)] * (not last)
        + [jax.ShapeDtypeStruct(((unit + 1) * spill + chunk * last, blk), bf16)],
        scratch_shapes=[
            pltpu.VMEM((3, width, blk, blk), bf16),
            pltpu.VMEM((4, blk, blk), bf16),
            pltpu.VMEM((4 * blk, blk), bf16),
            pltpu.VMEM((4 * blk, nops * blk), bf16),
            pltpu.VMEM((rows, 4 * blk), bf16),
            pltpu.VMEM((nops, rows, blk), f32),
            pltpu.VMEM((width, blk, blk), bf16),
            pltpu.VMEM((rows + blk, blk), f32),
            pltpu.VMEM((unit * spill + rows + blk, blk), bf16),
            pltpu.SemaphoreType.DMA((7 + unit,)),
            pltpu.SemaphoreType.DMA((4 + unit,)),
        ],
        input_output_aliases=aliases,
        compiler_params=pltpu.CompilerParams(vmem_limit_bytes=VMEM_LIMIT),
        cost_estimate=pl.CostEstimate(
            flops=COST, bytes_accessed=rows * blk, transcendentals=0
        ),
        name=f"sector_{unit}",
    )(*scalars, *operands)


def unpack_kernel(chunk, before, after, begin, last, plan, *refs):
    pieces = refs[: after - begin + last]
    handoff, held, stage, out, in_sems, out_sems = refs[-6:]
    room = 8
    width, blk = out.shape[1], out.shape[-1]
    units = handoff.shape[1]
    copies = []
    at = 0
    for i, piece in enumerate(pieces):
        copy = pltpu.make_async_copy(
            piece, held.at[pl.ds(at, piece.shape[0]), :], in_sems.at[i]
        )
        copy.start()
        copies.append(copy)
        at += piece.shape[0]
    for copy in copies:
        copy.wait()
    lane = lax.broadcasted_iota(jnp.int32, (blk, blk), 1)
    high = lax.broadcasted_iota(jnp.int32, (blk, blk), 0)

    def store(turn, slot):
        return pltpu.make_async_copy(out.at[turn], handoff.at[0, slot], out_sems.at[turn])

    def unit_step(u, carry):
        end, done = carry
        code = plan[0, u]
        keep = plan[0, room + u]
        slot = jnp.where(code > 0, code - 1, u)
        _, rows8, rows = packed_shape(keep, width, blk)
        start = jnp.maximum(end, u * chunk)
        end = start + rows
        active = jnp.bool_(True)
        if before:
            active = active & (end > before * chunk)
        if not last:
            active = active & (end <= after * chunk)
        turn = done % 2

        @pl.when(active)
        def _():
            @pl.when(done >= 2)
            def _():
                store(turn, slot).wait()

            shift_rows = start - begin * chunk

            def cast_step(i, carry):
                source = pl.ds(pl.multiple_of(shift_rows + i * blk, 16), blk)
                target = pl.ds(pl.multiple_of(i * blk, blk), blk)
                stage[target, :] = held[source, :].astype(jnp.float32)
                return carry

            lax.fori_loop(0, (rows + blk - 1) // blk, cast_step, 0)
            live = (high < keep) & (lane < keep)

            def column_step(v, carry):
                shift = (v * keep) % blk
                base = pl.multiple_of((v * keep) // blk * rows8, 8)
                this = stage[pl.ds(base, blk), :]
                following = stage[pl.ds(pl.multiple_of(base + rows8, 8), blk), :]
                value = jnp.where(lane >= shift, this, following)
                value = pltpu.roll(value, (blk - shift) % blk, 1)
                out[turn, v] = jnp.where(live, value, 0.0).astype(jnp.bfloat16)
                return carry

            lax.fori_loop(0, width, column_step, 0, unroll=width // 2)
            store(turn, slot).start()

        return end, done + active.astype(jnp.int32)

    _, done = lax.fori_loop(0, units, unit_step, (jnp.int32(0), jnp.int32(0)))

    for back in (1, 2):

        @pl.when(done >= back)
        def _(back=back):
            store((done - back) % 2, 0).wait()


def unpack_call(chunk, before, after, plan, pieces, tail, handoff, shape):
    width, blk = shape[2], shape[3]
    rows = width * blk
    begin = max(0, before - -(-rows // chunk)) if before else 0
    hbm_spec = pl.BlockSpec(memory_space=pltpu.HBM)
    any_spec = pl.BlockSpec(memory_space=pl.ANY)
    operands = list(pieces[begin:after]) + ([] if tail is None else [tail])
    count = len(operands)
    held = sum(piece.shape[0] for piece in operands)
    aliases = {}
    if handoff is not None:
        aliases[1 + count] = 0
        operands.append(handoff)
    return pl.pallas_call(
        functools.partial(unpack_kernel, chunk, before, after, begin, tail is not None),
        in_specs=[pl.BlockSpec(memory_space=pltpu.SMEM)]
        + [any_spec] * count
        + [hbm_spec] * (len(operands) - count),
        out_specs=hbm_spec,
        out_shape=jax.ShapeDtypeStruct(shape, jnp.bfloat16),
        scratch_shapes=[
            pltpu.VMEM((held + blk, blk), jnp.bfloat16),
            pltpu.VMEM((rows + 2 * blk, blk), jnp.float32),
            pltpu.VMEM((2, width, blk, blk), jnp.bfloat16),
            pltpu.SemaphoreType.DMA((count,)),
            pltpu.SemaphoreType.DMA((2,)),
        ],
        input_output_aliases=aliases,
        compiler_params=pltpu.CompilerParams(vmem_limit_bytes=VMEM_LIMIT),
        name=f"unpack_{after}",
    )(plan, *operands)


def send_tail(rows, chunk, shape, plan, excess, *pieces):
    got = passed_along(excess[:rows], "seg", 1)
    handoff = unpack_call(chunk, 0, len(pieces), plan, pieces, None, None, shape)
    return lax.dynamic_update_slice(excess, got, (0, 0)), handoff


def body(env_left, isometry, sing_vals, kept, twosite_sector, mpo_row, mpo_op, op_table):
    my_index = lax.axis_index("sec")
    devices, segments = lax.axis_size("sec"), lax.axis_size("seg")
    units, width, blk = env_left.shape[1:4]
    rows = width * blk
    chunk = int(rows * BASE) // 16 * 16
    routed, plan, tile = make_plan(
        isometry[0, 0], twosite_sector[0, 0], kept[SITES - 1, 0], my_index, devices, width, chunk
    )
    isom, plan_before, most, late_env = exchange(routed, tile, env_left, devices, segments)
    scalars = (plan, mpo_row.T, mpo_op.T, jnp.transpose(op_table, (1, 2, 0)))
    sing = jnp.transpose(sing_vals, (1, 0, 2))
    lower = passed_along(late_env, "sec", 1)
    env_right = excess = None
    pieces = []
    for unit in range(units):
        env_right, *sent, excess = sector_call(
            unit,
            chunk,
            scalars,
            env_left,
            lower if unit >= EARLY else None,
            isom,
            sing,
            env_right,
            excess,
            pieces[unit - 2] if 1 < unit < units - 1 else None,
        )
        pieces += [passed_along(piece, "seg", 1) for piece in sent]
    limits = []
    for share in TOTALS:
        limit = (int(units * share * rows) // 16 + 1) * 16 - (units - 1) * chunk
        limits.append(min(limit, excess.shape[0]))
    room = plan.shape[0] // 4
    need = most[0, 2 * room]
    level = sum((need > limit).astype(jnp.int32) for limit in limits[:-1])
    branches = [
        functools.partial(send_tail, limit, chunk, env_left.shape) for limit in limits
    ]
    early = units - 2
    tail, handoff = lax.switch(level, branches, plan_before, excess, *pieces[:early])
    handoff = unpack_call(
        chunk, early, units - 1, plan_before, pieces, tail, handoff, env_left.shape
    )
    return env_right, handoff


def solution(mesh):
    in_specs = (
        P("seg", "sec", None, None, None),
        P(None, "seg", "sec", None, None, None),
        P("seg", "sec", None),
        P(None, "seg", "sec"),
        P(None, "seg", None),
        P(),
        P(),
        P(),
    )
    out_specs = (P("seg", "sec", None, None, None), P("seg", "sec", None, None, None))
    return jax.shard_map(body, mesh=mesh, in_specs=in_specs, out_specs=out_specs, check_vma=False)
```

```python
import functools

import jax
import jax.numpy as jnp
from jax import lax
from jax.experimental import pallas as pl
from jax.experimental.pallas import tpu as pltpu
from jax.sharding import PartitionSpec as P

SITES = 1
CHARGES = (0, 1, 1, 2)
VMEM_LIMIT = 56 * 1024 * 1024
BASE = 0.6
TOTALS = (
    0.575, 0.6, 0.62, 0.64, 0.66, 0.68, 0.7, 0.72, 0.745, 0.775, 0.81, 0.86, 0.92, 1.0,
)
COST = 142606336
MESH = pl.DeviceIdType.MESH
EARLY = 4


def passed_along(block, axis, distance):
    devices = range(lax.axis_size(axis))
    route = [(i - distance, i) for i in devices if i - distance in devices]
    return lax.ppermute(block, axis, route)


def packed_shape(keep, width, blk):
    blocks = (width * keep + blk - 1) // blk
    rows = (keep + 7) // 8 * 8
    return blocks, rows, (blocks * rows + 15) // 16 * 16


def begin_of(plan, unit, width, blk, chunk):
    end = jnp.int32(0)
    begin = jnp.int32(0)
    for u in range(unit + 1):
        begin = jnp.maximum(end, u * chunk)
        end = begin + packed_shape(kept_of(plan, u), width, blk)[2]
    return begin, end


def kept_of(plan, unit):
    return plan[units_of(plan) + unit] if len(plan.shape) == 1 else plan[0, plan.shape[0] + unit]


def units_of(plan):
    return plan.shape[0] // 4


def plan_kernel(width, chunk, me_ref, sector_ref, kept_ref, src_ref, dst_ref, plan_ref, tile_ref):
    per_dev = src_ref.shape[0]
    blk = src_ref.shape[-1]
    room = units_of(plan_ref)
    first = me_ref[0] * per_dev
    for i in range(per_dev):
        owner = sector_ref[first + i] // per_dev
        dst_ref[owner] = src_ref[i]
    kept = [kept_ref[i] for i in range(per_dev)]

    def before(i, j):
        return kept[i] > kept[j] if i > j else kept[i] >= kept[j]

    def rank(j, members):
        total = jnp.int32(0)
        for i, inside in members:
            if i != j:
                total = total + (before(i, j) & inside).astype(jnp.int32)
        return total

    top = [(i, True) for i in range(2, per_dev)]
    high = {j: rank(j, top) for j in range(2, per_dev)}
    rest = [(0, True), (1, True)] + [(i, high[i] >= EARLY) for i in range(2, per_dev)]
    place = []
    for j in range(per_dev):
        late = EARLY + rank(j, rest)
        place.append(late if j < 2 else jnp.where(high[j] < EARLY, high[j], late))
    for i in range(4 * room):
        plan_ref[i] = 0
    for j in range(per_dev):
        plan_ref[place[j]] = j + 1
        plan_ref[room + place[j]] = kept[j]

    def find(n, carry):
        slot = sector_ref[n] - first
        inside = (slot >= 0) & (slot < per_dev)

        @pl.when(inside)
        def _():
            plan_ref[3 * room + slot] = n // per_dev

        return carry

    lax.fori_loop(0, sector_ref.shape[0], find, 0)
    _, end = begin_of(plan_ref, per_dev - 1, width, blk, chunk)
    plan_ref[2 * room] = end - (per_dev - 1) * chunk
    lane = lax.broadcasted_iota(jnp.int32, tile_ref.shape, 1)
    tile = jnp.zeros(tile_ref.shape, jnp.int32)
    for i in list(range(per_dev)) + list(range(room, room + per_dev)) + [2 * room]:
        tile = jnp.where(lane == i, plan_ref[i], tile)
    tile_ref[...] = tile


def make_plan(blocks, sector_row, kept, me, devices, width, chunk):
    scalar_spec = pl.BlockSpec(memory_space=pltpu.SMEM)
    vector_spec = pl.BlockSpec(memory_space=pltpu.VMEM)
    return pl.pallas_call(
        functools.partial(plan_kernel, width, chunk),
        in_specs=[scalar_spec, scalar_spec, scalar_spec, vector_spec],
        out_specs=[vector_spec, scalar_spec, vector_spec],
        out_shape=[
            jax.ShapeDtypeStruct((devices,) + blocks.shape[1:], blocks.dtype),
            jax.ShapeDtypeStruct((32,), jnp.int32),
            jax.ShapeDtypeStruct((8, 128), jnp.int32),
        ],
        name="make_plan",
    )(me.reshape(1), sector_row, kept, blocks)


def exchange_kernel(
    devices,
    segments,
    limits,
    routed,
    tile,
    env,
    isom,
    before,
    level,
    late,
    tiles,
    mine,
    ends,
    block_sems,
    tile_sems,
    end_sems,
    own_sem,
    late_sem,
):
    me = lax.axis_index("sec")
    seg = lax.axis_index("seg")
    peers = [lax.rem(me + k, devices) for k in range(1, devices)]
    others = [lax.rem(seg + k, segments) for k in range(1, segments)]
    barrier = pltpu.get_barrier_semaphore()
    for peer in peers:
        pl.semaphore_signal(barrier, inc=1, device_id={"sec": peer}, device_id_type=MESH)
    for other in others:
        pl.semaphore_signal(barrier, inc=1, device_id={"seg": other}, device_id_type=MESH)
    pl.semaphore_wait(barrier, len(peers) + len(others))

    own = pltpu.make_async_copy(routed.at[me], isom.at[me], own_sem)
    own.start()
    count = late.shape[0]
    aside = pltpu.make_async_copy(
        env.at[0, pl.ds(env.shape[1] - count, count)], late, late_sem
    )
    aside.start()

    def along(source, target, sems, axis, index, here, there):
        return pltpu.make_async_remote_copy(
            src_ref=source,
            dst_ref=target.at[here],
            send_sem=sems.at[0, index],
            recv_sem=sems.at[1, index],
            device_id={axis: there},
            device_id_type=MESH,
        )

    tile_copies = [
        along(tile, tiles, tile_sems, "sec", i, me, peer) for i, peer in enumerate(peers)
    ]
    block_copies = [
        along(routed.at[peer], isom, block_sems, "sec", i, me, peer)
        for i, peer in enumerate(peers)
    ]
    for copy in tile_copies + block_copies:
        copy.start()
    tiles[me] = tile[...]
    for copy in tile_copies:
        copy.wait()
    total = tiles[0]
    for i in range(1, devices):
        total = jnp.maximum(total, tiles[i])
    mine[0] = tile[...]
    mine[1] = total
    end_copies = [
        along(mine, ends, end_sems, "seg", i, seg, other) for i, other in enumerate(others)
    ]
    for copy in end_copies:
        copy.start()
    ends[seg] = mine[...]
    for copy in end_copies:
        copy.wait()
    total = ends[0, 1]
    for i in range(1, segments):
        total = jnp.maximum(total, ends[i, 1])
    level[...] = sum((total > limit).astype(jnp.int32) for limit in limits)
    before[...] = jnp.where(seg > 0, ends[jnp.maximum(seg - 1, 0), 0], 0)
    for copy in block_copies:
        copy.wait()
    own.wait()
    aside.wait()


def exchange(routed, tile, env, devices, segments, limits):
    vector_spec = pl.BlockSpec(memory_space=pltpu.VMEM)
    small = jax.ShapeDtypeStruct(tile.shape, tile.dtype)
    return pl.pallas_call(
        functools.partial(exchange_kernel, devices, segments, tuple(limits[:-1])),
        in_specs=[vector_spec, vector_spec, pl.BlockSpec(memory_space=pltpu.HBM)],
        out_specs=[vector_spec] * 4,
        out_shape=[
            jax.ShapeDtypeStruct(routed.shape, routed.dtype),
            small,
            small,
            jax.ShapeDtypeStruct((CHARGES[-1],) + env.shape[2:], env.dtype),
        ],
        scratch_shapes=[
            pltpu.VMEM((devices,) + tile.shape, tile.dtype),
            pltpu.VMEM((2,) + tile.shape, tile.dtype),
            pltpu.VMEM((segments, 2) + tile.shape, tile.dtype),
            pltpu.SemaphoreType.DMA((2, devices - 1)),
            pltpu.SemaphoreType.DMA((2, devices - 1)),
            pltpu.SemaphoreType.DMA((2, segments - 1)),
            pltpu.SemaphoreType.DMA,
            pltpu.SemaphoreType.DMA,
        ],
        compiler_params=pltpu.CompilerParams(
            collective_id=0, has_side_effects=True, vmem_limit_bytes=VMEM_LIMIT
        ),
        name="exchange",
    )(routed, tile, env)


def sector_kernel(unit, chunk, late, last, spill, plan, row, op, table, *refs):
    if late:
        lower, refs = refs[0], refs[1:]
    env, iso_all, sing = refs[:3]
    env_right, excess = refs[-14 + last], refs[-12]
    piece = None if last else refs[-13]
    e, iso, placed_t, mixer, left, prod, out, stage, packed, in_sems, out_sems = refs[-11:]
    room = units_of(plan)
    width, blk = e.shape[1], e.shape[-1]
    nops = table.shape[-1]
    slot = plan[unit] - 1
    keep = plan[room + unit]
    begin, _ = begin_of(plan, unit, width, blk, chunk)
    half = width // 2

    iso_copy = pltpu.make_async_copy(iso_all.at[plan[3 * room + slot]], iso, in_sems.at[0])
    iso_copy.start()
    spilled = begin - unit * chunk

    def spill_blocks(source, source_row, target, target_row, first, rows, held, sem, act):
        for i in range(rows // spill):

            @pl.when(i * spill < held)
            def _(i=i):
                act(
                    pltpu.make_async_copy(
                        source.at[pl.ds(source_row + i * spill, spill), :],
                        target.at[pl.ds(target_row + i * spill, spill), :],
                        sem.at[first + i],
                    )
                )

    start_copy = lambda copy: copy.start()
    wait_copy = lambda copy: copy.wait()
    if unit:
        spill_in = (refs[4], 0, packed, 0, 7, unit * spill, spilled, in_sems)
        spill_blocks(*spill_in, start_copy)
    for part in range(2):
        for c in range(3):
            rows = pl.ds(part * half, half)
            sem = in_sems.at[1 + 3 * part + c]
            target = e.at[c, rows]
            usual = pltpu.make_async_copy(env.at[0, jnp.maximum(slot - c, 0), rows], target, sem)
            if late and c:
                passed = pltpu.make_async_copy(
                    lower.at[jnp.clip(slot - c + 2, 0, 1), rows], target, sem
                )

                @pl.when(slot >= c)
                def _(usual=usual):
                    usual.start()

                @pl.when(slot < c)
                def _(passed=passed):
                    passed.start()

            else:
                usual.start()

    lane = lax.broadcasted_iota(jnp.int32, (blk, blk), 1)
    high = lax.broadcasted_iota(jnp.int32, (blk, blk), 0)
    inside = lane < keep
    scale = jnp.where(inside[:1], 1.0 / sing[slot], 0.0)
    scale = scale.astype(jnp.bfloat16).astype(jnp.float32)
    scale = jnp.broadcast_to(scale, (blk, blk))
    outer = scale * scale.T

    iso_copy.wait()
    placed = []
    for s in range(4):
        value = jnp.where(inside, iso[s].astype(jnp.float32), 0.0)
        placed.append(value)
        placed_t[s * blk : (s + 1) * blk, :] = value.T.astype(jnp.bfloat16)
    for x in range(nops):
        for p in range(4):
            total = None
            for s in range(4):
                if CHARGES[p] == CHARGES[s]:
                    term = table[p, s, x] * placed[s]
                    total = term if total is None else total + term
            mixer[p * blk : (p + 1) * blk, x * blk : (x + 1) * blk] = total.astype(jnp.bfloat16)

    tall = (keep + 15) // 16 * 16

    def bra_step(w, carry):
        rows = pl.ds(pl.multiple_of(w * tall, 16), blk)
        first = jnp.dot(placed_t[0:blk], e[0, w], preferred_element_type=jnp.float32)
        middle = jnp.dot(placed_t[blk : 3 * blk], e[1, w], preferred_element_type=jnp.float32)
        last = jnp.dot(placed_t[3 * blk :], e[2, w], preferred_element_type=jnp.float32)
        left[rows, 0:blk] = first.astype(jnp.bfloat16)
        left[rows, blk : 2 * blk] = middle[:blk].astype(jnp.bfloat16)
        left[rows, 2 * blk : 3 * blk] = middle[blk:].astype(jnp.bfloat16)
        left[rows, 3 * blk :] = last.astype(jnp.bfloat16)
        return carry

    def ket_step(begin, i, carry):
        rows = pl.ds(pl.multiple_of(begin + i * (32 * half), 16), 32 * half)
        for x in range(0, nops, 2):
            pair = jnp.dot(
                left[rows, :],
                mixer[:, x * blk : (x + 2) * blk],
                preferred_element_type=jnp.float32,
            )
            prod[x, rows, :] = pair[:, :blk]
            prod[x + 1, rows, :] = pair[:, blk:]
        return carry

    def product_part(part, carry):
        rows = pl.ds(part * half, half)
        for c in range(3):
            pltpu.make_async_copy(
                env.at[0, 0, rows], e.at[c, rows], in_sems.at[1 + 3 * part + c]
            ).wait()
        lax.fori_loop(0, half, lambda i, none: bra_step(part * half + i, none), 0, unroll=half)
        lax.fori_loop(
            0, (tall + 31) // 32, functools.partial(ket_step, part * (half * tall)), 0
        )
        return carry

    lax.fori_loop(0, 2, product_part, 0)

    _, rows8, count = packed_shape(keep, width, blk)
    live = high < keep

    def column_step(v, current):
        total = None
        for t in range(3):
            begin = pl.multiple_of(row[t, v] * tall, 16)
            term = prod[op[t, v], pl.ds(begin, blk), :]
            total = term if total is None else total + term
        value = jnp.where(live, total, 0.0).astype(jnp.bfloat16)
        out[v] = value
        shift = (v * keep) % blk
        turned = pltpu.roll(value.astype(jnp.float32) * outer, shift, 1)
        current = jnp.where(lane < shift, current, turned)
        stage[pl.ds(pl.multiple_of((v * keep) // blk * rows8, 8), blk), :] = current
        return jnp.where(shift + keep >= blk, turned, current)

    def out_copy(part):
        rows = pl.ds(part * half, half)
        return pltpu.make_async_copy(
            out.at[rows], env_right.at[0, slot, rows], out_sems.at[part]
        )

    def column_part(part, current):
        current = lax.fori_loop(
            0, half, lambda i, now: column_step(part * half + i, now), current, unroll=half
        )
        out_copy(part).start()
        return current

    current = lax.fori_loop(0, 2, column_part, jnp.zeros((blk, blk), jnp.float32))
    out_copies = [out_copy(0), out_copy(1)]
    stage[pl.ds(pl.multiple_of((width * keep) // blk * rows8, 8), blk), :] = current

    if unit:
        spill_blocks(*spill_in, wait_copy)

    def cast_step(i, carry):
        source = pl.ds(pl.multiple_of(i * blk, blk), blk)
        target = pl.ds(pl.multiple_of(begin - unit * chunk + i * blk, 16), blk)
        packed[target, :] = stage[source, :].astype(jnp.bfloat16)
        return carry

    lax.fori_loop(0, (count + blk - 1) // blk, cast_step, 0)
    target = excess.at[pl.ds(0, chunk), :] if last else piece
    out_copies.append(
        pltpu.make_async_copy(packed.at[pl.ds(0, chunk), :], target, out_sems.at[2])
    )
    out_copies[-1].start()
    spill_out = (packed, chunk, excess, chunk * last, 3, (unit + 1) * spill, spilled + count - chunk)
    spill_blocks(*spill_out, out_sems, start_copy)
    spill_blocks(*spill_out, out_sems, wait_copy)
    for copy in out_copies:
        copy.wait()


def sector_call(unit, chunk, scalars, env, lower, isom, sing, env_right, excess, arrived):
    width, blk = env.shape[2], env.shape[3]
    nops = scalars[3].shape[-1]
    hbm_spec = pl.BlockSpec(memory_space=pltpu.HBM)
    operands = [env, isom, sing]
    in_specs = [hbm_spec, hbm_spec, pl.BlockSpec(memory_space=pltpu.VMEM)]
    if lower is not None:
        operands.insert(0, lower)
        in_specs.insert(0, pl.BlockSpec(memory_space=pl.ANY))
    aliases = {}
    if unit:
        aliases[len(scalars) + len(operands)] = 0
    extra = [array for array in (env_right, excess, arrived) if array is not None]
    operands += extra
    in_specs += [hbm_spec] * len(extra)
    if arrived is not None:
        in_specs[-1] = pl.BlockSpec(memory_space=pl.ANY)
    rows = width * blk
    spill = rows - chunk
    last = unit == env.shape[1] - 1
    bf16, f32 = jnp.bfloat16, jnp.float32
    return pl.pallas_call(
        functools.partial(sector_kernel, unit, chunk, lower is not None, last, spill),
        in_specs=[pl.BlockSpec(memory_space=pltpu.SMEM)] * len(scalars) + in_specs,
        out_specs=[hbm_spec] * (3 - last),
        out_shape=[jax.ShapeDtypeStruct(env.shape, bf16)]
        + [jax.ShapeDtypeStruct((chunk, blk), bf16)] * (not last)
        + [jax.ShapeDtypeStruct(((unit + 1) * spill + chunk * last, blk), bf16)],
        scratch_shapes=[
            pltpu.VMEM((3, width, blk, blk), bf16),
            pltpu.VMEM((4, blk, blk), bf16),
            pltpu.VMEM((4 * blk, blk), bf16),
            pltpu.VMEM((4 * blk, nops * blk), bf16),
            pltpu.VMEM((rows, 4 * blk), bf16),
            pltpu.VMEM((nops, rows, blk), f32),
            pltpu.VMEM((width, blk, blk), bf16),
            pltpu.VMEM((rows + blk, blk), f32),
            pltpu.VMEM((unit * spill + rows + blk, blk), bf16),
            pltpu.SemaphoreType.DMA((7 + unit,)),
            pltpu.SemaphoreType.DMA((4 + unit,)),
        ],
        input_output_aliases=aliases,
        compiler_params=pltpu.CompilerParams(vmem_limit_bytes=VMEM_LIMIT),
        cost_estimate=pl.CostEstimate(
            flops=COST, bytes_accessed=rows * blk, transcendentals=0
        ),
        name=f"sector_{unit}",
    )(*scalars, *operands)


def unpack_kernel(chunk, before, after, begin, last, unroll, plan, *refs):
    pieces = refs[: after - begin + last]
    handoff, held, stage, out, in_sems, out_sems = refs[-6:]
    room = 8
    width, blk = out.shape[1], out.shape[-1]
    units = handoff.shape[1]
    copies = []
    at = 0
    for piece in pieces[: after - begin]:
        copies.append((piece, 0, at, piece.shape[0], None))
        at += piece.shape[0]
    if last:
        _, end = begin_of(plan, units - 1, width, blk, chunk)
        tail = pieces[-1]
        for first in range(0, tail.shape[0], chunk):
            count = min(chunk, tail.shape[0] - first)
            copies.append((tail, first, at + first, count, end - after * chunk > first))

    def each_copy(act):
        for i, (source, first, target, count, needed) in enumerate(copies):
            copy = pltpu.make_async_copy(
                source.at[pl.ds(first, count), :],
                held.at[pl.ds(target, count), :],
                in_sems.at[i],
            )
            if needed is None:
                act(copy)
            else:

                @pl.when(needed)
                def _(copy=copy):
                    act(copy)

    each_copy(lambda copy: copy.start())
    each_copy(lambda copy: copy.wait())
    lane = lax.broadcasted_iota(jnp.int32, (blk, blk), 1)
    high = lax.broadcasted_iota(jnp.int32, (blk, blk), 0)

    def store(turn, slot):
        return pltpu.make_async_copy(out.at[turn], handoff.at[0, slot], out_sems.at[turn])

    def unit_step(u, carry):
        end, done = carry
        code = plan[0, u]
        keep = plan[0, room + u]
        slot = jnp.where(code > 0, code - 1, u)
        _, rows8, rows = packed_shape(keep, width, blk)
        start = jnp.maximum(end, u * chunk)
        end = start + rows
        active = jnp.bool_(True)
        if before:
            active = active & (end > before * chunk)
        if not last:
            active = active & (end <= after * chunk)
        turn = done % 2

        @pl.when(active)
        def _():
            @pl.when(done >= 2)
            def _():
                store(turn, slot).wait()

            shift_rows = start - begin * chunk

            def cast_step(i, carry):
                source = pl.ds(pl.multiple_of(shift_rows + i * blk, 16), blk)
                target = pl.ds(pl.multiple_of(i * blk, blk), blk)
                stage[target, :] = held[source, :].astype(jnp.float32)
                return carry

            lax.fori_loop(0, (rows + blk - 1) // blk, cast_step, 0)
            live = (high < keep) & (lane < keep)

            def column_step(v, carry):
                shift = (v * keep) % blk
                base = pl.multiple_of((v * keep) // blk * rows8, 8)
                this = stage[pl.ds(base, blk), :]
                following = stage[pl.ds(pl.multiple_of(base + rows8, 8), blk), :]
                value = jnp.where(lane >= shift, this, following)
                value = pltpu.roll(value, (blk - shift) % blk, 1)
                out[turn, v] = jnp.where(live, value, 0.0).astype(jnp.bfloat16)
                return carry

            lax.fori_loop(0, width, column_step, 0, unroll=unroll)
            store(turn, slot).start()

        return end, done + active.astype(jnp.int32)

    _, done = lax.fori_loop(0, units, unit_step, (jnp.int32(0), jnp.int32(0)))

    for back in (1, 2):

        @pl.when(done >= back)
        def _(back=back):
            store((done - back) % 2, 0).wait()


def unpack_call(chunk, before, after, plan, pieces, tail, handoff, shape):
    units, width, blk = shape[1:4]
    rows = width * blk
    begin = max(0, before - -(-rows // chunk)) if before else 0
    unroll = 2 if tail is None else width // 2
    hbm_spec = pl.BlockSpec(memory_space=pltpu.HBM)
    any_spec = pl.BlockSpec(memory_space=pl.ANY)
    operands = list(pieces[begin:after]) + ([] if tail is None else [tail])
    count = len(operands)
    held = sum(piece.shape[0] for piece in operands)
    aliases = {}
    if handoff is not None:
        aliases[1 + count] = 0
        operands.append(handoff)
    return pl.pallas_call(
        functools.partial(unpack_kernel, chunk, before, after, begin, tail is not None, unroll),
        in_specs=[pl.BlockSpec(memory_space=pltpu.SMEM)]
        + [any_spec] * count
        + [hbm_spec] * (len(operands) - count),
        out_specs=hbm_spec,
        out_shape=jax.ShapeDtypeStruct(shape, jnp.bfloat16),
        scratch_shapes=[
            pltpu.VMEM((held + blk, blk), jnp.bfloat16),
            pltpu.VMEM((rows + 2 * blk, blk), jnp.float32),
            pltpu.VMEM((2, width, blk, blk), jnp.bfloat16),
            pltpu.SemaphoreType.DMA((count + units,)),
            pltpu.SemaphoreType.DMA((2,)),
        ],
        input_output_aliases=aliases,
        compiler_params=pltpu.CompilerParams(vmem_limit_bytes=VMEM_LIMIT),
        name=f"unpack_{after}",
    )(plan, *operands)


def send_tail(rows, chunk, shape, plan, excess, *pieces):
    got = passed_along(excess[:rows], "seg", 1)
    handoff = unpack_call(chunk, 0, len(pieces), plan, pieces, None, None, shape)
    return lax.dynamic_update_slice(excess, got, (0, 0)), handoff


def body(env_left, isometry, sing_vals, kept, twosite_sector, mpo_row, mpo_op, op_table):
    my_index = lax.axis_index("sec")
    devices, segments = lax.axis_size("sec"), lax.axis_size("seg")
    units, width, blk = env_left.shape[1:4]
    rows = width * blk
    chunk = int(rows * BASE) // 16 * 16
    routed, plan, tile = make_plan(
        isometry[0, 0], twosite_sector[0, 0], kept[SITES - 1, 0], my_index, devices, width, chunk
    )
    limits = []
    for share in TOTALS:
        limit = (int(units * share * rows) // 16 + 1) * 16 - (units - 1) * chunk
        limits.append(min(limit, units * rows - (units - 1) * chunk))
    isom, plan_before, level, late_env = exchange(
        routed, tile, env_left, devices, segments, limits
    )
    scalars = (plan, mpo_row.T, mpo_op.T, jnp.transpose(op_table, (1, 2, 0)))
    sing = jnp.transpose(sing_vals, (1, 0, 2))
    lower = passed_along(late_env, "sec", 1)
    env_right = excess = None
    pieces = []
    for unit in range(units):
        env_right, *sent, excess = sector_call(
            unit,
            chunk,
            scalars,
            env_left,
            lower if unit >= EARLY else None,
            isom,
            sing,
            env_right,
            excess,
            pieces[unit - 2] if 1 < unit < units - 1 else None,
        )
        pieces += [passed_along(piece, "seg", 1) for piece in sent]
    branches = [
        functools.partial(send_tail, limit, chunk, env_left.shape) for limit in limits
    ]
    early = units - 2
    tail, handoff = lax.switch(
        level[0, 2 * (plan.shape[0] // 4)], branches, plan_before, excess, *pieces[:early]
    )
    handoff = unpack_call(
        chunk, early, units - 1, plan_before, pieces, tail, handoff, env_left.shape
    )
    return env_right, handoff


def solution(mesh):
    in_specs = (
        P("seg", "sec", None, None, None),
        P(None, "seg", "sec", None, None, None),
        P("seg", "sec", None),
        P(None, "seg", "sec"),
        P(None, "seg", None),
        P(),
        P(),
        P(),
    )
    out_specs = (P("seg", "sec", None, None, None), P("seg", "sec", None, None, None))
    return jax.shard_map(body, mesh=mesh, in_specs=in_specs, out_specs=out_specs, check_vma=False)
```

```python
import functools

import jax
import jax.numpy as jnp
from jax import lax
from jax.experimental import pallas as pl
from jax.experimental.pallas import tpu as pltpu
from jax.sharding import PartitionSpec as P

SITES = 1
CHARGES = (0, 1, 1, 2)
VMEM_LIMIT = 56 * 1024 * 1024
BASE = 0.6
TOTALS = (
    0.575, 0.6, 0.62, 0.64, 0.66, 0.68, 0.7, 0.72, 0.745, 0.775, 0.81, 0.86, 0.92, 1.0,
)
COST = 142606336
MESH = pl.DeviceIdType.MESH
EARLY = 4


def passed_along(block, axis, distance):
    devices = range(lax.axis_size(axis))
    route = [(i - distance, i) for i in devices if i - distance in devices]
    return lax.ppermute(block, axis, route)


def packed_shape(keep, width, blk):
    blocks = (width * keep + blk - 1) // blk
    rows = (keep + 7) // 8 * 8
    return blocks, rows, (blocks * rows + 15) // 16 * 16


def begin_of(plan, unit, width, blk, chunk):
    end = jnp.int32(0)
    begin = jnp.int32(0)
    for u in range(unit + 1):
        begin = jnp.maximum(end, u * chunk)
        end = begin + packed_shape(kept_of(plan, u), width, blk)[2]
    return begin, end


def kept_of(plan, unit):
    return plan[units_of(plan) + unit] if len(plan.shape) == 1 else plan[0, plan.shape[0] + unit]


def units_of(plan):
    return plan.shape[0] // 4


def plan_kernel(width, chunk, me_ref, sector_ref, kept_ref, src_ref, dst_ref, plan_ref, tile_ref, held, sems):
    per_dev = src_ref.shape[0]
    blk = src_ref.shape[-1]
    room = units_of(plan_ref)
    first = me_ref[0] * per_dev
    copies = []
    for i in range(per_dev):
        owner = sector_ref[first + i] // per_dev
        copies.append(pltpu.make_async_copy(src_ref.at[i], held.at[owner], sems.at[i]))
        copies[-1].start()
    kept = [kept_ref[i] for i in range(per_dev)]

    def before(i, j):
        return kept[i] > kept[j] if i > j else kept[i] >= kept[j]

    def rank(j, members):
        total = jnp.int32(0)
        for i, inside in members:
            if i != j:
                total = total + (before(i, j) & inside).astype(jnp.int32)
        return total

    top = [(i, True) for i in range(2, per_dev)]
    high = {j: rank(j, top) for j in range(2, per_dev)}
    rest = [(0, True), (1, True)] + [(i, high[i] >= EARLY) for i in range(2, per_dev)]
    place = []
    for j in range(per_dev):
        late = EARLY + rank(j, rest)
        place.append(late if j < 2 else jnp.where(high[j] < EARLY, high[j], late))
    for i in range(4 * room):
        plan_ref[i] = 0
    for j in range(per_dev):
        plan_ref[place[j]] = j + 1
        plan_ref[room + place[j]] = kept[j]

    for copy in copies:
        copy.wait()
    routed = pltpu.make_async_copy(held, dst_ref, sems.at[per_dev])
    routed.start()

    def find(n, carry):
        slot = sector_ref[n] - first
        inside = (slot >= 0) & (slot < per_dev)

        @pl.when(inside)
        def _():
            plan_ref[3 * room + slot] = n // per_dev

        return carry

    lax.fori_loop(0, sector_ref.shape[0], find, 0)
    _, end = begin_of(plan_ref, per_dev - 1, width, blk, chunk)
    plan_ref[2 * room] = end - (per_dev - 1) * chunk
    lane = lax.broadcasted_iota(jnp.int32, tile_ref.shape, 1)
    tile = jnp.zeros(tile_ref.shape, jnp.int32)
    for i in list(range(per_dev)) + list(range(room, room + per_dev)) + [2 * room]:
        tile = jnp.where(lane == i, plan_ref[i], tile)
    tile_ref[...] = tile
    routed.wait()


def make_plan(blocks, sector_row, kept, me, devices, width, chunk):
    scalar_spec = pl.BlockSpec(memory_space=pltpu.SMEM)
    vector_spec = pl.BlockSpec(memory_space=pltpu.VMEM)
    hbm_spec = pl.BlockSpec(memory_space=pltpu.HBM)
    return pl.pallas_call(
        functools.partial(plan_kernel, width, chunk),
        in_specs=[scalar_spec, scalar_spec, scalar_spec, hbm_spec],
        out_specs=[hbm_spec, scalar_spec, vector_spec],
        out_shape=[
            jax.ShapeDtypeStruct((devices,) + blocks.shape[1:], blocks.dtype),
            jax.ShapeDtypeStruct((32,), jnp.int32),
            jax.ShapeDtypeStruct((8, 128), jnp.int32),
        ],
        scratch_shapes=[
            pltpu.VMEM((devices,) + blocks.shape[1:], blocks.dtype),
            pltpu.SemaphoreType.DMA((blocks.shape[0] + 1,)),
        ],
        name="make_plan",
    )(me.reshape(1), sector_row, kept, blocks)


def exchange_kernel(
    devices,
    segments,
    limits,
    routed,
    tile,
    env,
    isom,
    before,
    level,
    late,
    tiles,
    mine,
    ends,
    block_sems,
    tile_sems,
    end_sems,
    here,
    aside,
    own_sem,
    late_sem,
):
    me = lax.axis_index("sec")
    seg = lax.axis_index("seg")
    peers = [lax.rem(me + k, devices) for k in range(1, devices)]
    others = [lax.rem(seg + k, segments) for k in range(1, segments)]
    barrier = pltpu.get_barrier_semaphore()
    for peer in peers:
        pl.semaphore_signal(barrier, inc=1, device_id={"sec": peer}, device_id_type=MESH)
    for other in others:
        pl.semaphore_signal(barrier, inc=1, device_id={"seg": other}, device_id_type=MESH)
    pl.semaphore_wait(barrier, len(peers) + len(others))

    count = late.shape[0]
    copies_in = [
        pltpu.make_async_copy(routed.at[me], here, own_sem.at[0]),
        pltpu.make_async_copy(
            env.at[0, pl.ds(env.shape[1] - count, count)], aside, late_sem.at[0]
        ),
    ]
    copies_out = [
        pltpu.make_async_copy(here, isom.at[me], own_sem.at[1]),
        pltpu.make_async_copy(aside, late, late_sem.at[1]),
    ]
    for copy in copies_in:
        copy.start()

    def along(source, target, sems, axis, index, here, there):
        return pltpu.make_async_remote_copy(
            src_ref=source,
            dst_ref=target.at[here],
            send_sem=sems.at[0, index],
            recv_sem=sems.at[1, index],
            device_id={axis: there},
            device_id_type=MESH,
        )

    tile_copies = [
        along(tile, tiles, tile_sems, "sec", i, me, peer) for i, peer in enumerate(peers)
    ]
    block_copies = [
        along(routed.at[peer], isom, block_sems, "sec", i, me, peer)
        for i, peer in enumerate(peers)
    ]
    for copy in tile_copies + block_copies:
        copy.start()
    for copy, following in zip(copies_in, copies_out):
        copy.wait()
        following.start()
    tiles[me] = tile[...]
    for copy in tile_copies:
        copy.wait()
    total = tiles[0]
    for i in range(1, devices):
        total = jnp.maximum(total, tiles[i])
    mine[0] = tile[...]
    mine[1] = total
    end_copies = [
        along(mine, ends, end_sems, "seg", i, seg, other) for i, other in enumerate(others)
    ]
    for copy in end_copies:
        copy.start()
    ends[seg] = mine[...]
    for copy in end_copies:
        copy.wait()
    total = ends[0, 1]
    for i in range(1, segments):
        total = jnp.maximum(total, ends[i, 1])
    level[...] = sum((total > limit).astype(jnp.int32) for limit in limits)
    before[...] = jnp.where(seg > 0, ends[jnp.maximum(seg - 1, 0), 0], 0)
    for copy in block_copies:
        copy.wait()
    for copy in copies_out:
        copy.wait()


def exchange(routed, tile, env, devices, segments, limits):
    vector_spec = pl.BlockSpec(memory_space=pltpu.VMEM)
    hbm_spec = pl.BlockSpec(memory_space=pltpu.HBM)
    small = jax.ShapeDtypeStruct(tile.shape, tile.dtype)
    return pl.pallas_call(
        functools.partial(exchange_kernel, devices, segments, tuple(limits[:-1])),
        in_specs=[hbm_spec, vector_spec, hbm_spec],
        out_specs=[hbm_spec, vector_spec, vector_spec, hbm_spec],
        out_shape=[
            jax.ShapeDtypeStruct(routed.shape, routed.dtype),
            small,
            small,
            jax.ShapeDtypeStruct((CHARGES[-1],) + env.shape[2:], env.dtype),
        ],
        scratch_shapes=[
            pltpu.VMEM((devices,) + tile.shape, tile.dtype),
            pltpu.VMEM((2,) + tile.shape, tile.dtype),
            pltpu.VMEM((segments, 2) + tile.shape, tile.dtype),
            pltpu.SemaphoreType.DMA((2, devices - 1)),
            pltpu.SemaphoreType.DMA((2, devices - 1)),
            pltpu.SemaphoreType.DMA((2, segments - 1)),
            pltpu.VMEM(routed.shape[1:], routed.dtype),
            pltpu.VMEM((CHARGES[-1],) + env.shape[2:], env.dtype),
            pltpu.SemaphoreType.DMA((2,)),
            pltpu.SemaphoreType.DMA((2,)),
        ],
        compiler_params=pltpu.CompilerParams(
            collective_id=0, has_side_effects=True, vmem_limit_bytes=VMEM_LIMIT
        ),
        name="exchange",
    )(routed, tile, env)


def sector_kernel(unit, chunk, late, last, spill, plan, row, op, table, *refs):
    if late:
        lower, refs = refs[0], refs[1:]
    env, iso_all, sing = refs[:3]
    env_right, excess = refs[-14 + last], refs[-12]
    piece = None if last else refs[-13]
    e, iso, placed_t, mixer, left, prod, out, stage, packed, in_sems, out_sems = refs[-11:]
    room = units_of(plan)
    width, blk = e.shape[1], e.shape[-1]
    nops = table.shape[-1]
    slot = plan[unit] - 1
    keep = plan[room + unit]
    begin, _ = begin_of(plan, unit, width, blk, chunk)
    half = width // 2

    iso_copy = pltpu.make_async_copy(iso_all.at[plan[3 * room + slot]], iso, in_sems.at[0])
    iso_copy.start()
    spilled = begin - unit * chunk

    def spill_blocks(source, source_row, target, target_row, first, rows, held, sem, act):
        for i in range(rows // spill):

            @pl.when(i * spill < held)
            def _(i=i):
                act(
                    pltpu.make_async_copy(
                        source.at[pl.ds(source_row + i * spill, spill), :],
                        target.at[pl.ds(target_row + i * spill, spill), :],
                        sem.at[first + i],
                    )
                )

    start_copy = lambda copy: copy.start()
    wait_copy = lambda copy: copy.wait()
    if unit:
        spill_in = (refs[4], 0, packed, 0, 7, unit * spill, spilled, in_sems)
        spill_blocks(*spill_in, start_copy)
    for part in range(2):
        for c in range(3):
            rows = pl.ds(part * half, half)
            sem = in_sems.at[1 + 3 * part + c]
            target = e.at[c, rows]
            usual = pltpu.make_async_copy(env.at[0, jnp.maximum(slot - c, 0), rows], target, sem)
            if late and c:
                passed = pltpu.make_async_copy(
                    lower.at[jnp.clip(slot - c + 2, 0, 1), rows], target, sem
                )

                @pl.when(slot >= c)
                def _(usual=usual):
                    usual.start()

                @pl.when(slot < c)
                def _(passed=passed):
                    passed.start()

            else:
                usual.start()

    lane = lax.broadcasted_iota(jnp.int32, (blk, blk), 1)
    high = lax.broadcasted_iota(jnp.int32, (blk, blk), 0)
    inside = lane < keep
    scale = jnp.where(inside[:1], 1.0 / sing[slot], 0.0)
    scale = scale.astype(jnp.bfloat16).astype(jnp.float32)
    scale = jnp.broadcast_to(scale, (blk, blk))
    outer = scale * scale.T

    iso_copy.wait()
    placed = []
    for s in range(4):
        value = jnp.where(inside, iso[s].astype(jnp.float32), 0.0)
        placed.append(value)
        placed_t[s * blk : (s + 1) * blk, :] = value.T.astype(jnp.bfloat16)
    for x in range(nops):
        for p in range(4):
            total = None
            for s in range(4):
                if CHARGES[p] == CHARGES[s]:
                    term = table[p, s, x] * placed[s]
                    total = term if total is None else total + term
            mixer[p * blk : (p + 1) * blk, x * blk : (x + 1) * blk] = total.astype(jnp.bfloat16)

    tall = (keep + 15) // 16 * 16

    def bra_step(w, carry):
        rows = pl.ds(pl.multiple_of(w * tall, 16), blk)
        first = jnp.dot(placed_t[0:blk], e[0, w], preferred_element_type=jnp.float32)
        middle = jnp.dot(placed_t[blk : 3 * blk], e[1, w], preferred_element_type=jnp.float32)
        last = jnp.dot(placed_t[3 * blk :], e[2, w], preferred_element_type=jnp.float32)
        left[rows, 0:blk] = first.astype(jnp.bfloat16)
        left[rows, blk : 2 * blk] = middle[:blk].astype(jnp.bfloat16)
        left[rows, 2 * blk : 3 * blk] = middle[blk:].astype(jnp.bfloat16)
        left[rows, 3 * blk :] = last.astype(jnp.bfloat16)
        return carry

    def ket_step(begin, i, carry):
        rows = pl.ds(pl.multiple_of(begin + i * (32 * half), 16), 32 * half)
        for x in range(0, nops, 2):
            pair = jnp.dot(
                left[rows, :],
                mixer[:, x * blk : (x + 2) * blk],
                preferred_element_type=jnp.float32,
            )
            prod[x, rows, :] = pair[:, :blk]
            prod[x + 1, rows, :] = pair[:, blk:]
        return carry

    def product_part(part, carry):
        rows = pl.ds(part * half, half)
        for c in range(3):
            pltpu.make_async_copy(
                env.at[0, 0, rows], e.at[c, rows], in_sems.at[1 + 3 * part + c]
            ).wait()
        lax.fori_loop(0, half, lambda i, none: bra_step(part * half + i, none), 0, unroll=half)
        lax.fori_loop(
            0, (tall + 31) // 32, functools.partial(ket_step, part * (half * tall)), 0
        )
        return carry

    lax.fori_loop(0, 2, product_part, 0)

    _, rows8, count = packed_shape(keep, width, blk)
    live = high < keep

    def column_step(v, current):
        total = None
        for t in range(3):
            begin = pl.multiple_of(row[t, v] * tall, 16)
            term = prod[op[t, v], pl.ds(begin, blk), :]
            total = term if total is None else total + term
        value = jnp.where(live, total, 0.0).astype(jnp.bfloat16)
        out[v] = value
        shift = (v * keep) % blk
        turned = pltpu.roll(value.astype(jnp.float32) * outer, shift, 1)
        current = jnp.where(lane < shift, current, turned)
        stage[pl.ds(pl.multiple_of((v * keep) // blk * rows8, 8), blk), :] = current
        return jnp.where(shift + keep >= blk, turned, current)

    def out_copy(part):
        rows = pl.ds(part * half, half)
        return pltpu.make_async_copy(
            out.at[rows], env_right.at[0, slot, rows], out_sems.at[part]
        )

    def column_part(part, current):
        current = lax.fori_loop(
            0, half, lambda i, now: column_step(part * half + i, now), current, unroll=half
        )
        out_copy(part).start()
        return current

    current = lax.fori_loop(0, 2, column_part, jnp.zeros((blk, blk), jnp.float32))
    out_copies = [out_copy(0), out_copy(1)]
    stage[pl.ds(pl.multiple_of((width * keep) // blk * rows8, 8), blk), :] = current

    if unit:
        spill_blocks(*spill_in, wait_copy)

    def cast_step(i, carry):
        source = pl.ds(pl.multiple_of(i * blk, blk), blk)
        target = pl.ds(pl.multiple_of(begin - unit * chunk + i * blk, 16), blk)
        packed[target, :] = stage[source, :].astype(jnp.bfloat16)
        return carry

    lax.fori_loop(0, (count + blk - 1) // blk, cast_step, 0)
    target = excess.at[pl.ds(0, chunk), :] if last else piece
    out_copies.append(
        pltpu.make_async_copy(packed.at[pl.ds(0, chunk), :], target, out_sems.at[2])
    )
    out_copies[-1].start()
    spill_out = (packed, chunk, excess, chunk * last, 3, (unit + 1) * spill, spilled + count - chunk)
    spill_blocks(*spill_out, out_sems, start_copy)
    spill_blocks(*spill_out, out_sems, wait_copy)
    for copy in out_copies:
        copy.wait()


def sector_call(unit, chunk, scalars, env, lower, isom, sing, env_right, excess, arrived):
    width, blk = env.shape[2], env.shape[3]
    nops = scalars[3].shape[-1]
    hbm_spec = pl.BlockSpec(memory_space=pltpu.HBM)
    operands = [env, isom, sing]
    in_specs = [hbm_spec, hbm_spec, pl.BlockSpec(memory_space=pltpu.VMEM)]
    if lower is not None:
        operands.insert(0, lower)
        in_specs.insert(0, pl.BlockSpec(memory_space=pl.ANY))
    aliases = {}
    if unit:
        aliases[len(scalars) + len(operands)] = 0
    extra = [array for array in (env_right, excess, arrived) if array is not None]
    operands += extra
    in_specs += [hbm_spec] * len(extra)
    if arrived is not None:
        in_specs[-1] = pl.BlockSpec(memory_space=pl.ANY)
    rows = width * blk
    spill = rows - chunk
    last = unit == env.shape[1] - 1
    bf16, f32 = jnp.bfloat16, jnp.float32
    return pl.pallas_call(
        functools.partial(sector_kernel, unit, chunk, lower is not None, last, spill),
        in_specs=[pl.BlockSpec(memory_space=pltpu.SMEM)] * len(scalars) + in_specs,
        out_specs=[hbm_spec] * (3 - last),
        out_shape=[jax.ShapeDtypeStruct(env.shape, bf16)]
        + [jax.ShapeDtypeStruct((chunk, blk), bf16)] * (not last)
        + [jax.ShapeDtypeStruct(((unit + 1) * spill + chunk * last, blk), bf16)],
        scratch_shapes=[
            pltpu.VMEM((3, width, blk, blk), bf16),
            pltpu.VMEM((4, blk, blk), bf16),
            pltpu.VMEM((4 * blk, blk), bf16),
            pltpu.VMEM((4 * blk, nops * blk), bf16),
            pltpu.VMEM((rows, 4 * blk), bf16),
            pltpu.VMEM((nops, rows, blk), f32),
            pltpu.VMEM((width, blk, blk), bf16),
            pltpu.VMEM((rows + blk, blk), f32),
            pltpu.VMEM((unit * spill + rows + blk, blk), bf16),
            pltpu.SemaphoreType.DMA((7 + unit,)),
            pltpu.SemaphoreType.DMA((4 + unit,)),
        ],
        input_output_aliases=aliases,
        compiler_params=pltpu.CompilerParams(vmem_limit_bytes=VMEM_LIMIT),
        cost_estimate=pl.CostEstimate(
            flops=COST, bytes_accessed=rows * blk, transcendentals=0
        ),
        name=f"sector_{unit}",
    )(*scalars, *operands)


def unpack_kernel(chunk, before, after, begin, last, unroll, plan, *refs):
    pieces = refs[: after - begin + last]
    handoff, held, stage, out, in_sems, out_sems = refs[-6:]
    room = 8
    width, blk = out.shape[1], out.shape[-1]
    units = handoff.shape[1]
    copies = []
    at = 0
    for piece in pieces[: after - begin]:
        copies.append((piece, 0, at, piece.shape[0], None))
        at += piece.shape[0]
    if last:
        _, end = begin_of(plan, units - 1, width, blk, chunk)
        tail = pieces[-1]
        for first in range(0, tail.shape[0], chunk):
            count = min(chunk, tail.shape[0] - first)
            copies.append((tail, first, at + first, count, end - after * chunk > first))

    def each_copy(act):
        for i, (source, first, target, count, needed) in enumerate(copies):
            copy = pltpu.make_async_copy(
                source.at[pl.ds(first, count), :],
                held.at[pl.ds(target, count), :],
                in_sems.at[i],
            )
            if needed is None:
                act(copy)
            else:

                @pl.when(needed)
                def _(copy=copy):
                    act(copy)

    each_copy(lambda copy: copy.start())
    each_copy(lambda copy: copy.wait())
    lane = lax.broadcasted_iota(jnp.int32, (blk, blk), 1)
    high = lax.broadcasted_iota(jnp.int32, (blk, blk), 0)

    def store(turn, slot):
        return pltpu.make_async_copy(out.at[turn], handoff.at[0, slot], out_sems.at[turn])

    def unit_step(u, carry):
        end, done = carry
        code = plan[0, u]
        keep = plan[0, room + u]
        slot = jnp.where(code > 0, code - 1, u)
        _, rows8, rows = packed_shape(keep, width, blk)
        start = jnp.maximum(end, u * chunk)
        end = start + rows
        active = jnp.bool_(True)
        if before:
            active = active & (end > before * chunk)
        if not last:
            active = active & (end <= after * chunk)
        turn = done % 2

        @pl.when(active)
        def _():
            @pl.when(done >= 2)
            def _():
                store(turn, slot).wait()

            shift_rows = start - begin * chunk

            def cast_step(i, carry):
                source = pl.ds(pl.multiple_of(shift_rows + i * blk, 16), blk)
                target = pl.ds(pl.multiple_of(i * blk, blk), blk)
                stage[target, :] = held[source, :].astype(jnp.float32)
                return carry

            lax.fori_loop(0, (rows + blk - 1) // blk, cast_step, 0)
            live = (high < keep) & (lane < keep)

            def column_step(tall, v, carry):
                shift = (v * keep) % blk
                base = pl.multiple_of((v * keep) // blk * rows8, 8)
                this = stage[pl.ds(base, tall), :]
                following = stage[pl.ds(pl.multiple_of(base + rows8, 8), tall), :]
                value = jnp.where(lane[:tall] >= shift, this, following)
                value = pltpu.roll(value, (blk - shift) % blk, 1)
                out[turn, v, :tall] = jnp.where(live[:tall], value, 0.0).astype(jnp.bfloat16)
                if tall < blk:
                    out[turn, v, tall:] = jnp.zeros((blk - tall, blk), jnp.bfloat16)
                return carry

            def columns(tall):
                step = functools.partial(column_step, tall)
                lax.fori_loop(0, width, step, 0, unroll=unroll)

            if last:
                pl.when(keep <= blk // 2)(lambda: columns(blk // 2))
                pl.when(keep > blk // 2)(lambda: columns(blk))
            else:
                columns(blk)
            store(turn, slot).start()

        return end, done + active.astype(jnp.int32)

    _, done = lax.fori_loop(0, units, unit_step, (jnp.int32(0), jnp.int32(0)))

    for back in (1, 2):

        @pl.when(done >= back)
        def _(back=back):
            store((done - back) % 2, 0).wait()


def unpack_call(chunk, before, after, plan, pieces, tail, handoff, shape):
    units, width, blk = shape[1:4]
    rows = width * blk
    begin = max(0, before - -(-rows // chunk)) if before else 0
    unroll = 2 if tail is None else width // 2
    hbm_spec = pl.BlockSpec(memory_space=pltpu.HBM)
    any_spec = pl.BlockSpec(memory_space=pl.ANY)
    operands = list(pieces[begin:after]) + ([] if tail is None else [tail])
    count = len(operands)
    held = sum(piece.shape[0] for piece in operands)
    aliases = {}
    if handoff is not None:
        aliases[1 + count] = 0
        operands.append(handoff)
    return pl.pallas_call(
        functools.partial(unpack_kernel, chunk, before, after, begin, tail is not None, unroll),
        in_specs=[pl.BlockSpec(memory_space=pltpu.SMEM)]
        + [any_spec] * count
        + [hbm_spec] * (len(operands) - count),
        out_specs=hbm_spec,
        out_shape=jax.ShapeDtypeStruct(shape, jnp.bfloat16),
        scratch_shapes=[
            pltpu.VMEM((held + blk, blk), jnp.bfloat16),
            pltpu.VMEM((rows + 2 * blk, blk), jnp.float32),
            pltpu.VMEM((2, width, blk, blk), jnp.bfloat16),
            pltpu.SemaphoreType.DMA((count + units,)),
            pltpu.SemaphoreType.DMA((2,)),
        ],
        input_output_aliases=aliases,
        compiler_params=pltpu.CompilerParams(vmem_limit_bytes=VMEM_LIMIT),
        name=f"unpack_{after}",
    )(plan, *operands)


def send_tail(rows, chunk, shape, plan, excess, *pieces):
    got = passed_along(excess[:rows], "seg", 1)
    handoff = unpack_call(chunk, 0, len(pieces), plan, pieces, None, None, shape)
    return lax.dynamic_update_slice(excess, got, (0, 0)), handoff


def body(env_left, isometry, sing_vals, kept, twosite_sector, mpo_row, mpo_op, op_table):
    my_index = lax.axis_index("sec")
    devices, segments = lax.axis_size("sec"), lax.axis_size("seg")
    units, width, blk = env_left.shape[1:4]
    rows = width * blk
    chunk = int(rows * BASE) // 16 * 16
    routed, plan, tile = make_plan(
        isometry[0, 0], twosite_sector[0, 0], kept[SITES - 1, 0], my_index, devices, width, chunk
    )
    limits = []
    for share in TOTALS:
        limit = (int(units * share * rows) // 16 + 1) * 16 - (units - 1) * chunk
        limits.append(min(limit, units * rows - (units - 1) * chunk))
    isom, plan_before, level, late_env = exchange(
        routed, tile, env_left, devices, segments, limits
    )
    scalars = (plan, mpo_row.T, mpo_op.T, jnp.transpose(op_table, (1, 2, 0)))
    sing = jnp.transpose(sing_vals, (1, 0, 2))
    lower = passed_along(late_env, "sec", 1)
    env_right = excess = None
    pieces = []
    for unit in range(units):
        env_right, *sent, excess = sector_call(
            unit,
            chunk,
            scalars,
            env_left,
            lower if unit >= EARLY else None,
            isom,
            sing,
            env_right,
            excess,
            pieces[unit - 2] if 1 < unit < units - 1 else None,
        )
        pieces += [passed_along(piece, "seg", 1) for piece in sent]
    branches = [
        functools.partial(send_tail, limit, chunk, env_left.shape) for limit in limits
    ]
    early = units - 2
    tail, handoff = lax.switch(
        level[0, 2 * (plan.shape[0] // 4)], branches, plan_before, excess, *pieces[:early]
    )
    handoff = unpack_call(
        chunk, early, units - 1, plan_before, pieces, tail, handoff, env_left.shape
    )
    return env_right, handoff


def solution(mesh):
    in_specs = (
        P("seg", "sec", None, None, None),
        P(None, "seg", "sec", None, None, None),
        P("seg", "sec", None),
        P(None, "seg", "sec"),
        P(None, "seg", None),
        P(),
        P(),
        P(),
    )
    out_specs = (P("seg", "sec", None, None, None), P("seg", "sec", None, None, None))
    return jax.shard_map(body, mesh=mesh, in_specs=in_specs, out_specs=out_specs, check_vma=False)
```

```python
import functools

import jax
import jax.numpy as jnp
from jax import lax
from jax.experimental import pallas as pl
from jax.experimental.pallas import tpu as pltpu
from jax.sharding import PartitionSpec as P

SITES = 1
CHARGES = (0, 1, 1, 2)
VMEM_LIMIT = 56 * 1024 * 1024
BASE = 0.6
TOTALS = (
    0.575, 0.6, 0.62, 0.64, 0.66, 0.68, 0.7, 0.72, 0.745, 0.775, 0.81, 0.86, 0.92, 1.0,
)
COST = 142606336
MESH = pl.DeviceIdType.MESH
EARLY = 4


def passed_along(block, axis, distance):
    devices = range(lax.axis_size(axis))
    route = [(i - distance, i) for i in devices if i - distance in devices]
    return lax.ppermute(block, axis, route)


def packed_shape(keep, width, blk):
    blocks = (width * keep + blk - 1) // blk
    rows = (keep + 7) // 8 * 8
    return blocks, rows, (blocks * rows + 15) // 16 * 16


def begin_of(plan, unit, width, blk, chunk):
    end = jnp.int32(0)
    begin = jnp.int32(0)
    for u in range(unit + 1):
        begin = jnp.maximum(end, u * chunk)
        end = begin + packed_shape(kept_of(plan, u), width, blk)[2]
    return begin, end


def kept_of(plan, unit):
    return plan[units_of(plan) + unit] if len(plan.shape) == 1 else plan[0, plan.shape[0] + unit]


def units_of(plan):
    return plan.shape[0] // 4


def plan_kernel(width, chunk, me_ref, sector_ref, kept_ref, src_ref, dst_ref, plan_ref, tile_ref, held, sems):
    per_dev = src_ref.shape[0]
    blk = src_ref.shape[-1]
    room = units_of(plan_ref)
    first = me_ref[0] * per_dev
    copies = []
    for i in range(per_dev):
        owner = sector_ref[first + i] // per_dev
        copies.append(pltpu.make_async_copy(src_ref.at[i], held.at[owner], sems.at[i]))
        copies[-1].start()
    kept = [kept_ref[i] for i in range(per_dev)]

    def before(i, j):
        return kept[i] > kept[j] if i > j else kept[i] >= kept[j]

    def rank(j, members):
        total = jnp.int32(0)
        for i, inside in members:
            if i != j:
                total = total + (before(i, j) & inside).astype(jnp.int32)
        return total

    top = [(i, True) for i in range(2, per_dev)]
    high = {j: rank(j, top) for j in range(2, per_dev)}
    rest = [(0, True), (1, True)] + [(i, high[i] >= EARLY) for i in range(2, per_dev)]
    place = []
    for j in range(per_dev):
        late = EARLY + rank(j, rest)
        place.append(late if j < 2 else jnp.where(high[j] < EARLY, high[j], late))
    for i in range(4 * room):
        plan_ref[i] = 0
    for j in range(per_dev):
        plan_ref[place[j]] = j + 1
        plan_ref[room + place[j]] = kept[j]

    for copy in copies:
        copy.wait()
    routed = pltpu.make_async_copy(held, dst_ref, sems.at[per_dev])
    routed.start()

    def find(n, carry):
        slot = sector_ref[n] - first
        inside = (slot >= 0) & (slot < per_dev)

        @pl.when(inside)
        def _():
            plan_ref[3 * room + slot] = n // per_dev

        return carry

    lax.fori_loop(0, sector_ref.shape[0], find, 0)
    _, end = begin_of(plan_ref, per_dev - 1, width, blk, chunk)
    plan_ref[2 * room] = end - (per_dev - 1) * chunk
    lane = lax.broadcasted_iota(jnp.int32, tile_ref.shape, 1)
    tile = jnp.zeros(tile_ref.shape, jnp.int32)
    for i in list(range(per_dev)) + list(range(room, room + per_dev)) + [2 * room]:
        tile = jnp.where(lane == i, plan_ref[i], tile)
    tile_ref[...] = tile
    routed.wait()


def make_plan(blocks, sector_row, kept, me, devices, width, chunk):
    scalar_spec = pl.BlockSpec(memory_space=pltpu.SMEM)
    vector_spec = pl.BlockSpec(memory_space=pltpu.VMEM)
    hbm_spec = pl.BlockSpec(memory_space=pltpu.HBM)
    return pl.pallas_call(
        functools.partial(plan_kernel, width, chunk),
        in_specs=[scalar_spec, scalar_spec, scalar_spec, hbm_spec],
        out_specs=[hbm_spec, scalar_spec, vector_spec],
        out_shape=[
            jax.ShapeDtypeStruct((devices,) + blocks.shape[1:], blocks.dtype),
            jax.ShapeDtypeStruct((32,), jnp.int32),
            jax.ShapeDtypeStruct((8, 128), jnp.int32),
        ],
        scratch_shapes=[
            pltpu.VMEM((devices,) + blocks.shape[1:], blocks.dtype),
            pltpu.SemaphoreType.DMA((blocks.shape[0] + 1,)),
        ],
        name="make_plan",
    )(me.reshape(1), sector_row, kept, blocks)


def exchange_kernel(
    devices,
    segments,
    limits,
    routed,
    tile,
    env,
    isom,
    before,
    level,
    late,
    tiles,
    mine,
    ends,
    block_sems,
    tile_sems,
    end_sems,
    here,
    aside,
    own_sem,
    late_sem,
):
    me = lax.axis_index("sec")
    seg = lax.axis_index("seg")
    peers = [lax.rem(me + k, devices) for k in range(1, devices)]
    others = [lax.rem(seg + k, segments) for k in range(1, segments)]
    barrier = pltpu.get_barrier_semaphore()
    for peer in peers:
        pl.semaphore_signal(barrier, inc=1, device_id={"sec": peer}, device_id_type=MESH)
    for other in others:
        pl.semaphore_signal(barrier, inc=1, device_id={"seg": other}, device_id_type=MESH)
    pl.semaphore_wait(barrier, len(peers) + len(others))

    count = late.shape[0]
    copies_in = [
        pltpu.make_async_copy(routed.at[me], here, own_sem.at[0]),
        pltpu.make_async_copy(
            env.at[0, pl.ds(env.shape[1] - count, count)], aside, late_sem.at[0]
        ),
    ]
    copies_out = [
        pltpu.make_async_copy(here, isom.at[me], own_sem.at[1]),
        pltpu.make_async_copy(aside, late, late_sem.at[1]),
    ]
    for copy in copies_in:
        copy.start()

    def along(source, target, sems, axis, index, here, there):
        return pltpu.make_async_remote_copy(
            src_ref=source,
            dst_ref=target.at[here],
            send_sem=sems.at[0, index],
            recv_sem=sems.at[1, index],
            device_id={axis: there},
            device_id_type=MESH,
        )

    tile_copies = [
        along(tile, tiles, tile_sems, "sec", i, me, peer) for i, peer in enumerate(peers)
    ]
    block_copies = [
        along(routed.at[peer], isom, block_sems, "sec", i, me, peer)
        for i, peer in enumerate(peers)
    ]
    for copy in tile_copies + block_copies:
        copy.start()
    for copy, following in zip(copies_in, copies_out):
        copy.wait()
        following.start()
    tiles[me] = tile[...]
    for copy in tile_copies:
        copy.wait()
    total = tiles[0]
    for i in range(1, devices):
        total = jnp.maximum(total, tiles[i])
    mine[0] = tile[...]
    mine[1] = total
    end_copies = [
        along(mine, ends, end_sems, "seg", i, seg, other) for i, other in enumerate(others)
    ]
    for copy in end_copies:
        copy.start()
    ends[seg] = mine[...]
    for copy in end_copies:
        copy.wait()
    total = ends[0, 1]
    for i in range(1, segments):
        total = jnp.maximum(total, ends[i, 1])
    level[...] = sum((total > limit).astype(jnp.int32) for limit in limits)
    before[...] = jnp.where(seg > 0, ends[jnp.maximum(seg - 1, 0), 0], 0)
    for copy in block_copies:
        copy.wait()
    for copy in copies_out:
        copy.wait()


def exchange(routed, tile, env, devices, segments, limits):
    vector_spec = pl.BlockSpec(memory_space=pltpu.VMEM)
    hbm_spec = pl.BlockSpec(memory_space=pltpu.HBM)
    small = jax.ShapeDtypeStruct(tile.shape, tile.dtype)
    return pl.pallas_call(
        functools.partial(exchange_kernel, devices, segments, tuple(limits[:-1])),
        in_specs=[hbm_spec, vector_spec, hbm_spec],
        out_specs=[hbm_spec, vector_spec, vector_spec, hbm_spec],
        out_shape=[
            jax.ShapeDtypeStruct(routed.shape, routed.dtype),
            small,
            small,
            jax.ShapeDtypeStruct((CHARGES[-1],) + env.shape[2:], env.dtype),
        ],
        scratch_shapes=[
            pltpu.VMEM((devices,) + tile.shape, tile.dtype),
            pltpu.VMEM((2,) + tile.shape, tile.dtype),
            pltpu.VMEM((segments, 2) + tile.shape, tile.dtype),
            pltpu.SemaphoreType.DMA((2, devices - 1)),
            pltpu.SemaphoreType.DMA((2, devices - 1)),
            pltpu.SemaphoreType.DMA((2, segments - 1)),
            pltpu.VMEM(routed.shape[1:], routed.dtype),
            pltpu.VMEM((CHARGES[-1],) + env.shape[2:], env.dtype),
            pltpu.SemaphoreType.DMA((2,)),
            pltpu.SemaphoreType.DMA((2,)),
        ],
        compiler_params=pltpu.CompilerParams(
            collective_id=0, has_side_effects=True, vmem_limit_bytes=VMEM_LIMIT
        ),
        name="exchange",
    )(routed, tile, env)


def sector_kernel(unit, chunk, late, last, spill, plan, row, op, table, *refs):
    if late:
        lower, refs = refs[0], refs[1:]
    env, iso_all, sing = refs[:3]
    env_right, excess = refs[-14 + last], refs[-12]
    piece = None if last else refs[-13]
    e, iso, placed_t, mixer, left, prod, out, stage, packed, in_sems, out_sems = refs[-11:]
    room = units_of(plan)
    width, blk = e.shape[1], e.shape[-1]
    nops = table.shape[-1]
    slot = plan[unit] - 1
    keep = plan[room + unit]
    begin, _ = begin_of(plan, unit, width, blk, chunk)
    half = width // 2

    iso_copy = pltpu.make_async_copy(iso_all.at[plan[3 * room + slot]], iso, in_sems.at[0])
    iso_copy.start()
    spilled = begin - unit * chunk

    def spill_blocks(source, source_row, target, target_row, first, rows, held, sem, act):
        for i in range(rows // spill):

            @pl.when(i * spill < held)
            def _(i=i):
                act(
                    pltpu.make_async_copy(
                        source.at[pl.ds(source_row + i * spill, spill), :],
                        target.at[pl.ds(target_row + i * spill, spill), :],
                        sem.at[first + i],
                    )
                )

    start_copy = lambda copy: copy.start()
    wait_copy = lambda copy: copy.wait()
    if unit:
        spill_in = (refs[4], 0, packed, 0, 7, unit * spill, spilled, in_sems)
        spill_blocks(*spill_in, start_copy)
    for part in range(2):
        for c in range(3):
            rows = pl.ds(part * half, half)
            sem = in_sems.at[1 + 3 * part + c]
            target = e.at[c, rows]
            usual = pltpu.make_async_copy(env.at[0, jnp.maximum(slot - c, 0), rows], target, sem)
            if late and c:
                passed = pltpu.make_async_copy(
                    lower.at[jnp.clip(slot - c + 2, 0, 1), rows], target, sem
                )

                @pl.when(slot >= c)
                def _(usual=usual):
                    usual.start()

                @pl.when(slot < c)
                def _(passed=passed):
                    passed.start()

            else:
                usual.start()

    lane = lax.broadcasted_iota(jnp.int32, (blk, blk), 1)
    high = lax.broadcasted_iota(jnp.int32, (blk, blk), 0)
    inside = lane < keep
    scale = jnp.where(inside[:1], 1.0 / sing[slot], 0.0)
    scale = scale.astype(jnp.bfloat16).astype(jnp.float32)
    scale = jnp.broadcast_to(scale, (blk, blk))
    outer = scale * scale.T

    iso_copy.wait()
    placed = []
    for s in range(4):
        value = jnp.where(inside, iso[s].astype(jnp.float32), 0.0)
        placed.append(value)
        placed_t[s * blk : (s + 1) * blk, :] = value.T.astype(jnp.bfloat16)
    for x in range(nops):
        for p in range(4):
            total = None
            for s in range(4):
                if CHARGES[p] == CHARGES[s]:
                    term = table[p, s, x] * placed[s]
                    total = term if total is None else total + term
            mixer[p * blk : (p + 1) * blk, x * blk : (x + 1) * blk] = total.astype(jnp.bfloat16)

    tall = (keep + 15) // 16 * 16

    def bra_step(w, carry):
        rows = pl.ds(pl.multiple_of(w * tall, 16), blk)
        first = jnp.dot(placed_t[0:blk], e[0, w], preferred_element_type=jnp.float32)
        middle = jnp.dot(placed_t[blk : 3 * blk], e[1, w], preferred_element_type=jnp.float32)
        last = jnp.dot(placed_t[3 * blk :], e[2, w], preferred_element_type=jnp.float32)
        left[rows, 0:blk] = first.astype(jnp.bfloat16)
        left[rows, blk : 2 * blk] = middle[:blk].astype(jnp.bfloat16)
        left[rows, 2 * blk : 3 * blk] = middle[blk:].astype(jnp.bfloat16)
        left[rows, 3 * blk :] = last.astype(jnp.bfloat16)
        return carry

    step = 32 if unit else 64

    def ket_step(begin, i, carry):
        rows = pl.ds(pl.multiple_of(begin + i * (step * half), 16), step * half)
        for x in range(0, nops, 2):
            pair = jnp.dot(
                left[rows, :],
                mixer[:, x * blk : (x + 2) * blk],
                preferred_element_type=jnp.float32,
            )
            prod[x, rows, :] = pair[:, :blk]
            prod[x + 1, rows, :] = pair[:, blk:]
        return carry

    def product_part(part, carry):
        rows = pl.ds(part * half, half)
        for c in range(3):
            pltpu.make_async_copy(
                env.at[0, 0, rows], e.at[c, rows], in_sems.at[1 + 3 * part + c]
            ).wait()
        lax.fori_loop(0, half, lambda i, none: bra_step(part * half + i, none), 0, unroll=half)
        lax.fori_loop(
            0, (tall + step - 1) // step, functools.partial(ket_step, part * (half * tall)), 0
        )
        return carry

    lax.fori_loop(0, 2, product_part, 0)

    _, rows8, count = packed_shape(keep, width, blk)
    live = high < keep

    def column_step(v, current):
        total = None
        for t in range(3):
            begin = pl.multiple_of(row[t, v] * tall, 16)
            term = prod[op[t, v], pl.ds(begin, blk), :]
            total = term if total is None else total + term
        value = jnp.where(live, total, 0.0).astype(jnp.bfloat16)
        out[v] = value
        shift = (v * keep) % blk
        turned = pltpu.roll(value.astype(jnp.float32) * outer, shift, 1)
        current = jnp.where(lane < shift, current, turned)
        stage[pl.ds(pl.multiple_of((v * keep) // blk * rows8, 8), blk), :] = current
        return jnp.where(shift + keep >= blk, turned, current)

    def out_copy(part):
        rows = pl.ds(part * half, half)
        return pltpu.make_async_copy(
            out.at[rows], env_right.at[0, slot, rows], out_sems.at[part]
        )

    def column_part(part, current):
        current = lax.fori_loop(
            0, half, lambda i, now: column_step(part * half + i, now), current, unroll=half
        )
        out_copy(part).start()
        return current

    current = lax.fori_loop(0, 2, column_part, jnp.zeros((blk, blk), jnp.float32))
    out_copies = [out_copy(0), out_copy(1)]
    stage[pl.ds(pl.multiple_of((width * keep) // blk * rows8, 8), blk), :] = current

    if unit:
        spill_blocks(*spill_in, wait_copy)

    def cast_step(i, carry):
        source = pl.ds(pl.multiple_of(i * blk, blk), blk)
        target = pl.ds(pl.multiple_of(begin - unit * chunk + i * blk, 16), blk)
        packed[target, :] = stage[source, :].astype(jnp.bfloat16)
        return carry

    lax.fori_loop(0, (count + blk - 1) // blk, cast_step, 0)
    target = excess.at[pl.ds(0, chunk), :] if last else piece
    out_copies.append(
        pltpu.make_async_copy(packed.at[pl.ds(0, chunk), :], target, out_sems.at[2])
    )
    out_copies[-1].start()
    spill_out = (packed, chunk, excess, chunk * last, 3, (unit + 1) * spill, spilled + count - chunk)
    spill_blocks(*spill_out, out_sems, start_copy)
    spill_blocks(*spill_out, out_sems, wait_copy)
    for copy in out_copies:
        copy.wait()


def sector_call(unit, chunk, scalars, env, lower, isom, sing, env_right, excess, arrived):
    width, blk = env.shape[2], env.shape[3]
    nops = scalars[3].shape[-1]
    hbm_spec = pl.BlockSpec(memory_space=pltpu.HBM)
    operands = [env, isom, sing]
    in_specs = [hbm_spec, hbm_spec, pl.BlockSpec(memory_space=pltpu.VMEM)]
    if lower is not None:
        operands.insert(0, lower)
        in_specs.insert(0, pl.BlockSpec(memory_space=pl.ANY))
    aliases = {}
    if unit:
        aliases[len(scalars) + len(operands)] = 0
    extra = [array for array in (env_right, excess, arrived) if array is not None]
    operands += extra
    in_specs += [hbm_spec] * len(extra)
    if arrived is not None:
        in_specs[-1] = pl.BlockSpec(memory_space=pl.ANY)
    rows = width * blk
    spill = rows - chunk
    last = unit == env.shape[1] - 1
    bf16, f32 = jnp.bfloat16, jnp.float32
    return pl.pallas_call(
        functools.partial(sector_kernel, unit, chunk, lower is not None, last, spill),
        in_specs=[pl.BlockSpec(memory_space=pltpu.SMEM)] * len(scalars) + in_specs,
        out_specs=[hbm_spec] * (3 - last),
        out_shape=[jax.ShapeDtypeStruct(env.shape, bf16)]
        + [jax.ShapeDtypeStruct((chunk, blk), bf16)] * (not last)
        + [jax.ShapeDtypeStruct(((unit + 1) * spill + chunk * last, blk), bf16)],
        scratch_shapes=[
            pltpu.VMEM((3, width, blk, blk), bf16),
            pltpu.VMEM((4, blk, blk), bf16),
            pltpu.VMEM((4 * blk, blk), bf16),
            pltpu.VMEM((4 * blk, nops * blk), bf16),
            pltpu.VMEM((rows, 4 * blk), bf16),
            pltpu.VMEM((nops, rows, blk), f32),
            pltpu.VMEM((width, blk, blk), bf16),
            pltpu.VMEM((rows + blk, blk), f32),
            pltpu.VMEM((unit * spill + rows + blk, blk), bf16),
            pltpu.SemaphoreType.DMA((7 + unit,)),
            pltpu.SemaphoreType.DMA((4 + unit,)),
        ],
        input_output_aliases=aliases,
        compiler_params=pltpu.CompilerParams(vmem_limit_bytes=VMEM_LIMIT),
        cost_estimate=pl.CostEstimate(
            flops=COST, bytes_accessed=rows * blk, transcendentals=0
        ),
        name=f"sector_{unit}",
    )(*scalars, *operands)


def unpack_kernel(chunk, before, after, begin, last, unroll, plan, *refs):
    pieces = refs[: after - begin + last]
    handoff, held, stage, out, in_sems, out_sems = refs[-6:]
    room = 8
    width, blk = out.shape[1], out.shape[-1]
    units = handoff.shape[1]
    copies = []
    at = 0
    for piece in pieces[: after - begin]:
        copies.append((piece, 0, at, piece.shape[0], None))
        at += piece.shape[0]
    if last:
        _, end = begin_of(plan, units - 1, width, blk, chunk)
        tail = pieces[-1]
        for first in range(0, tail.shape[0], chunk):
            count = min(chunk, tail.shape[0] - first)
            copies.append((tail, first, at + first, count, end - after * chunk > first))

    def each_copy(act):
        for i, (source, first, target, count, needed) in enumerate(copies):
            copy = pltpu.make_async_copy(
                source.at[pl.ds(first, count), :],
                held.at[pl.ds(target, count), :],
                in_sems.at[i],
            )
            if needed is None:
                act(copy)
            else:

                @pl.when(needed)
                def _(copy=copy):
                    act(copy)

    each_copy(lambda copy: copy.start())
    each_copy(lambda copy: copy.wait())
    lane = lax.broadcasted_iota(jnp.int32, (blk, blk), 1)
    high = lax.broadcasted_iota(jnp.int32, (blk, blk), 0)

    def store(turn, slot):
        return pltpu.make_async_copy(out.at[turn], handoff.at[0, slot], out_sems.at[turn])

    def unit_step(u, carry):
        end, done = carry
        code = plan[0, u]
        keep = plan[0, room + u]
        slot = jnp.where(code > 0, code - 1, u)
        _, rows8, rows = packed_shape(keep, width, blk)
        start = jnp.maximum(end, u * chunk)
        end = start + rows
        active = jnp.bool_(True)
        if before:
            active = active & (end > before * chunk)
        if not last:
            active = active & (end <= after * chunk)
        turn = done % 2

        @pl.when(active)
        def _():
            @pl.when(done >= 2)
            def _():
                store(turn, slot).wait()

            shift_rows = start - begin * chunk

            def cast_step(i, carry):
                source = pl.ds(pl.multiple_of(shift_rows + i * blk, 16), blk)
                target = pl.ds(pl.multiple_of(i * blk, blk), blk)
                stage[target, :] = held[source, :].astype(jnp.float32)
                return carry

            lax.fori_loop(0, (rows + blk - 1) // blk, cast_step, 0)
            live = (high < keep) & (lane < keep)

            def column_step(tall, v, carry):
                shift = (v * keep) % blk
                base = pl.multiple_of((v * keep) // blk * rows8, 8)
                this = stage[pl.ds(base, tall), :]
                following = stage[pl.ds(pl.multiple_of(base + rows8, 8), tall), :]
                value = jnp.where(lane[:tall] >= shift, this, following)
                value = pltpu.roll(value, (blk - shift) % blk, 1)
                out[turn, v, :tall] = jnp.where(live[:tall], value, 0.0).astype(jnp.bfloat16)
                if tall < blk:
                    out[turn, v, tall:] = jnp.zeros((blk - tall, blk), jnp.bfloat16)
                return carry

            def columns(tall):
                step = functools.partial(column_step, tall)
                lax.fori_loop(0, width, step, 0, unroll=unroll)

            if last:
                pl.when(keep <= blk // 2)(lambda: columns(blk // 2))
                pl.when(keep > blk // 2)(lambda: columns(blk))
            else:
                columns(blk)
            store(turn, slot).start()

        return end, done + active.astype(jnp.int32)

    _, done = lax.fori_loop(0, units, unit_step, (jnp.int32(0), jnp.int32(0)))

    for back in (1, 2):

        @pl.when(done >= back)
        def _(back=back):
            store((done - back) % 2, 0).wait()


def unpack_call(chunk, before, after, plan, pieces, tail, handoff, shape):
    units, width, blk = shape[1:4]
    rows = width * blk
    begin = max(0, before - -(-rows // chunk)) if before else 0
    unroll = 2 if tail is None else width // 2
    hbm_spec = pl.BlockSpec(memory_space=pltpu.HBM)
    any_spec = pl.BlockSpec(memory_space=pl.ANY)
    operands = list(pieces[begin:after]) + ([] if tail is None else [tail])
    count = len(operands)
    held = sum(piece.shape[0] for piece in operands)
    aliases = {}
    if handoff is not None:
        aliases[1 + count] = 0
        operands.append(handoff)
    return pl.pallas_call(
        functools.partial(unpack_kernel, chunk, before, after, begin, tail is not None, unroll),
        in_specs=[pl.BlockSpec(memory_space=pltpu.SMEM)]
        + [any_spec] * count
        + [hbm_spec] * (len(operands) - count),
        out_specs=hbm_spec,
        out_shape=jax.ShapeDtypeStruct(shape, jnp.bfloat16),
        scratch_shapes=[
            pltpu.VMEM((held + blk, blk), jnp.bfloat16),
            pltpu.VMEM((rows + 2 * blk, blk), jnp.float32),
            pltpu.VMEM((2, width, blk, blk), jnp.bfloat16),
            pltpu.SemaphoreType.DMA((count + units,)),
            pltpu.SemaphoreType.DMA((2,)),
        ],
        input_output_aliases=aliases,
        compiler_params=pltpu.CompilerParams(vmem_limit_bytes=VMEM_LIMIT),
        name=f"unpack_{after}",
    )(plan, *operands)


def send_tail(rows, chunk, shape, plan, excess, *pieces):
    got = passed_along(excess[:rows], "seg", 1)
    handoff = unpack_call(chunk, 0, len(pieces), plan, pieces, None, None, shape)
    return lax.dynamic_update_slice(excess, got, (0, 0)), handoff


def body(env_left, isometry, sing_vals, kept, twosite_sector, mpo_row, mpo_op, op_table):
    my_index = lax.axis_index("sec")
    devices, segments = lax.axis_size("sec"), lax.axis_size("seg")
    units, width, blk = env_left.shape[1:4]
    rows = width * blk
    chunk = int(rows * BASE) // 16 * 16
    routed, plan, tile = make_plan(
        isometry[0, 0], twosite_sector[0, 0], kept[SITES - 1, 0], my_index, devices, width, chunk
    )
    limits = []
    for share in TOTALS:
        limit = (int(units * share * rows) // 16 + 1) * 16 - (units - 1) * chunk
        limits.append(min(limit, units * rows - (units - 1) * chunk))
    isom, plan_before, level, late_env = exchange(
        routed, tile, env_left, devices, segments, limits
    )
    scalars = (plan, mpo_row.T, mpo_op.T, jnp.transpose(op_table, (1, 2, 0)))
    sing = jnp.transpose(sing_vals, (1, 0, 2))
    lower = passed_along(late_env, "sec", 1)
    env_right = excess = None
    pieces = []
    for unit in range(units):
        env_right, *sent, excess = sector_call(
            unit,
            chunk,
            scalars,
            env_left,
            lower if unit >= EARLY else None,
            isom,
            sing,
            env_right,
            excess,
            pieces[unit - 2] if 1 < unit < units - 1 else None,
        )
        pieces += [passed_along(piece, "seg", 1) for piece in sent]
    branches = [
        functools.partial(send_tail, limit, chunk, env_left.shape) for limit in limits
    ]
    early = units - 2
    tail, handoff = lax.switch(
        level[0, 2 * (plan.shape[0] // 4)], branches, plan_before, excess, *pieces[:early]
    )
    handoff = unpack_call(
        chunk, early, units - 1, plan_before, pieces, tail, handoff, env_left.shape
    )
    return env_right, handoff


def solution(mesh):
    in_specs = (
        P("seg", "sec", None, None, None),
        P(None, "seg", "sec", None, None, None),
        P("seg", "sec", None),
        P(None, "seg", "sec"),
        P(None, "seg", None),
        P(),
        P(),
        P(),
    )
    out_specs = (P("seg", "sec", None, None, None), P("seg", "sec", None, None, None))
    return jax.shard_map(body, mesh=mesh, in_specs=in_specs, out_specs=out_specs, check_vma=False)
```
